32 devices in a mesh: dp: 8 (over z, y), fsdp: 4 (over x, core).
Axes of the slice: x: 2, y: 2, z: 4, core: 2. Of those that a mesh axis runs over, the one named last changes fastest.
Arguments:
- inputs: bfloat16 [32, 1024, 768], P(('dp', 'fsdp')), may hold values from -6 to 6
- encoded: bfloat16 [32, 512, 768], P(('dp', 'fsdp')), may hold values from -6 to 6
- out_grad: bfloat16 [32, 1024, 768], P(('dp', 'fsdp')), may hold values from -6 to 6
- prefix: int32 [32], P(('dp', 'fsdp')), may hold values from 102 to 512
- bucket_map: int32 [2, 1024], replicated, may hold values from 0 to 31, as said below
- bias_table: bfloat16 [32, 12], replicated, may hold values from -4 to 4
- norm_self: bfloat16 [768], P(('dp', 'fsdp')), may hold values from 0.099609375 to 1.8984375
- self_query: bfloat16 [768, 768], P(('dp', 'fsdp')), may hold values from -0.02734375 to 0.02734375
- self_key: bfloat16 [768, 768], P(('dp', 'fsdp')), may hold values from -0.21875 to 0.21875
- self_value: bfloat16 [768, 768], P(('dp', 'fsdp')), may hold values from -0.21875 to 0.21875
- self_out: bfloat16 [768, 768], P(('dp', 'fsdp')), may hold values from -1 to 1
- norm_cross: bfloat16 [768], P(('dp', 'fsdp')), may hold values from 0.099609375 to 1.8984375
- cross_query: bfloat16 [768, 768], P(('dp', 'fsdp')), may hold values from -0.02734375 to 0.02734375
- cross_key: bfloat16 [768, 768], P(('dp', 'fsdp')), may hold values from -0.21875 to 0.21875
- cross_value: bfloat16 [768, 768], P(('dp', 'fsdp')), may hold values from -0.21875 to 0.21875
- cross_out: bfloat16 [768, 768], P(('dp', 'fsdp')), may hold values from -1 to 1
- norm_feed: bfloat16 [768], P(('dp', 'fsdp')), may hold values from 0.099609375 to 1.8984375
- feed_gate: bfloat16 [768, 2048], P(('dp', 'fsdp')), may hold values from -0.21875 to 0.21875
- feed_up: bfloat16 [768, 2048], P(('dp', 'fsdp')), may hold values from -0.21875 to 0.21875
- feed_down: bfloat16 [2048, 768], P(('dp', 'fsdp')), may hold values from -0.125 to 0.125
Outputs:
- output: bfloat16 [32, 1024, 768], P(('dp', 'fsdp'))
- inputs_grad: float32 [32, 1024, 768], P(('dp', 'fsdp'))
- encoded_grad: float32 [32, 512, 768], P(('dp', 'fsdp'))
- table_grad: float32 [32, 12], replicated
- norm_self_grad: float32 [768], P(('dp', 'fsdp'))
- self_query_grad: float32 [768, 768], P(('dp', 'fsdp'))
- self_key_grad: float32 [768, 768], P(('dp', 'fsdp'))
- self_value_grad: float32 [768, 768], P(('dp', 'fsdp'))
- self_out_grad: float32 [768, 768], P(('dp', 'fsdp'))
- norm_cross_grad: float32 [768], P(('dp', 'fsdp'))
- cross_query_grad: float32 [768, 768], P(('dp', 'fsdp'))
- cross_key_grad: float32 [768, 768], P(('dp', 'fsdp'))
- cross_value_grad: float32 [768, 768], P(('dp', 'fsdp'))
- cross_out_grad: float32 [768, 768], P(('dp', 'fsdp'))
- norm_feed_grad: float32 [768], P(('dp', 'fsdp'))
- feed_gate_grad: float32 [768, 2048], P(('dp', 'fsdp'))
- feed_up_grad: float32 [768, 2048], P(('dp', 'fsdp'))
- feed_down_grad: float32 [2048, 768], P(('dp', 'fsdp'))
The draws below stay inside these ranges and needn't reach their ends.
Inputs may be any that keep to these rules, and one draw needn't show every extreme that they name: bucket_map[0, d] is the bucket of a key d positions before its query; bucket_map[1, a] is the bucket within one half of a key a positions away; both rows never fall as the distance grows, equal the distance for the nearest 32/2 and 8 distances, and end at 31 and 15.
All inputs are finite; a program needn't handle non-finite values.
Results may differ from the reference program's by a relative error of at most 0.023.
Values may be sent and summed in bfloat16 or wider, within the bound.
A program may use at most 320 MiB of HBM per device.

```python
import jax
import jax.numpy as jnp
from jax import lax

D = 768
H = 12
DH = 64
FF = 2048
NB = 32
MAXD = 128
LEN = 1024
ENC = 512
SEQS = 32


def draw_bucket_map(key, part):
    quarter = NB // 4
    half = NB // 2
    upper = min(MAXD, LEN - 1)
    causal_marks = jax.random.permutation(jax.random.fold_in(key, 11), upper - half)[:half - 1] + half + 1
    two_way_marks = jax.random.permutation(jax.random.fold_in(key, 12), upper - quarter)[:quarter - 1] + quarter + 1
    distance = jnp.arange(LEN, dtype=jnp.int32)
    causal_count = jnp.sum((causal_marks[None, :] <= distance[:, None]).astype(jnp.int32), axis=1)
    two_way_count = jnp.sum((two_way_marks[None, :] <= distance[:, None]).astype(jnp.int32), axis=1)
    causal = jnp.where(distance < half, distance, half + causal_count)
    two_way = jnp.where(distance < quarter, distance, quarter + two_way_count)
    return jnp.stack([causal, two_way]).astype(jnp.int32)


def place_ends(entries, key, least, top_value):
    dims = entries.shape
    spot = [jax.random.randint(jax.random.fold_in(key, axis), (), 0, dims[axis]) for axis in range(len(dims))]
    entries = entries.at[tuple(spot)].set(least)
    longest = dims.index(max(dims))
    spot[longest] = (spot[longest] + 1) % dims[longest]
    return entries.at[tuple(spot)].set(top_value)


def with_spikes(entries, key, source, target, shards_of, factor):
    def block_of(axis_at):
        return (jnp.arange(entries.shape[axis_at]) // (entries.shape[axis_at] // shards_of)).reshape((-1,) + (1,) * (entries.ndim - 1 - axis_at))

    first = jax.random.permutation(key, shards_of)[block_of(target)]
    other_side = (block_of(target) + shards_of // 2) % shards_of
    return jnp.where((block_of(source) == first) | (block_of(source) == other_side), factor * entries, entries)


def level_of(stream_key, shape, shards, smallest, high):
    def one(dim, shards_of):
        draws = jax.random.uniform(jax.random.fold_in(jax.random.fold_in(stream_key, 6), dim), (shards_of,), jnp.float32, smallest / len(shards), high / len(shards))
        return jnp.repeat(jnp.exp(draws), shape[dim] // shards_of).reshape((-1,) + (1,) * (len(shape) - dim - 1))

    factor_of = one(*shards[0])
    for cut in shards[1:]:
        factor_of = factor_of * one(*cut)
    return factor_of


def centred(key, extent, spread, most, cuts=(), kind=jnp.bfloat16):
    entries = jax.random.normal(key, extent, jnp.float32) * spread
    if len(cuts) > 0:
        entries = level_of(key, extent, cuts, -0.22, 0.18) * entries
    return jnp.clip(entries, min=-most, max=most).astype(kind)


def gaussian_with(key, extent, spread, reach, cuts, heavy, kind=jnp.bfloat16):
    array = spread * jax.random.normal(key, extent, jnp.float32)
    if cuts:
        array = array * level_of(key, extent, cuts, -0.22, 0.18)
    return jnp.clip(with_spikes(array, jax.random.fold_in(key, 3), *heavy), -reach, reach).astype(kind)


def setup_inputs(seed: int = 0) -> dict:
    key_list = jax.random.split(jax.random.key(seed), 21)
    return {
        "inputs": gaussian_with(key_list[0], (SEQS, LEN, D), 1.0, 6.0, ((0, 32),), (0, 2, 32, 2.75)),
        "encoded": gaussian_with(key_list[1], (SEQS, ENC, D), 1.0, 6.0, ((0, 32),), (0, 2, 32, 2.75)),
        "out_grad": centred(key_list[2], (SEQS, LEN, D), 1.0, 6.0, ((0, 32),)),
        "prefix": place_ends(jax.random.randint(key_list[3], (SEQS,), LEN // 10, LEN // 2 + 1), jax.random.fold_in(key_list[3], 1), LEN // 10, (LEN // 2 + 1) - 1).astype(jnp.int32),
        "bucket_map": draw_bucket_map(jax.random.fold_in(key_list[20], 71), 0),
        "bias_table": centred(key_list[5], (NB, H), 1.0, 4.0),
        "norm_self": jnp.clip(1.0 + 0.18 * jax.random.normal(key_list[6], (D,), jnp.float32), 0.099609375, 1.8984375).astype(jnp.bfloat16),
        "self_query": centred(key_list[7], (D, H * DH), (D * DH) ** -0.5, 0.02734375, ((0, 32),)),
        "self_key": centred(key_list[8], (D, H * DH), D ** -0.5, 0.21875, ((0, 32),)),
        "self_value": centred(key_list[9], (D, H * DH), D ** -0.5, 0.21875, ((0, 32),)),
        "self_out": centred(key_list[10], (H * DH, D), 32 ** -0.5, 1.0, ((0, 32),)),
        "norm_cross": jnp.clip(1.0 + 0.18 * jax.random.normal(key_list[11], (D,), jnp.float32), 0.099609375, 1.8984375).astype(jnp.bfloat16),
        "cross_query": centred(key_list[12], (D, H * DH), (D * DH) ** -0.5, 0.02734375, ((0, 32),)),
        "cross_key": centred(key_list[13], (D, H * DH), D ** -0.5, 0.21875, ((0, 32),)),
        "cross_value": centred(key_list[14], (D, H * DH), D ** -0.5, 0.21875, ((0, 32),)),
        "cross_out": centred(key_list[15], (H * DH, D), 32 ** -0.5, 1.0, ((0, 32),)),
        "norm_feed": jnp.clip(1.0 + 0.18 * jax.random.normal(key_list[16], (D,), jnp.float32), 0.099609375, 1.8984375).astype(jnp.bfloat16),
        "feed_gate": centred(key_list[17], (D, FF), D ** -0.5, 0.21875, ((0, 32),)),
        "feed_up": centred(key_list[18], (D, FF), D ** -0.5, 0.21875, ((0, 32),)),
        "feed_down": centred(key_list[19], (FF, D), FF ** -0.5, 0.125, ((0, 32),)),
    }


@jax.custom_vjp
def low(v):
    return lax.optimization_barrier(v.astype(jnp.bfloat16)).astype(jnp.float32)

@jax.custom_vjp
def low_back(v):
    return v

def low_keep(v):
    return (low(v), None)

def low_pass(kept, grad):
    return (grad,)

def back_keep(v):
    return (v, None)

def back_low(kept, grad):
    return (low(grad),)
low.defvjp(low_keep, low_pass)
low_back.defvjp(back_keep, back_low)
negative = -1e+30

def product(left, right):
    return jnp.dot(left, right, preferred_element_type=jnp.float32, precision=lax.Precision.HIGHEST)

def rms_scale(value, gain):
    scale = lax.rsqrt(lax.optimization_barrier(jnp.mean(value * value, axis=-1, keepdims=True)) + 1e-06)
    return value * scale * gain

def bucket_layout(limit, bucket_map, length):
    query_place = jnp.arange(length, dtype=jnp.int32)[:, None]
    key_place = jnp.arange(length, dtype=jnp.int32)[None, :]
    offset = key_place - query_place
    causal = bucket_map[0][jnp.clip(-offset, 0, length - 1)]
    two_way = bucket_map[1][jnp.abs(offset)] + NB // 2 * (offset > 0).astype(jnp.int32)
    inside = (query_place < limit) & (key_place < limit)
    allowed = (key_place <= query_place) | (key_place < limit)
    return (jnp.where(inside, two_way, causal), allowed)

def attend(query, keys, values, bias, allowed):
    scores = jnp.einsum('qhd,khd->hqk', query, keys, precision=lax.Precision.HIGHEST)
    if bias is not None:
        scores = scores + bias
    scores = low_back(scores)
    if allowed is not None:
        scores = jnp.where(allowed[None], scores, negative)
    probs = low(jax.nn.softmax(scores, axis=-1))
    mixed = jnp.einsum('hqk,khd->qhd', probs, values, precision=lax.Precision.HIGHEST)
    return low_back(low(mixed))

def layer(weights, tokens, memory, limit, bucket_map):
    table, norm_self, self_query, self_key, self_value, self_out, norm_cross, cross_query, cross_key, cross_value, cross_out, norm_feed, feed_gate, feed_up, feed_down = weights
    length = tokens.shape[0]
    source = memory.shape[0]
    buckets, allowed = bucket_layout(limit, bucket_map, length)
    bias = jnp.transpose(table[buckets], (2, 0, 1))
    normed = low(rms_scale(tokens, norm_self))
    query = low_back(low(product(normed, self_query))).reshape(length, H, DH)
    keys = low_back(low(product(normed, self_key))).reshape(length, H, DH)
    values = low_back(low(product(normed, self_value))).reshape(length, H, DH)
    mixed = attend(query, keys, values, bias, allowed).reshape(length, H * DH)
    first = tokens + low_back(product(mixed, self_out))
    normed = low(rms_scale(first, norm_cross))
    query = low_back(low(product(normed, cross_query))).reshape(length, H, DH)
    keys = low_back(low(product(memory, cross_key))).reshape(source, H, DH)
    values = low_back(low(product(memory, cross_value))).reshape(source, H, DH)
    mixed = attend(query, keys, values, None, None).reshape(length, H * DH)
    second = first + low_back(product(mixed, cross_out))
    normed = low(rms_scale(second, norm_feed))
    gate = low_back(product(normed, feed_gate))
    upward = low_back(product(normed, feed_up))
    hidden = low(jax.nn.gelu(gate, approximate=True) * upward)
    return second + low_back(product(hidden, feed_down))

def reference(inputs, encoded, out_grad, prefix, bucket_map, bias_table, norm_self, self_query, self_key, self_value, self_out, norm_cross, cross_query, cross_key, cross_value, cross_out, norm_feed, feed_gate, feed_up, feed_down):
    weights = tuple((item.astype(jnp.float32) for item in (bias_table, norm_self, self_query, self_key, self_value, self_out, norm_cross, cross_query, cross_key, cross_value, cross_out, norm_feed, feed_gate, feed_up, feed_down)))
    tokens = inputs.astype(jnp.float32)
    memory = encoded.astype(jnp.float32)

    def whole(weights, tokens, memory):

        def single(item):
            return layer(weights, item[0], item[1], item[2], bucket_map)
        return lax.map(jax.checkpoint(single), (tokens, memory, prefix))
    result, pull = jax.vjp(whole, weights, tokens, memory)
    grad_weights, grad_tokens, grad_memory = pull(out_grad.astype(jnp.float32))
    return (result.astype(jnp.bfloat16), grad_tokens, grad_memory, grad_weights[0], grad_weights[1], grad_weights[2], grad_weights[3], grad_weights[4], grad_weights[5], grad_weights[6], grad_weights[7], grad_weights[8], grad_weights[9], grad_weights[10], grad_weights[11], grad_weights[12], grad_weights[13], grad_weights[14])
```

```python
import functools

import jax
import jax.numpy as jnp
import numpy as np
from jax import lax
from jax.experimental import pallas as pl
from jax.experimental.pallas import tpu as pltpu
from jax.sharding import PartitionSpec as P

DH = 64
NB = 32
PAIR = 2 * DH
SUB = 128
NEG = -1e30
F32 = jnp.float32
BF16 = jnp.bfloat16
AXES = ("dp", "fsdp")


def dot(a, b, ca=1, cb=0):
    return lax.dot_general(a, b, (((ca,), (cb,)), ((), ())), preferred_element_type=F32)


def exact_dot(a, b, ca=1, cb=0):
    return lax.dot_general(
        a,
        b,
        (((ca,), (cb,)), ((), ())),
        preferred_element_type=F32,
        precision=lax.Precision.HIGHEST,
    )


def rms(value):
    return lax.rsqrt(jnp.mean(value * value, axis=-1, keepdims=True) + 1e-06)


class Band:
    def __init__(self, length, reach):
        self.far = length
        self.reach = reach
        self.causal = length + reach
        self.two_way = 2 * reach
        self.width = self.causal + self.two_way
        self.query_zero = length - SUB
        self.query_zero_two = reach - SUB
        self.key_zero = reach - SUB
        self.key_zero_two = reach - SUB

    def distances(self, rows):
        lanes = np.arange(self.causal)
        lanes_two = np.arange(self.two_way)
        if rows == "queries":
            causal = self.query_zero - lanes
            two_way = self.query_zero_two - lanes_two
        else:
            causal = lanes - self.key_zero
            two_way = lanes_two - self.key_zero_two
        causal = (causal + self.reach - 1) % self.causal - (self.reach - 1) if rows == "queries" else (
            causal + self.reach
        ) % self.causal - self.reach
        two_way = (two_way + self.reach - 1) % self.two_way - (self.reach - 1) if rows == "queries" else (
            two_way + self.reach
        ) % self.two_way - self.reach
        return causal, two_way


def lane_buckets(bucket_map, band, rows):
    causal, two_way = band.distances(rows)
    top = bucket_map.shape[1] - 1
    one = bucket_map[0][np.clip(causal, 0, top)]
    one = jnp.where(causal < 0, -1, one)
    two = bucket_map[1][np.clip(np.abs(two_way), 0, top)] + (NB // 2) * (two_way < 0).astype(np.int32)
    return jnp.concatenate([one, two]).reshape(1, -1)


def one_hot(buckets_ref):
    width = buckets_ref.shape[1]
    return buckets_ref[...] == lax.broadcasted_iota(jnp.int32, (NB, width), 0)


def spread(row, width):
    return pltpu.roll(jnp.broadcast_to(row, (SUB, width)), 0, 1, stride=1, stride_axis=0)


def fold(band):
    width = band.shape[1]
    half = SUB // 2
    while half >= 8:
        band = band[:half] + pltpu.roll(band[half:], width - half, 1)
        half //= 2
    row = lax.broadcasted_iota(jnp.int32, band.shape, 0)
    for bit in (4, 2, 1):
        band = jnp.where((row & bit) != 0, pltpu.roll(band, width - bit, 1), band)
    return jnp.sum(band, axis=0, keepdims=True)


def fill_bands(head, bias_ref, band, causal_ref, two_ref):
    row = bias_ref[pl.ds(head, 1), :]
    causal_ref[...] = spread(row[:, : band.causal], band.causal)
    two_ref[...] = spread(row[:, band.causal :], band.two_way)


def bias_rows(table_ref, buckets_ref):
    hot = one_hot(buckets_ref)
    bias = dot(table_ref[...], jnp.where(hot, 1.0, 0.0).astype(BF16))
    return jnp.where(buckets_ref[...] < 0, NEG, bias)


def head_cols(head):
    group = head // 2
    return pl.ds(pl.multiple_of(group * PAIR, PAIR), PAIR), head % 2


def pick_lanes(half):
    return lax.broadcasted_iota(jnp.int32, (1, PAIR), 1) // DH == half


def soft_rows(scores):
    high = jnp.max(scores, axis=-1, keepdims=True)
    weights = jnp.exp(scores - high)
    total = jnp.sum(weights, axis=-1, keepdims=True)
    return weights.astype(BF16), total, high + jnp.log(total)


def store_head(mixed_ref, lse_ref, rows, cols, head, half, out, total, lse):
    pick = pick_lanes(half)
    mixed_ref[rows, cols] = jnp.where(pick, (out / total).astype(BF16), mixed_ref[rows, cols])
    lane = lax.broadcasted_iota(jnp.int32, (1, lse_ref.shape[1]), 1)
    lse_ref[rows, :] = jnp.where(lane == head, lse, lse_ref[rows, :])


def self_forward_head(head, limit, q_ref, k_ref, v_ref, causal_ref, two_ref, band, mixed_ref, lse_ref):
    length = q_ref.shape[0]
    cols, half = head_cols(head)
    pick = pick_lanes(half)
    block = 256
    for start in range(0, length, block):
        keys = max(start + block, band.reach)
        rows = pl.ds(start, block)
        query = jnp.where(pick, q_ref[rows, cols], 0)
        scores = dot(query, k_ref[pl.ds(0, keys), cols], 1, 1)
        parts = []
        for first in range(start, start + block, SUB):
            at = band.query_zero - first
            bias = causal_ref[:, at : at + keys]
            if start < band.reach:
                at = band.query_zero_two - first
                two = two_ref[:, at : at + keys]
                inside = (first + lax.broadcasted_iota(jnp.int32, (SUB, keys), 0) < limit) & (
                    lax.broadcasted_iota(jnp.int32, (SUB, keys), 1) < limit
                )
                bias = jnp.where(inside, two, bias)
            parts.append(bias)
        weights, total, lse = soft_rows(scores + jnp.concatenate(parts, axis=0))
        out = dot(weights, v_ref[pl.ds(0, keys), cols])
        store_head(mixed_ref, lse_ref, rows, cols, head, half, out, total, lse)


def cross_forward_head(head, q_ref, k_ref, v_ref, mixed_ref, lse_ref):
    length = q_ref.shape[0]
    cols, half = head_cols(head)
    pick = pick_lanes(half)
    block = 256
    for start in range(0, length, block):
        rows = pl.ds(start, block)
        query = jnp.where(pick, q_ref[rows, cols], 0)
        weights, total, lse = soft_rows(dot(query, k_ref[:, cols], 1, 1))
        out = dot(weights, v_ref[:, cols])
        store_head(mixed_ref, lse_ref, rows, cols, head, half, out, total, lse)


def row_blocks(count, block, step):
    @pl.loop(0, count // block)
    def _(index):
        step(pl.ds(pl.multiple_of(index * block, block), block))


def forward_kernel(
    limit_ref, tokens_ref, memory_ref, gains_ref, table_ref, buckets_ref,
    wq_ref, wk_ref, wv_ref, wo_ref, cq_ref, ck_ref, cv_ref, co_ref,
    q1_ref, k1_ref, v1_ref, mixed1_ref, lse1_ref, first_ref,
    q2_ref, k2_ref, v2_ref, mixed2_ref, lse2_ref, second_ref,
    bias_ref, causal_ref, two_ref,
    *, band, heads,
):
    length = tokens_ref.shape[0]
    bias_ref[...] = bias_rows(table_ref, buckets_ref)

    def project_self(rows):
        value = tokens_ref[rows, :].astype(F32)
        normed = (value * rms(value) * gains_ref[0:1, :]).astype(BF16)
        q1_ref[rows, :] = dot(normed, wq_ref[...]).astype(BF16)
        k1_ref[rows, :] = dot(normed, wk_ref[...]).astype(BF16)
        v1_ref[rows, :] = dot(normed, wv_ref[...]).astype(BF16)

    row_blocks(length, 256, project_self)
    lse1_ref[...] = jnp.zeros_like(lse1_ref)
    lse2_ref[...] = jnp.zeros_like(lse2_ref)
    mixed1_ref[...] = jnp.zeros_like(mixed1_ref)
    mixed2_ref[...] = jnp.zeros_like(mixed2_ref)

    @pl.loop(0, heads)
    def _(head):
        fill_bands(head, bias_ref, band, causal_ref, two_ref)
        self_forward_head(head, limit_ref[0], q1_ref, k1_ref, v1_ref, causal_ref, two_ref, band, mixed1_ref, lse1_ref)

    def project_memory(rows):
        k2_ref[rows, :] = dot(memory_ref[rows, :], ck_ref[...]).astype(BF16)
        v2_ref[rows, :] = dot(memory_ref[rows, :], cv_ref[...]).astype(BF16)

    row_blocks(memory_ref.shape[0], 256, project_memory)

    def project_cross(rows):
        value = tokens_ref[rows, :].astype(F32) + dot(mixed1_ref[rows, :], wo_ref[...])
        first_ref[rows, :] = value
        normed = (value * rms(value) * gains_ref[1:2, :]).astype(BF16)
        q2_ref[rows, :] = dot(normed, cq_ref[...]).astype(BF16)

    row_blocks(length, 256, project_cross)

    @pl.loop(0, heads)
    def _(head):
        cross_forward_head(head, q2_ref, k2_ref, v2_ref, mixed2_ref, lse2_ref)

    def project_second(rows):
        second_ref[rows, :] = first_ref[rows, :] + dot(mixed2_ref[rows, :], co_ref[...])

    row_blocks(length, 256, project_second)


def norm_back_rows(value, gain, grad):
    scale = rms(value)
    unit = value * scale
    scaled = grad * gain
    back = scale * (scaled - unit * jnp.mean(scaled * unit, axis=-1, keepdims=True))
    return back, jnp.sum(grad * unit, axis=0, keepdims=True)


GELU_A = 0.7978845608028654
GELU_B = 0.044715


def feed_kernel(
    second_ref, gout_ref, gains_ref, gate_ref, up_ref, down_ref,
    output_ref, gsecond_ref, ggain_ref, dgate_ref, dup_ref, ddown_ref,
    normed_ref, flipped_ref, out_ref, back_ref, hidden_ref, ggate_ref, gup_ref,
):
    step = pl.program_id(0)
    length = second_ref.shape[0]
    block = 256

    @pl.when(step == 0)
    def _():
        def prepare(rows):
            value = second_ref[rows, :]
            normed = (value * rms(value) * gains_ref[2:3, :]).astype(BF16)
            normed_ref[rows, :] = normed
            flipped_ref[:, rows] = normed.T
            out_ref[rows, :] = value
            back_ref[rows, :] = jnp.zeros_like(value)

        row_blocks(length, block, prepare)

    def rows_step(rows):
        normed = normed_ref[rows, :]
        gate = dot(normed, gate_ref[...])
        upward = dot(normed, up_ref[...])
        square = gate * gate
        bend = jnp.tanh(GELU_A * gate * (1.0 + GELU_B * square))
        half = 0.5 * (1.0 + bend)
        active = gate * half
        hidden = (active * upward).astype(BF16)
        hidden_ref[rows, :] = hidden
        out_ref[rows, :] += dot(hidden, down_ref[...])
        ghidden = dot(gout_ref[rows, :], down_ref[...], 1, 1)
        slope = half + 0.5 * gate * (1.0 - bend * bend) * (GELU_A * (1.0 + 3.0 * GELU_B * square))
        ggate = (ghidden * upward * slope).astype(BF16)
        gup = (ghidden * active).astype(BF16)
        ggate_ref[rows, :] = ggate
        gup_ref[rows, :] = gup
        back_ref[rows, :] += dot(ggate, gate_ref[...], 1, 1) + dot(gup, up_ref[...], 1, 1)

    row_blocks(length, block, rows_step)
    ddown_ref[...] = dot(hidden_ref[...].T, gout_ref[...]).astype(BF16)
    dgate_ref[...] = dot(flipped_ref[...], ggate_ref[...]).astype(BF16)
    dup_ref[...] = dot(flipped_ref[...], gup_ref[...]).astype(BF16)

    @pl.when(step == pl.num_programs(0) - 1)
    def _():
        ggain_ref[...] = jnp.zeros_like(ggain_ref)

        def finish(rows):
            output_ref[rows, :] = out_ref[rows, :].astype(BF16)
            back, ggain = norm_back_rows(second_ref[rows, :], gains_ref[2:3, :], back_ref[rows, :])
            gsecond_ref[rows, :] = back + gout_ref[rows, :].astype(F32)
            ggain_ref[0:1, :] += ggain

        row_blocks(length, block, finish)


def backward_head_prepare(group_cols, gm_ref, mixed_ref, delta_ref):
    product = (gm_ref[:, group_cols].astype(F32) * mixed_ref[:, group_cols].astype(F32)).T
    delta_ref[0:1, :] = jnp.sum(product[:DH], axis=0, keepdims=True)
    delta_ref[1:2, :] = jnp.sum(product[DH:], axis=0, keepdims=True)


def backward_block(key_rows, cols, half, start, bias, q_ref, k_ref, v_ref, gm_ref, lse, delta, gk_ref, gv_ref, gqt_ref):
    length = q_ref.shape[0]
    pick = pick_lanes(half)
    queries = pl.ds(start, length - start)
    query = jnp.where(pick, q_ref[queries, cols], 0)
    grad = jnp.where(pick, gm_ref[queries, cols], 0)
    keys = k_ref[key_rows, cols]
    scores = dot(keys, query, 1, 1)
    if bias is not None:
        scores = scores + bias
    probs = jnp.exp(scores - lse[:, start:])
    gv = dot(probs.astype(BF16), grad)
    gprobs = dot(v_ref[key_rows, cols], grad, 1, 1)
    gscores = probs * (gprobs - delta[:, start:])
    low = gscores.astype(BF16)
    gk = dot(low, query)
    gk_ref[key_rows, cols] = jnp.where(pick, gk.astype(BF16), gk_ref[key_rows, cols])
    gv_ref[key_rows, cols] = jnp.where(pick, gv.astype(BF16), gv_ref[key_rows, cols])
    gqt_ref[:, queries] += dot(jnp.where(pick, keys, 0).T, low)
    return gscores


def self_backward_head(
    head, limit, q_ref, k_ref, v_ref, gm_ref, mixed_ref, lse_ref, delta_ref, causal_ref, two_ref, band,
    gk_ref, gv_ref, gqt_ref, causal_sum_ref, two_sum_ref,
):
    length = q_ref.shape[0]
    cols, half = head_cols(head)
    lse = lse_ref[pl.ds(head, 1), :]
    delta = delta_ref[pl.ds(half, 1), :]
    reach = band.reach
    block = 256
    for first in range(0, length, block):
        start = 0 if first < reach else first
        count = length - start
        parts = []
        for key in range(first, first + block, SUB):
            at = band.key_zero - key + start
            bias = causal_ref[:, at : at + count]
            if first < reach:
                at = band.key_zero_two - key
                two = two_ref[:, at : at + reach]
                inside = (key + lax.broadcasted_iota(jnp.int32, (SUB, reach), 0) < limit) & (
                    lax.broadcasted_iota(jnp.int32, (SUB, reach), 1) < limit
                )
                bias = jnp.concatenate([jnp.where(inside, two, bias[:, :reach]), bias[:, reach:]], axis=1)
            parts.append(bias)
        gscores = backward_block(
            pl.ds(first, block), cols, half, start, jnp.concatenate(parts, axis=0),
            q_ref, k_ref, v_ref, gm_ref, lse, delta, gk_ref, gv_ref, gqt_ref,
        )
        for key in range(first, first + block, SUB):
            part = gscores[key - first : key - first + SUB]
            at = band.key_zero - key + start
            if first < reach:
                inside = (key + lax.broadcasted_iota(jnp.int32, (SUB, reach), 0) < limit) & (
                    lax.broadcasted_iota(jnp.int32, (SUB, reach), 1) < limit
                )
                head_part = part[:, :reach]
                at_two = band.key_zero_two - key
                two_sum_ref[:, at_two : at_two + reach] += jnp.where(inside, head_part, 0.0)
                causal_sum_ref[:, at : at + reach] += jnp.where(inside, 0.0, head_part)
                causal_sum_ref[:, at + reach : at + count] += part[:, reach:]
            else:
                causal_sum_ref[:, at : at + count] += part


def cross_backward_kernel(
    gsecond_ref, first_ref, memory_ref, gains_ref, q_ref, k_ref, v_ref, mixed1_ref, mixed2_ref, lse_ref,
    wo_ref, cq_ref, ck_ref, cv_ref, co_ref,
    gmem_ref, gfirst_ref, gm1_ref, ggain_ref, dwo_ref, dcq_ref, dck_ref, dcv_ref, dco_ref,
    gm_ref, branch_ref, flipped_ref, lse_rows_ref, delta_ref, gq_ref, gk_ref, gv_ref, gqt_ref,
    *, heads,
):
    length, width = first_ref.shape
    source = memory_ref.shape[0]
    block = 256

    def prepare(rows):
        branch = gsecond_ref[rows, :].astype(BF16)
        branch_ref[rows, :] = branch
        gm_ref[rows, :] = dot(branch, co_ref[...], 1, 1).astype(BF16)
        flipped_ref[:, rows] = mixed2_ref[rows, :].T

    row_blocks(length, block, prepare)

    def out_grad(rows):
        dco_ref[rows, :] = dot(flipped_ref[rows, :], branch_ref[...]).astype(BF16)

    row_blocks(width, block, out_grad)
    lse_rows_ref[...] = lse_ref[...].T
    gk_ref[...] = jnp.zeros_like(gk_ref)
    gv_ref[...] = jnp.zeros_like(gv_ref)

    @pl.loop(0, heads // 2)
    def _(group):
        cols = pl.ds(pl.multiple_of(group * PAIR, PAIR), PAIR)
        backward_head_prepare(cols, gm_ref, mixed2_ref, delta_ref)
        gqt_ref[...] = jnp.zeros_like(gqt_ref)

        @pl.loop(0, 2)
        def _(half):
            head = group * 2 + half
            for first in range(0, source, block):
                backward_block(
                    pl.ds(first, block), cols, half, 0, None, q_ref, k_ref, v_ref, gm_ref,
                    lse_rows_ref[pl.ds(head, 1), :], delta_ref[pl.ds(half, 1), :], gk_ref, gv_ref, gqt_ref,
                )

        gq_ref[:, cols] = gqt_ref[...].T.astype(BF16)

    def memory_grad(rows):
        gmem_ref[rows, :] = dot(gk_ref[rows, :], ck_ref[...], 1, 1) + dot(gv_ref[rows, :], cv_ref[...], 1, 1)
        flipped_ref[:, rows] = memory_ref[rows, :].T

    row_blocks(source, block, memory_grad)

    def memory_weights(rows):
        flipped = flipped_ref[rows, :source]
        dck_ref[rows, :] = dot(flipped, gk_ref[...]).astype(BF16)
        dcv_ref[rows, :] = dot(flipped, gv_ref[...]).astype(BF16)

    row_blocks(width, block, memory_weights)
    ggain_ref[...] = jnp.zeros_like(ggain_ref)

    def first_grad(rows):
        value = first_ref[rows, :]
        flipped_ref[:, rows] = (value * rms(value) * gains_ref[1:2, :]).astype(BF16).T
        back, ggain = norm_back_rows(value, gains_ref[1:2, :], dot(gq_ref[rows, :], cq_ref[...], 1, 1))
        ggain_ref[0:1, :] += ggain
        gfirst = back + gsecond_ref[rows, :]
        gfirst_ref[rows, :] = gfirst
        branch = gfirst.astype(BF16)
        branch_ref[rows, :] = branch
        gm1_ref[rows, :] = dot(branch, wo_ref[...], 1, 1).astype(BF16)

    row_blocks(length, block, first_grad)

    def query_weights(rows):
        dcq_ref[rows, :] = dot(flipped_ref[rows, :], gq_ref[...]).astype(BF16)

    row_blocks(width, block, query_weights)

    def flip_mixed(rows):
        flipped_ref[:, rows] = mixed1_ref[rows, :].T

    row_blocks(length, block, flip_mixed)

    def out_weights(rows):
        dwo_ref[rows, :] = dot(flipped_ref[rows, :], branch_ref[...]).astype(BF16)

    row_blocks(width, block, out_weights)


def self_backward_kernel(
    limit_ref, tokens_ref, gains_ref, table_ref, buckets_ref, q_ref, k_ref, v_ref, mixed_ref, lse_ref, gm_ref, gfirst_ref,
    wq_ref, wk_ref, wv_ref,
    gtokens_ref, ggain_ref, gtable_ref, dwq_ref, dwk_ref, dwv_ref,
    bias_ref, causal_ref, two_ref, flipped_ref, lse_rows_ref, delta_ref, gq_ref, gk_ref, gv_ref, gqt_ref,
    causal_sum_ref, two_sum_ref, sums_ref,
    *, band, heads,
):
    length, width = tokens_ref.shape
    block = 256
    bias_ref[...] = bias_rows(table_ref, buckets_ref)
    lse_rows_ref[...] = lse_ref[...].T
    gk_ref[...] = jnp.zeros_like(gk_ref)
    gv_ref[...] = jnp.zeros_like(gv_ref)
    sums_ref[...] = jnp.zeros_like(sums_ref)

    @pl.loop(0, heads // 2)
    def _(group):
        cols = pl.ds(pl.multiple_of(group * PAIR, PAIR), PAIR)
        backward_head_prepare(cols, gm_ref, mixed_ref, delta_ref)
        gqt_ref[...] = jnp.zeros_like(gqt_ref)

        @pl.loop(0, 2)
        def _(half):
            head = group * 2 + half
            fill_bands(head, bias_ref, band, causal_ref, two_ref)
            causal_sum_ref[...] = jnp.zeros_like(causal_sum_ref)
            two_sum_ref[...] = jnp.zeros_like(two_sum_ref)
            self_backward_head(
                head, limit_ref[0], q_ref, k_ref, v_ref, gm_ref, mixed_ref, lse_rows_ref, delta_ref,
                causal_ref, two_ref, band, gk_ref, gv_ref, gqt_ref, causal_sum_ref, two_sum_ref,
            )
            sums_ref[pl.ds(head, 1), : band.causal] = fold(causal_sum_ref[...])
            sums_ref[pl.ds(head, 1), band.causal :] = fold(two_sum_ref[...])

        gq_ref[:, cols] = gqt_ref[...].T.astype(BF16)

    hot = jnp.where(one_hot(buckets_ref), 1.0, 0.0)
    gtable_ref[...] = exact_dot(sums_ref[...], hot, 1, 1)
    ggain_ref[...] = jnp.zeros_like(ggain_ref)

    def tokens_grad(rows):
        value = tokens_ref[rows, :].astype(F32)
        flipped_ref[:, rows] = (value * rms(value) * gains_ref[0:1, :]).astype(BF16).T
        grad = dot(gq_ref[rows, :], wq_ref[...], 1, 1)
        grad += dot(gk_ref[rows, :], wk_ref[...], 1, 1)
        grad += dot(gv_ref[rows, :], wv_ref[...], 1, 1)
        back, ggain = norm_back_rows(value, gains_ref[0:1, :], grad)
        ggain_ref[0:1, :] += ggain
        gtokens_ref[rows, :] = back + gfirst_ref[rows, :]

    row_blocks(length, block, tokens_grad)

    def weights(rows):
        flipped = flipped_ref[rows, :]
        dwq_ref[rows, :] = dot(flipped, gq_ref[...]).astype(BF16)
        dwk_ref[rows, :] = dot(flipped, gk_ref[...]).astype(BF16)
        dwv_ref[rows, :] = dot(flipped, gv_ref[...]).astype(BF16)

    row_blocks(width, block, weights)


def vmem(*shapes):
    return [pltpu.VMEM(shape, dtype) for shape, dtype in shapes]


def params(**kw):
    return pltpu.CompilerParams(vmem_limit_bytes=60 * 1024 * 1024, **kw)


def weight_block(number, width):
    return pl.BlockSpec((width, width), lambda *_: (0, number))


def per_device(
    inputs, encoded, out_grad, prefix, bucket_map, bias_table,
    norm_self, self_query, self_key, self_value, self_out,
    norm_cross, cross_query, cross_key, cross_value, cross_out,
    norm_feed, feed_gate, feed_up, feed_down,
):
    seqs, length, width = inputs.shape
    source = encoded.shape[1]
    heads = bias_table.shape[1]
    ff = feed_gate.shape[1]
    band = Band(length, length // 2)
    tokens = inputs.reshape(length, width)
    memory = encoded.reshape(source, width)
    gout = out_grad.reshape(length, width)
    lanes = 16
    table = jnp.pad(bias_table.T, ((0, lanes - heads), (0, 0)))
    query_buckets = lane_buckets(bucket_map, band, "queries")
    key_buckets = lane_buckets(bucket_map, band, "keys")

    attention = lax.all_gather(
        jnp.concatenate(
            [self_query, self_key, self_value, self_out, cross_query, cross_key, cross_value, cross_out], axis=1
        ),
        AXES, axis=0, tiled=True,
    )
    feed = lax.all_gather(jnp.concatenate([feed_gate, feed_up], axis=1), AXES, axis=0, tiled=True)
    down = lax.all_gather(feed_down, AXES, axis=0, tiled=True)
    gains = lax.all_gather(jnp.stack([norm_self, norm_cross, norm_feed]), AXES, axis=1, tiled=True)
    gains = jnp.pad(gains.astype(F32), ((0, 5), (0, 0)))

    whole = pl.BlockSpec(memory_space=pltpu.VMEM)
    scalar = pl.BlockSpec(memory_space=pltpu.SMEM)

    def weights(*numbers):
        return [weight_block(number, width) for number in numbers]

    def full(shape):
        return pl.BlockSpec(shape, lambda *_: (0,) * len(shape))

    def like(shape, dtype):
        return jax.ShapeDtypeStruct(shape, dtype)

    act = like((length, width), BF16)
    mem = like((source, width), BF16)
    act32 = like((length, width), F32)
    lse_shape = like((length, SUB), F32)
    outs = [act, act, act, act, lse_shape, act32, act, mem, mem, act, lse_shape, act32]
    q1, k1, v1, mixed1, lse1, first, q2, k2, v2, mixed2, lse2, second = pl.pallas_call(
        functools.partial(forward_kernel, band=band, heads=heads),
        out_shape=outs,
        grid=(1,),
        in_specs=[scalar] + [full(a.shape) for a in (tokens, memory, gains, table, query_buckets)] + weights(*range(8)),
        out_specs=[full(o.shape) for o in outs],
        scratch_shapes=vmem(
            ((lanes, band.width), F32), ((SUB, band.causal), F32), ((SUB, band.two_way), F32)
        ),
        compiler_params=params(),
        name="forward",
    )(prefix, tokens, memory, gains, table, query_buckets, *([attention] * 8))

    fblock = 256
    ggain_shape = like((8, width), F32)
    feed_out = [
        act, act32, ggain_shape, like((width, ff), BF16), like((width, ff), BF16), like((ff, width), BF16)
    ]
    output, gsecond, ggain_feed, dgate, dup, ddown = pl.pallas_call(
        feed_kernel,
        out_shape=feed_out,
        grid=(ff // fblock,),
        in_specs=[full(second.shape), full(gout.shape), full(gains.shape)]
        + [
            pl.BlockSpec((width, fblock), lambda i: (0, i)),
            pl.BlockSpec((width, fblock), lambda i: (0, i + ff // fblock)),
            pl.BlockSpec((fblock, width), lambda i: (i, 0)),
        ],
        out_specs=[full(o.shape) for o in feed_out[:3]]
        + [
            pl.BlockSpec((width, fblock), lambda i: (0, i)),
            pl.BlockSpec((width, fblock), lambda i: (0, i)),
            pl.BlockSpec((fblock, width), lambda i: (i, 0)),
        ],
        scratch_shapes=vmem(
            ((length, width), BF16), ((width, length), BF16), ((length, width), F32), ((length, width), F32),
            ((length, fblock), BF16), ((length, fblock), BF16), ((length, fblock), BF16),
        ),
        compiler_params=params(),
        name="feed",
    )(second, gout, gains, feed, feed, down)

    square = like((width, width), BF16)
    cross_out_shapes = [like((source, width), F32), act32, act, ggain_shape] + [square] * 5
    cross_in = (gsecond, first, memory, gains, q2, k2, v2, mixed1, mixed2, lse2)
    gmem, gfirst, gm1, ggain_cross, dwo, dcq, dck, dcv, dco = pl.pallas_call(
        functools.partial(cross_backward_kernel, heads=heads),
        out_shape=cross_out_shapes,
        grid=(1,),
        in_specs=[full(a.shape) for a in cross_in] + weights(3, 4, 5, 6, 7),
        out_specs=[full(o.shape) for o in cross_out_shapes],
        scratch_shapes=vmem(
            ((length, width), BF16), ((length, width), BF16), ((width, length), BF16), ((SUB, length), F32),
            ((8, length), F32), ((length, width), BF16), ((source, width), BF16), ((source, width), BF16),
            ((PAIR, length), F32),
        ),
        compiler_params=params(),
        name="cross_backward",
    )(*cross_in, *([attention] * 5))

    self_out_shapes = [act32, ggain_shape, like((lanes, NB), F32)] + [square] * 3
    self_in = (tokens, gains, table, key_buckets, q1, k1, v1, mixed1, lse1, gm1, gfirst)
    gtokens, ggain_self, gtable, dwq, dwk, dwv = pl.pallas_call(
        functools.partial(self_backward_kernel, band=band, heads=heads),
        out_shape=self_out_shapes,
        grid=(1,),
        in_specs=[scalar] + [full(a.shape) for a in self_in] + weights(0, 1, 2),
        out_specs=[full(o.shape) for o in self_out_shapes],
        scratch_shapes=vmem(
            ((lanes, band.width), F32), ((SUB, band.causal), F32), ((SUB, band.two_way), F32), ((width, length), BF16),
            ((SUB, length), F32), ((8, length), F32), ((length, width), BF16), ((length, width), BF16),
            ((length, width), BF16), ((PAIR, length), F32), ((SUB, band.causal), F32), ((SUB, band.two_way), F32),
            ((lanes, band.width), F32),
        ),
        compiler_params=params(),
        name="self_backward",
    )(prefix, *self_in, *([attention] * 3))

    table_grad = lax.psum(gtable[:heads].T, AXES)
    ggains = lax.psum_scatter(
        jnp.stack([ggain_self[0], ggain_cross[0], ggain_feed[0]]), AXES, scatter_dimension=1, tiled=True
    )

    def scatter(parts):
        return lax.psum_scatter(jnp.concatenate(parts, axis=1), AXES, scatter_dimension=0, tiled=True).astype(F32)

    feed_grads = scatter([dgate, dup])
    down_grad = lax.psum_scatter(ddown, AXES, scatter_dimension=0, tiled=True).astype(F32)
    squares = scatter([dwq, dwk, dwv, dwo, dcq, dck, dcv, dco])
    pieces = [squares[:, i * width : (i + 1) * width] for i in range(8)]
    return (
        output.reshape(inputs.shape),
        gtokens.reshape(inputs.shape),
        gmem.reshape(encoded.shape),
        table_grad,
        ggains[0], pieces[0], pieces[1], pieces[2], pieces[3],
        ggains[1], pieces[4], pieces[5], pieces[6], pieces[7],
        ggains[2], feed_grads[:, :ff], feed_grads[:, ff:], down_grad,
    )


def solution(mesh):
    rows = P(AXES, None)
    gain = P(AXES)
    block = P(AXES, None, None)
    return jax.shard_map(
        per_device,
        mesh=mesh,
        in_specs=(block, block, block, gain, P(), P())
        + (gain, rows, rows, rows, rows)
        + (gain, rows, rows, rows, rows)
        + (gain, rows, rows, rows),
        out_specs=(block, block, block, P())
        + (gain, rows, rows, rows, rows)
        + (gain, rows, rows, rows, rows)
        + (gain, rows, rows, rows),
        check_vma=False,
    )
```

```python
import functools

import jax
import jax.numpy as jnp
from jax import lax
from jax.experimental import pallas as pl
from jax.experimental.pallas import tpu as pltpu
from jax.sharding import PartitionSpec as P

DH = 64
NB = 32
PAIR = 2 * DH
SUB = 128
NEG = -1e30
F32 = jnp.float32
BF16 = jnp.bfloat16
AXES = ("dp", "fsdp")


def dot(a, b, ca=1, cb=0):
    return lax.dot_general(a, b, (((ca,), (cb,)), ((), ())), preferred_element_type=F32)


def exact_dot(a, b, ca=1, cb=0):
    return lax.dot_general(
        a,
        b,
        (((ca,), (cb,)), ((), ())),
        preferred_element_type=F32,
        precision=lax.Precision.HIGHEST,
    )


def rms(value):
    return lax.rsqrt(jnp.mean(value * value, axis=-1, keepdims=True) + 1e-06)


MESH = pl.DeviceIdType.MESH
EVERY = slice(None)


class Place:
    def __init__(self, sizes):
        self.sizes = grid_of(sizes)
        across, inner = lax.axis_index("dp"), lax.axis_index("fsdp")
        deep, high, wide, cores = self.sizes
        self.at = {
            "z": lax.div(across, high),
            "y": lax.rem(across, high),
            "x": lax.div(inner, cores),
            "c": lax.rem(inner, cores),
        }

    def device(self, **moved):
        at = {**self.at, **moved}
        deep, high, wide, cores = self.sizes
        return (at["z"] * high + at["y"], at["x"] * cores + at["c"])

    def size(self, axis):
        return self.sizes["zyxc".index(axis)]

    def others(self, axis):
        size = self.size(axis)
        return [lax.rem(self.at[axis] + step, size) for step in range(1, size)]

    def meet(self):
        barrier = pltpu.get_barrier_semaphore()
        peers = [self.device(**{axis: other}) for axis in "zyxc" for other in self.others(axis)]
        for peer in peers:
            pl.semaphore_signal(barrier, inc=1, device_id=peer, device_id_type=MESH)
        pl.semaphore_wait(barrier, len(peers))


def grid_of(sizes):
    wide = sizes["fsdp"] // 2
    return (sizes["dp"] // wide, wide, wide, 2)


class Gather:
    PHASES = 4

    def __init__(self, place, pieces, shards, outs, local_sem, send_sem, recv_sem):
        self.place, self.pieces, self.shards, self.outs = place, pieces, shards, outs
        self.local_sem, self.send_sem, self.recv_sem = local_sem, send_sem, recv_sem

    @staticmethod
    def copies(sizes, pieces):
        return len(pieces) * sum(size - 1 for size in grid_of(sizes))

    def view(self, piece, *index):
        array, first, rows, order = piece
        start = self.place.at["c"] * self.shards[array].shape[0] + first
        return self.outs[array].at[(*index, pl.ds(pl.multiple_of(start, 8), rows), EVERY)]

    def phase(self, number, phase):
        piece = self.pieces[number]
        place = self.place
        at = place.at
        deep, high, wide, cores = place.sizes
        array, first, rows, order = piece
        base = number * sum(size - 1 for size in place.sizes)
        if phase == 0:
            axis, skip = "z", 0
            source = self.shards[array].at[pl.ds(first, rows), :]
            target = self.view(piece, at["z"], at["y"], at["x"])
        elif phase == 3:
            axis, skip = "c", deep + high + wide - 3
            source = target = self.view(piece, EVERY, EVERY, EVERY)
        else:
            axis = order[phase - 1]
            skip = deep - 1 + (phase - 1) * (high - 1)
            if phase == 1:
                source = self.view(piece, EVERY, at["y"], at["x"])
            elif axis == "y":
                source = self.view(piece, EVERY, at["y"], EVERY)
            else:
                source = self.view(piece, EVERY, EVERY, at["x"])
            target = source
        copies = []
        for step, other in enumerate(place.others(axis)):
            slot = base + skip + step
            copies.append(
                pltpu.make_async_remote_copy(
                    source,
                    target,
                    self.send_sem.at[slot],
                    self.recv_sem.at[slot],
                    device_id=place.device(**{axis: other}),
                    device_id_type=MESH,
                )
            )
        if phase == 0:
            copies.append(pltpu.make_async_copy(source, target, self.local_sem.at[number]))
        return copies

    def advance(self, numbers, phase):
        for number in numbers:
            if phase > 0:
                for copy in self.phase(number, phase - 1):
                    copy.wait()
            if phase < self.PHASES:
                for copy in self.phase(number, phase):
                    copy.start()


class Band:
    def __init__(self, length, reach):
        self.reach = reach
        self.causal = length + reach
        self.two_way = 2 * reach
        self.width = self.causal + self.two_way
        self.query_zero = length - SUB
        self.query_zero_two = reach - SUB
        self.key_zero = reach - SUB

    def distances(self, rows):
        causal = lax.broadcasted_iota(jnp.int32, (1, self.causal), 1)
        two_way = lax.broadcasted_iota(jnp.int32, (1, self.two_way), 1)
        if rows == "queries":
            causal, two_way = self.query_zero - causal, self.query_zero_two - two_way
            return (
                jnp.where(causal <= -self.reach, causal + self.causal, causal),
                jnp.where(two_way <= -self.reach, two_way + self.two_way, two_way),
            )
        causal, two_way = causal - self.key_zero, two_way - self.key_zero
        return (
            jnp.where(causal >= self.causal - self.reach, causal - self.causal, causal),
            jnp.where(two_way >= self.reach, two_way - self.two_way, two_way),
        )


def one_hot(map_ref, band, rows):
    bucket = lax.broadcasted_iota(jnp.int32, (NB, 1), 0)

    def edges(row, number):
        entries = map_ref[row : row + 1, :]
        below = jnp.sum((entries < number).astype(jnp.int32), axis=1, keepdims=True)
        return below, below + jnp.sum((entries == number).astype(jnp.int32), axis=1, keepdims=True)

    causal, two_way = band.distances(rows)
    low, high = edges(0, bucket)
    one = (causal >= low) & (causal < high)
    ahead = bucket >= NB // 2
    low, high = edges(1, jnp.where(ahead, bucket - NB // 2, bucket))
    apart = jnp.abs(two_way)
    two = (apart >= low) & (apart < high) & ((two_way < 0) == ahead)
    return jnp.concatenate([jnp.where(one, 1.0, 0.0), jnp.where(two, 1.0, 0.0)], axis=1), causal


def spread(row, width):
    return pltpu.roll(jnp.broadcast_to(row, (SUB, width)), 0, 1, stride=1, stride_axis=0)


def fold(band):
    width = band.shape[1]
    half = SUB // 2
    while half >= 8:
        band = band[:half] + pltpu.roll(band[half:], width - half, 1)
        half //= 2
    row = lax.broadcasted_iota(jnp.int32, band.shape, 0)
    for bit in (4, 2, 1):
        band = jnp.where((row & bit) != 0, pltpu.roll(band, width - bit, 1), band)
    return jnp.sum(band, axis=0, keepdims=True)


def fill_bands(head, bias_ref, band, causal_ref, two_ref):
    row = bias_ref[pl.ds(head, 1), :]
    causal_ref[...] = spread(row[:, : band.causal], band.causal)
    two_ref[...] = spread(row[:, band.causal :], band.two_way)


def bias_rows(table_ref, map_ref, band, rows):
    hot, causal = one_hot(map_ref, band, rows)
    bias = dot(table_ref[...], hot.astype(BF16), 0, 0)
    return jnp.concatenate([jnp.where(causal < 0, NEG, bias[:, : band.causal]), bias[:, band.causal :]], axis=1)


def head_cols(head):
    group = head // 2
    return pl.ds(pl.multiple_of(group * PAIR, PAIR), PAIR), head % 2


def pick_lanes(half):
    return lax.broadcasted_iota(jnp.int32, (1, PAIR), 1) // DH == half


def soft_rows(scores):
    high = jnp.max(scores, axis=-1, keepdims=True)
    weights = jnp.exp(scores - high)
    total = jnp.sum(weights, axis=-1, keepdims=True)
    return weights.astype(BF16), total, high + jnp.log(total)


def store_head(mixed_ref, lse_ref, rows, cols, head, half, out, total, lse):
    pick = pick_lanes(half)
    mixed_ref[rows, cols] = jnp.where(pick, (out / total).astype(BF16), mixed_ref[rows, cols])
    lane = lax.broadcasted_iota(jnp.int32, (1, lse_ref.shape[1]), 1)
    lse_ref[rows, :] = jnp.where(lane == head, lse, lse_ref[rows, :])


def self_forward_head(head, limit, q_ref, k_ref, v_ref, causal_ref, two_ref, band, mixed_ref, lse_ref):
    length = q_ref.shape[0]
    cols, half = head_cols(head)
    pick = pick_lanes(half)
    block = 256
    for start in range(0, length, block):
        keys = max(start + block, band.reach)
        rows = pl.ds(start, block)
        query = jnp.where(pick, q_ref[rows, cols], 0)
        scores = dot(query, k_ref[pl.ds(0, keys), cols], 1, 1)
        parts = []
        for first in range(start, start + block, SUB):
            at = band.query_zero - first
            bias = causal_ref[:, at : at + keys]
            if start < band.reach:
                at = band.query_zero_two - first
                two = two_ref[:, at : at + keys]
                inside = (first + lax.broadcasted_iota(jnp.int32, (SUB, keys), 0) < limit) & (
                    lax.broadcasted_iota(jnp.int32, (SUB, keys), 1) < limit
                )
                bias = jnp.where(inside, two, bias)
            parts.append(bias)
        weights, total, lse = soft_rows(scores + jnp.concatenate(parts, axis=0))
        out = dot(weights, v_ref[pl.ds(0, keys), cols])
        store_head(mixed_ref, lse_ref, rows, cols, head, half, out, total, lse)


def cross_forward_head(head, q_ref, k_ref, v_ref, mixed_ref, lse_ref):
    length = q_ref.shape[0]
    cols, half = head_cols(head)
    pick = pick_lanes(half)
    block = 256
    for start in range(0, length, block):
        rows = pl.ds(start, block)
        query = jnp.where(pick, q_ref[rows, cols], 0)
        weights, total, lse = soft_rows(dot(query, k_ref[:, cols], 1, 1))
        out = dot(weights, v_ref[:, cols])
        store_head(mixed_ref, lse_ref, rows, cols, head, half, out, total, lse)


def row_blocks(count, block, step):
    @pl.loop(0, count // block)
    def _(index):
        step(pl.ds(pl.multiple_of(index * block, block), block))


def gain_rows(gathered, width):
    devices = gathered.shape[0]
    share = width // devices
    lane = lax.broadcasted_iota(jnp.int32, (SUB, width), 1)
    select = jnp.where(lax.rem(lane, share) == lax.broadcasted_iota(jnp.int32, (SUB, width), 0), 1.0, 0.0)
    first = share * lax.broadcasted_iota(jnp.int32, (devices, width), 0)
    lane = lax.broadcasted_iota(jnp.int32, (devices, width), 1)
    own = (lane >= first) & (lane < first + share)
    rows = []
    for number in range(8):
        spread_out = exact_dot(gathered[:, number, :], select)
        rows.append(jnp.sum(jnp.where(own, spread_out, 0.0), axis=0, keepdims=True))
    return jnp.concatenate(rows, axis=0)


ATTENTION = 8
SHARDS = 12


def gather_pieces(rows, down_rows):
    head, tail = rows // 3 // 8 * 8, rows - rows // 3 // 8 * 8
    first = [(0, 0, rows, "xy"), (1, 0, rows, "yx"), (2, 0, head, "xy"), (2, head, tail, "yx"), (11, 0, 8, "xy")]
    rest = [(3, 0, rows, "xy"), (4, 0, rows, "yx"), (5, 0, rows, "xy"), (6, 0, rows, "yx")]
    rest += [(7, 0, tail, "xy"), (7, tail, head, "yx")]
    feed = [(8, 0, rows, "xy"), (9, 0, rows, "yx")]
    feed += [(10, 0, down_rows // 2, "xy"), (10, down_rows // 2, down_rows // 2, "yx")]
    pieces = first + rest + feed
    numbers = list(range(len(pieces)))
    groups = numbers[: len(first)], numbers[len(first) : len(first) + len(rest)], numbers[len(first) + len(rest) :]
    return pieces, groups


def forward_kernel(
    limit_ref, tokens_ref, memory_ref, table_ref, map_ref, gain1_ref, gain2_ref, gain3_ref, *refs, band, heads, plan,
):
    count = SHARDS - 1 if plan else ATTENTION
    shards, refs = refs[:count], refs[count:]
    if plan:
        gathered, refs = refs[:SHARDS], refs[SHARDS:]
    else:
        gathered = shards
    (
        gains_ref, q1_ref, k1_ref, v1_ref, mixed1_ref, lse1_ref, first_ref,
        q2_ref, k2_ref, v2_ref, mixed2_ref, lse2_ref, second_ref,
        bias_ref, causal_ref, two_ref, weights_ref, share_ref, tile_ref, load_sem, *gather_sems,
    ) = refs
    length, width = tokens_ref.shape
    if plan:
        sizes, pieces, (soon, later, feed) = plan
        place = Place(sizes)
        gather = Gather(place, pieces, (*shards, share_ref), gathered, *gather_sems)

    def advance(*steps):
        if plan:
            for numbers, phase in steps:
                gather.advance({"soon": soon, "later": later, "feed": feed}[numbers], phase)

    def load(number):
        return pltpu.make_async_copy(gathered[number].reshape(width, width), weights_ref.at[number], load_sem.at[number])

    def load_tile():
        return pltpu.make_async_copy(gathered[SHARDS - 1].reshape(tile_ref.shape), tile_ref, load_sem.at[ATTENTION])

    gain_refs = (gain1_ref, gain2_ref, gain3_ref)
    if plan:
        share_ref[...] = jnp.zeros_like(share_ref)
        for number, gain_ref in enumerate(gain_refs):
            share_ref[number : number + 1, : gain_ref.shape[1]] = gain_ref[...].astype(F32)
        place.meet()
    advance(("soon", 0))
    bias_ref[...] = bias_rows(table_ref, map_ref, band, "queries")
    lse1_ref[...] = jnp.zeros_like(lse1_ref)
    lse2_ref[...] = jnp.zeros_like(lse2_ref)
    mixed1_ref[...] = jnp.zeros_like(mixed1_ref)
    mixed2_ref[...] = jnp.zeros_like(mixed2_ref)
    advance(("soon", 1), ("later", 0), ("feed", 0), ("soon", 2), ("soon", 3), ("later", 1), ("soon", 4))
    for number in range(3):
        load(number).start()
    if plan:
        load_tile().start()
        load_tile().wait()
        gains_ref[...] = gain_rows(tile_ref[...], width)
    else:
        gains_ref[...] = jnp.zeros_like(gains_ref)
        for number, gain_ref in enumerate(gain_refs):
            gains_ref[number : number + 1, :] = gain_ref[...].astype(F32)
    for number in range(3):
        load(number).wait()

    def project_self(rows):
        value = tokens_ref[rows, :].astype(F32)
        normed = (value * rms(value) * gains_ref[0:1, :]).astype(BF16)
        q1_ref[rows, :] = dot(normed, weights_ref[0]).astype(BF16)
        k1_ref[rows, :] = dot(normed, weights_ref[1]).astype(BF16)
        v1_ref[rows, :] = dot(normed, weights_ref[2]).astype(BF16)

    row_blocks(length, 256, project_self)
    advance(("later", 2))

    @pl.loop(0, heads)
    def _(head):
        fill_bands(head, bias_ref, band, causal_ref, two_ref)
        self_forward_head(head, limit_ref[0], q1_ref, k1_ref, v1_ref, causal_ref, two_ref, band, mixed1_ref, lse1_ref)

        @pl.when(head == heads // 4)
        def _():
            advance(("feed", 1), ("later", 3))

        @pl.when(head == heads // 2)
        def _():
            advance(("later", 4))
            for number in range(3, ATTENTION):
                load(number).start()
            advance(("feed", 2))

    for number in range(3, ATTENTION):
        load(number).wait()

    def project_memory(rows):
        k2_ref[rows, :] = dot(memory_ref[rows, :], weights_ref[5]).astype(BF16)
        v2_ref[rows, :] = dot(memory_ref[rows, :], weights_ref[6]).astype(BF16)

    row_blocks(memory_ref.shape[0], 256, project_memory)

    def project_cross(rows):
        value = tokens_ref[rows, :].astype(F32) + dot(mixed1_ref[rows, :], weights_ref[3])
        first_ref[rows, :] = value
        normed = (value * rms(value) * gains_ref[1:2, :]).astype(BF16)
        q2_ref[rows, :] = dot(normed, weights_ref[4]).astype(BF16)

    row_blocks(length, 256, project_cross)
    advance(("feed", 3))

    @pl.loop(0, heads)
    def _(head):
        cross_forward_head(head, q2_ref, k2_ref, v2_ref, mixed2_ref, lse2_ref)

    def project_second(rows):
        second_ref[rows, :] = first_ref[rows, :] + dot(mixed2_ref[rows, :], weights_ref[7])

    row_blocks(length, 256, project_second)
    advance(("feed", 4))


def norm_back_rows(value, gain, grad):
    scale = rms(value)
    unit = value * scale
    scaled = grad * gain
    back = scale * (scaled - unit * jnp.mean(scaled * unit, axis=-1, keepdims=True))
    return back, jnp.sum(grad * unit, axis=0, keepdims=True)


GELU_A = 0.7978845608028654
GELU_B = 0.044715


def feed_kernel(
    second_ref, gout_ref, gains_ref, gate_ref, up_ref, down_ref,
    output_ref, gsecond_ref, ggain_ref, dgate_ref, dup_ref, ddown_ref,
    normed_ref, flipped_ref, out_ref, back_ref, hidden_ref, ggate_ref, gup_ref,
):
    step = pl.program_id(0)
    length = second_ref.shape[0]
    block = 256

    @pl.when(step == 0)
    def _():
        def prepare(rows):
            value = second_ref[rows, :]
            normed = (value * rms(value) * gains_ref[2:3, :]).astype(BF16)
            normed_ref[rows, :] = normed
            flipped_ref[:, rows] = normed.T
            out_ref[rows, :] = value
            back_ref[rows, :] = jnp.zeros_like(value)

        row_blocks(length, block, prepare)

    def rows_step(rows):
        normed = normed_ref[rows, :]
        gate = dot(normed, gate_ref[...])
        upward = dot(normed, up_ref[...])
        square = gate * gate
        bend = jnp.tanh(GELU_A * gate * (1.0 + GELU_B * square))
        half = 0.5 * (1.0 + bend)
        active = gate * half
        hidden = (active * upward).astype(BF16)
        hidden_ref[rows, :] = hidden
        out_ref[rows, :] += dot(hidden, down_ref[...])
        ghidden = dot(gout_ref[rows, :], down_ref[...], 1, 1)
        slope = half + 0.5 * gate * (1.0 - bend * bend) * (GELU_A * (1.0 + 3.0 * GELU_B * square))
        ggate = (ghidden * upward * slope).astype(BF16)
        gup = (ghidden * active).astype(BF16)
        ggate_ref[rows, :] = ggate
        gup_ref[rows, :] = gup
        back_ref[rows, :] += dot(ggate, gate_ref[...], 1, 1) + dot(gup, up_ref[...], 1, 1)

    row_blocks(length, block, rows_step)
    ddown_ref[...] = dot(hidden_ref[...].T, gout_ref[...]).astype(BF16)
    dgate_ref[...] = dot(flipped_ref[...], ggate_ref[...]).astype(BF16)
    dup_ref[...] = dot(flipped_ref[...], gup_ref[...]).astype(BF16)

    @pl.when(step == pl.num_programs(0) - 1)
    def _():
        ggain_ref[...] = jnp.zeros_like(ggain_ref)

        def finish(rows):
            output_ref[rows, :] = out_ref[rows, :].astype(BF16)
            back, ggain = norm_back_rows(second_ref[rows, :], gains_ref[2:3, :], back_ref[rows, :])
            gsecond_ref[rows, :] = back + gout_ref[rows, :].astype(F32)
            ggain_ref[0:1, :] += ggain

        row_blocks(length, block, finish)


def backward_head_prepare(group_cols, gm_ref, mixed_ref, delta_ref):
    product = (gm_ref[:, group_cols].astype(F32) * mixed_ref[:, group_cols].astype(F32)).T
    delta_ref[0:1, :] = jnp.sum(product[:DH], axis=0, keepdims=True)
    delta_ref[1:2, :] = jnp.sum(product[DH:], axis=0, keepdims=True)


def backward_block(key_rows, cols, half, start, bias, q_ref, k_ref, v_ref, gm_ref, lse, delta, gk_ref, gv_ref, gqt_ref):
    length = q_ref.shape[0]
    pick = pick_lanes(half)
    queries = pl.ds(start, length - start)
    query = jnp.where(pick, q_ref[queries, cols], 0)
    grad = jnp.where(pick, gm_ref[queries, cols], 0)
    keys = k_ref[key_rows, cols]
    scores = dot(keys, query, 1, 1)
    if bias is not None:
        scores = scores + bias
    probs = jnp.exp(scores - lse[:, start:])
    gv = dot(probs.astype(BF16), grad)
    gprobs = dot(v_ref[key_rows, cols], grad, 1, 1)
    gscores = probs * (gprobs - delta[:, start:])
    low = gscores.astype(BF16)
    gk = dot(low, query)
    gk_ref[key_rows, cols] = jnp.where(pick, gk.astype(BF16), gk_ref[key_rows, cols])
    gv_ref[key_rows, cols] = jnp.where(pick, gv.astype(BF16), gv_ref[key_rows, cols])
    gqt_ref[:, queries] += dot(jnp.where(pick, keys, 0).T, low)
    return gscores


def self_backward_head(
    head, limit, q_ref, k_ref, v_ref, gm_ref, mixed_ref, lse_ref, delta_ref, causal_ref, two_ref, band,
    gk_ref, gv_ref, gqt_ref, causal_sum_ref, two_sum_ref,
):
    length = q_ref.shape[0]
    cols, half = head_cols(head)
    lse = lse_ref[pl.ds(head, 1), :]
    delta = delta_ref[pl.ds(half, 1), :]
    reach = band.reach
    block = 256
    for first in range(0, length, block):
        start = 0 if first < reach else first
        count = length - start
        parts = []
        for key in range(first, first + block, SUB):
            at = band.key_zero - key + start
            bias = causal_ref[:, at : at + count]
            if first < reach:
                at = band.key_zero - key
                two = two_ref[:, at : at + reach]
                inside = (key + lax.broadcasted_iota(jnp.int32, (SUB, reach), 0) < limit) & (
                    lax.broadcasted_iota(jnp.int32, (SUB, reach), 1) < limit
                )
                bias = jnp.concatenate([jnp.where(inside, two, bias[:, :reach]), bias[:, reach:]], axis=1)
            parts.append(bias)
        gscores = backward_block(
            pl.ds(first, block), cols, half, start, jnp.concatenate(parts, axis=0),
            q_ref, k_ref, v_ref, gm_ref, lse, delta, gk_ref, gv_ref, gqt_ref,
        )
        for key in range(first, first + block, SUB):
            part = gscores[key - first : key - first + SUB]
            at = band.key_zero - key + start
            if first < reach:
                inside = (key + lax.broadcasted_iota(jnp.int32, (SUB, reach), 0) < limit) & (
                    lax.broadcasted_iota(jnp.int32, (SUB, reach), 1) < limit
                )
                head_part = part[:, :reach]
                at_two = band.key_zero - key
                two_sum_ref[:, at_two : at_two + reach] += jnp.where(inside, head_part, 0.0)
                causal_sum_ref[:, at : at + reach] += jnp.where(inside, 0.0, head_part)
                causal_sum_ref[:, at + reach : at + count] += part[:, reach:]
            else:
                causal_sum_ref[:, at : at + count] += part


def cross_backward_kernel(
    gsecond_ref, first_ref, memory_ref, gains_ref, q_ref, k_ref, v_ref, mixed1_ref, mixed2_ref, lse_ref,
    wo_ref, cq_ref, ck_ref, cv_ref, co_ref,
    gmem_ref, gfirst_ref, gm1_ref, ggain_ref, dwo_ref, dcq_ref, dck_ref, dcv_ref, dco_ref,
    gm_ref, branch_ref, flipped_ref, lse_rows_ref, delta_ref, gq_ref, gk_ref, gv_ref, gqt_ref,
    *, heads,
):
    length, width = first_ref.shape
    source = memory_ref.shape[0]
    block = 256

    def prepare(rows):
        branch = gsecond_ref[rows, :].astype(BF16)
        branch_ref[rows, :] = branch
        gm_ref[rows, :] = dot(branch, co_ref[...], 1, 1).astype(BF16)
        flipped_ref[:, rows] = mixed2_ref[rows, :].T

    row_blocks(length, block, prepare)

    def out_grad(rows):
        dco_ref[rows, :] = dot(flipped_ref[rows, :], branch_ref[...]).astype(BF16)

    row_blocks(width, block, out_grad)
    lse_rows_ref[...] = lse_ref[...].T
    gk_ref[...] = jnp.zeros_like(gk_ref)
    gv_ref[...] = jnp.zeros_like(gv_ref)

    @pl.loop(0, heads // 2)
    def _(group):
        cols = pl.ds(pl.multiple_of(group * PAIR, PAIR), PAIR)
        backward_head_prepare(cols, gm_ref, mixed2_ref, delta_ref)
        gqt_ref[...] = jnp.zeros_like(gqt_ref)

        @pl.loop(0, 2)
        def _(half):
            head = group * 2 + half
            for first in range(0, source, block):
                backward_block(
                    pl.ds(first, block), cols, half, 0, None, q_ref, k_ref, v_ref, gm_ref,
                    lse_rows_ref[pl.ds(head, 1), :], delta_ref[pl.ds(half, 1), :], gk_ref, gv_ref, gqt_ref,
                )

        gq_ref[:, cols] = gqt_ref[...].T.astype(BF16)

    def memory_grad(rows):
        gmem_ref[rows, :] = dot(gk_ref[rows, :], ck_ref[...], 1, 1) + dot(gv_ref[rows, :], cv_ref[...], 1, 1)
        flipped_ref[:, rows] = memory_ref[rows, :].T

    row_blocks(source, block, memory_grad)

    def memory_weights(rows):
        flipped = flipped_ref[rows, :source]
        dck_ref[rows, :] = dot(flipped, gk_ref[...]).astype(BF16)
        dcv_ref[rows, :] = dot(flipped, gv_ref[...]).astype(BF16)

    row_blocks(width, block, memory_weights)
    ggain_ref[...] = jnp.zeros_like(ggain_ref)

    def first_grad(rows):
        value = first_ref[rows, :]
        flipped_ref[:, rows] = (value * rms(value) * gains_ref[1:2, :]).astype(BF16).T
        back, ggain = norm_back_rows(value, gains_ref[1:2, :], dot(gq_ref[rows, :], cq_ref[...], 1, 1))
        ggain_ref[0:1, :] += ggain
        gfirst = back + gsecond_ref[rows, :]
        gfirst_ref[rows, :] = gfirst
        branch = gfirst.astype(BF16)
        branch_ref[rows, :] = branch
        gm1_ref[rows, :] = dot(branch, wo_ref[...], 1, 1).astype(BF16)

    row_blocks(length, block, first_grad)

    def query_weights(rows):
        dcq_ref[rows, :] = dot(flipped_ref[rows, :], gq_ref[...]).astype(BF16)

    row_blocks(width, block, query_weights)

    def flip_mixed(rows):
        flipped_ref[:, rows] = mixed1_ref[rows, :].T

    row_blocks(length, block, flip_mixed)

    def out_weights(rows):
        dwo_ref[rows, :] = dot(flipped_ref[rows, :], branch_ref[...]).astype(BF16)

    row_blocks(width, block, out_weights)


def self_backward_kernel(
    limit_ref, tokens_ref, gains_ref, table_ref, map_ref, q_ref, k_ref, v_ref, mixed_ref, lse_ref, gm_ref, gfirst_ref,
    wq_ref, wk_ref, wv_ref,
    gtokens_ref, ggain_ref, gtable_ref, dwq_ref, dwk_ref, dwv_ref,
    bias_ref, causal_ref, two_ref, flipped_ref, lse_rows_ref, delta_ref, gq_ref, gk_ref, gv_ref, gqt_ref,
    causal_sum_ref, two_sum_ref, sums_ref,
    *, band, heads,
):
    length, width = tokens_ref.shape
    block = 256
    bias_ref[...] = bias_rows(table_ref, map_ref, band, "keys")
    lse_rows_ref[...] = lse_ref[...].T
    gk_ref[...] = jnp.zeros_like(gk_ref)
    gv_ref[...] = jnp.zeros_like(gv_ref)
    sums_ref[...] = jnp.zeros_like(sums_ref)

    @pl.loop(0, heads // 2)
    def _(group):
        cols = pl.ds(pl.multiple_of(group * PAIR, PAIR), PAIR)
        backward_head_prepare(cols, gm_ref, mixed_ref, delta_ref)
        gqt_ref[...] = jnp.zeros_like(gqt_ref)

        @pl.loop(0, 2)
        def _(half):
            head = group * 2 + half
            fill_bands(head, bias_ref, band, causal_ref, two_ref)
            causal_sum_ref[...] = jnp.zeros_like(causal_sum_ref)
            two_sum_ref[...] = jnp.zeros_like(two_sum_ref)
            self_backward_head(
                head, limit_ref[0], q_ref, k_ref, v_ref, gm_ref, mixed_ref, lse_rows_ref, delta_ref,
                causal_ref, two_ref, band, gk_ref, gv_ref, gqt_ref, causal_sum_ref, two_sum_ref,
            )
            sums_ref[pl.ds(head, 1), : band.causal] = fold(causal_sum_ref[...])
            sums_ref[pl.ds(head, 1), band.causal :] = fold(two_sum_ref[...])

        gq_ref[:, cols] = gqt_ref[...].T.astype(BF16)

    hot, unused = one_hot(map_ref, band, "keys")
    gtable_ref[...] = exact_dot(sums_ref[...], hot, 1, 1)
    ggain_ref[...] = jnp.zeros_like(ggain_ref)

    def tokens_grad(rows):
        value = tokens_ref[rows, :].astype(F32)
        flipped_ref[:, rows] = (value * rms(value) * gains_ref[0:1, :]).astype(BF16).T
        grad = dot(gq_ref[rows, :], wq_ref[...], 1, 1)
        grad += dot(gk_ref[rows, :], wk_ref[...], 1, 1)
        grad += dot(gv_ref[rows, :], wv_ref[...], 1, 1)
        back, ggain = norm_back_rows(value, gains_ref[0:1, :], grad)
        ggain_ref[0:1, :] += ggain
        gtokens_ref[rows, :] = back + gfirst_ref[rows, :]

    row_blocks(length, block, tokens_grad)

    def weights(rows):
        flipped = flipped_ref[rows, :]
        dwq_ref[rows, :] = dot(flipped, gq_ref[...]).astype(BF16)
        dwk_ref[rows, :] = dot(flipped, gk_ref[...]).astype(BF16)
        dwv_ref[rows, :] = dot(flipped, gv_ref[...]).astype(BF16)

    row_blocks(width, block, weights)


def vmem(*shapes):
    return [pltpu.VMEM(shape, dtype) for shape, dtype in shapes]


def params(**kw):
    return pltpu.CompilerParams(vmem_limit_bytes=60 * 1024 * 1024, **kw)


def per_device(
    inputs, encoded, out_grad, prefix, bucket_map, bias_table,
    norm_self, self_query, self_key, self_value, self_out,
    norm_cross, cross_query, cross_key, cross_value, cross_out,
    norm_feed, feed_gate, feed_up, feed_down,
):
    seqs, length, width = inputs.shape
    source = encoded.shape[1]
    heads = bias_table.shape[1]
    ff = feed_gate.shape[1]
    band = Band(length, length // 2)
    tokens = inputs.reshape(length, width)
    memory = encoded.reshape(source, width)
    gout = out_grad.reshape(length, width)
    gains_in = [norm_self, norm_cross, norm_feed]
    projections = [self_query, self_key, self_value, self_out, cross_query, cross_key, cross_value, cross_out]
    feeds = [feed_gate, feed_up, feed_down]
    sizes = dict(dp=lax.axis_size("dp"), fsdp=lax.axis_size("fsdp"))
    devices = sizes["dp"] * sizes["fsdp"]
    own = self_query.shape[0] % 8 == 0
    if own:
        pieces, groups = gather_pieces(self_query.shape[0], feed_down.shape[0])
        plan = (sizes, pieces, groups)
        copies = Gather.copies(sizes, pieces)
        shards = projections + feeds
    else:
        plan = None
        gains_in = [lax.all_gather(gain, AXES, axis=0, tiled=True) for gain in gains_in]
        shards = [lax.all_gather(shard, AXES, axis=0, tiled=True) for shard in projections]
        gate_full, up_full, down = [lax.all_gather(shard, AXES, axis=0, tiled=True) for shard in feeds]
    gains_in = [gain.reshape(1, -1) for gain in gains_in]

    remote = pl.BlockSpec(memory_space=pl.ANY)
    scalar = pl.BlockSpec(memory_space=pltpu.SMEM)

    def full(shape):
        return pl.BlockSpec(shape, lambda *_: (0,) * len(shape))

    def like(shape, dtype):
        return jax.ShapeDtypeStruct(shape, dtype)

    act = like((length, width), BF16)
    mem = like((source, width), BF16)
    act32 = like((length, width), F32)
    lse_shape = like((length, SUB), F32)
    gain_shape = like((8, width), F32)
    outs = [gain_shape, act, act, act, act, lse_shape, act32, act, mem, mem, act, lse_shape, act32]
    gathered_shapes = []
    if own:
        chips, cores = grid_of(sizes)[:3], grid_of(sizes)[3]
        gathered_shapes = [like(chips + (cores * shard.shape[0], shard.shape[1]), shard.dtype) for shard in shards]
        gathered_shapes.append(like(chips + (cores * 8, SUB), F32))
    forward_in = (tokens, memory, bias_table, bucket_map, *gains_in)
    results = pl.pallas_call(
        functools.partial(forward_kernel, band=band, heads=heads, plan=plan),
        out_shape=gathered_shapes + outs,
        grid=(1,),
        in_specs=[scalar] + [full(a.shape) for a in forward_in] + [remote] * len(shards),
        out_specs=[remote] * len(gathered_shapes) + [full(o.shape) for o in outs],
        scratch_shapes=vmem(
            ((heads, band.width), F32), ((SUB, band.causal), F32), ((SUB, band.two_way), F32),
            ((ATTENTION, width, width), BF16), ((8, SUB), F32), ((devices, 8, SUB), F32),
        )
        + [pltpu.SemaphoreType.DMA((ATTENTION + 1,))]
        + ([pltpu.SemaphoreType.DMA((number,)) for number in (len(pieces), copies, copies)] if own else []),
        compiler_params=params(collective_id=0, has_side_effects=True) if own else params(),
        name="forward",
    )(prefix, *forward_in, *shards)
    attention = shards
    if own:
        gathered, results = results[:SHARDS], results[SHARDS:]
        attention = [part.reshape(width, width) for part in gathered[:ATTENTION]]
        gate_full, up_full = gathered[8].reshape(width, ff), gathered[9].reshape(width, ff)
        down = gathered[10].reshape(ff, width)
    gains, q1, k1, v1, mixed1, lse1, first, q2, k2, v2, mixed2, lse2, second = results

    fblock = 256
    ggain_shape = like((8, width), F32)
    feed_out = [
        act, act32, ggain_shape, like((width, ff), BF16), like((width, ff), BF16), like((ff, width), BF16)
    ]
    output, gsecond, ggain_feed, dgate, dup, ddown = pl.pallas_call(
        feed_kernel,
        out_shape=feed_out,
        grid=(ff // fblock,),
        in_specs=[full(second.shape), full(gout.shape), full(gains.shape)]
        + [
            pl.BlockSpec((width, fblock), lambda i: (0, i)),
            pl.BlockSpec((width, fblock), lambda i: (0, i)),
            pl.BlockSpec((fblock, width), lambda i: (i, 0)),
        ],
        out_specs=[full(o.shape) for o in feed_out[:3]]
        + [
            pl.BlockSpec((width, fblock), lambda i: (0, i)),
            pl.BlockSpec((width, fblock), lambda i: (0, i)),
            pl.BlockSpec((fblock, width), lambda i: (i, 0)),
        ],
        scratch_shapes=vmem(
            ((length, width), BF16), ((width, length), BF16), ((length, width), F32), ((length, width), F32),
            ((length, fblock), BF16), ((length, fblock), BF16), ((length, fblock), BF16),
        ),
        compiler_params=params(),
        name="feed",
    )(second, gout, gains, gate_full, up_full, down)

    square = like((width, width), BF16)
    cross_out_shapes = [like((source, width), F32), act32, act, ggain_shape] + [square] * 5
    cross_in = (gsecond, first, memory, gains, q2, k2, v2, mixed1, mixed2, lse2)
    gmem, gfirst, gm1, ggain_cross, dwo, dcq, dck, dcv, dco = pl.pallas_call(
        functools.partial(cross_backward_kernel, heads=heads),
        out_shape=cross_out_shapes,
        grid=(1,),
        in_specs=[full(a.shape) for a in cross_in] + [full((width, width))] * 5,
        out_specs=[full(o.shape) for o in cross_out_shapes],
        scratch_shapes=vmem(
            ((length, width), BF16), ((length, width), BF16), ((width, length), BF16), ((SUB, length), F32),
            ((8, length), F32), ((length, width), BF16), ((source, width), BF16), ((source, width), BF16),
            ((PAIR, length), F32),
        ),
        compiler_params=params(),
        name="cross_backward",
    )(*cross_in, *attention[3:])

    self_out_shapes = [act32, ggain_shape, like((heads, NB), F32)] + [square] * 3
    self_in = (tokens, gains, bias_table, bucket_map, q1, k1, v1, mixed1, lse1, gm1, gfirst)
    gtokens, ggain_self, gtable, dwq, dwk, dwv = pl.pallas_call(
        functools.partial(self_backward_kernel, band=band, heads=heads),
        out_shape=self_out_shapes,
        grid=(1,),
        in_specs=[scalar] + [full(a.shape) for a in self_in] + [full((width, width))] * 3,
        out_specs=[full(o.shape) for o in self_out_shapes],
        scratch_shapes=vmem(
            ((heads, band.width), F32), ((SUB, band.causal), F32), ((SUB, band.two_way), F32), ((width, length), BF16),
            ((SUB, length), F32), ((8, length), F32), ((length, width), BF16), ((length, width), BF16),
            ((length, width), BF16), ((PAIR, length), F32), ((SUB, band.causal), F32), ((SUB, band.two_way), F32),
            ((heads, band.width), F32),
        ),
        compiler_params=params(),
        name="self_backward",
    )(prefix, *self_in, *attention[:3])

    table_grad = lax.psum(gtable.T, AXES)
    ggains = lax.psum_scatter(
        jnp.stack([ggain_self[0], ggain_cross[0], ggain_feed[0]]), AXES, scatter_dimension=1, tiled=True
    )

    def scatter(parts):
        return lax.psum_scatter(jnp.concatenate(parts, axis=1), AXES, scatter_dimension=0, tiled=True).astype(F32)

    feed_grads = scatter([dgate, dup])
    down_grad = lax.psum_scatter(ddown, AXES, scatter_dimension=0, tiled=True).astype(F32)
    squares = scatter([dwq, dwk, dwv, dwo, dcq, dck, dcv, dco])
    pieces = [squares[:, i * width : (i + 1) * width] for i in range(8)]
    return (
        output.reshape(inputs.shape),
        gtokens.reshape(inputs.shape),
        gmem.reshape(encoded.shape),
        table_grad,
        ggains[0], pieces[0], pieces[1], pieces[2], pieces[3],
        ggains[1], pieces[4], pieces[5], pieces[6], pieces[7],
        ggains[2], feed_grads[:, :ff], feed_grads[:, ff:], down_grad,
    )


def solution(mesh):
    rows = P(AXES, None)
    gain = P(AXES)
    block = P(AXES, None, None)
    return jax.shard_map(
        per_device,
        mesh=mesh,
        in_specs=(block, block, block, gain, P(), P())
        + (gain, rows, rows, rows, rows)
        + (gain, rows, rows, rows, rows)
        + (gain, rows, rows, rows),
        out_specs=(block, block, block, P())
        + (gain, rows, rows, rows, rows)
        + (gain, rows, rows, rows, rows)
        + (gain, rows, rows, rows),
        check_vma=False,
    )
```

```python
import functools

import jax
import jax.numpy as jnp
from jax import lax
from jax.experimental import pallas as pl
from jax.experimental.pallas import tpu as pltpu
from jax.sharding import PartitionSpec as P

DH = 64
NB = 32
PAIR = 2 * DH
SUB = 128
NEG = -1e30
F32 = jnp.float32
BF16 = jnp.bfloat16
AXES = ("dp", "fsdp")


def dot(a, b, ca=1, cb=0):
    return lax.dot_general(a, b, (((ca,), (cb,)), ((), ())), preferred_element_type=F32)


def exact_dot(a, b, ca=1, cb=0):
    return lax.dot_general(
        a,
        b,
        (((ca,), (cb,)), ((), ())),
        preferred_element_type=F32,
        precision=lax.Precision.HIGHEST,
    )


def rms(value):
    return lax.rsqrt(jnp.mean(value * value, axis=-1, keepdims=True) + 1e-06)


MESH = pl.DeviceIdType.MESH
EVERY = slice(None)


class Place:
    def __init__(self, sizes):
        self.sizes = grid_of(sizes)
        across, inner = lax.axis_index("dp"), lax.axis_index("fsdp")
        deep, high, wide, cores = self.sizes
        self.at = {
            "z": lax.div(across, high),
            "y": lax.rem(across, high),
            "x": lax.div(inner, cores),
            "c": lax.rem(inner, cores),
        }

    def device(self, **moved):
        at = {**self.at, **moved}
        deep, high, wide, cores = self.sizes
        return (at["z"] * high + at["y"], at["x"] * cores + at["c"])

    def size(self, axis):
        return self.sizes["zyxc".index(axis)]

    def others(self, axis):
        size = self.size(axis)
        return [lax.rem(self.at[axis] + step, size) for step in range(1, size)]

    def meet(self):
        barrier = pltpu.get_barrier_semaphore()
        peers = [self.device(**{axis: other}) for axis in "zyxc" for other in self.others(axis)]
        for peer in peers:
            pl.semaphore_signal(barrier, inc=1, device_id=peer, device_id_type=MESH)
        pl.semaphore_wait(barrier, len(peers))


def grid_of(sizes):
    wide = sizes["fsdp"] // 2
    return (sizes["dp"] // wide, wide, wide, 2)


class Gather:
    PHASES = 4

    def __init__(self, place, pieces, shards, outs, local_sem, send_sem, recv_sem):
        self.place, self.pieces, self.shards, self.outs = place, pieces, shards, outs
        self.local_sem, self.send_sem, self.recv_sem = local_sem, send_sem, recv_sem

    @staticmethod
    def copies(sizes, pieces):
        return len(pieces) * sum(size - 1 for size in grid_of(sizes))

    def view(self, piece, *index):
        array, first, rows, order = piece
        start = self.place.at["c"] * self.shards[array].shape[0] + first
        return self.outs[array].at[(*index, pl.ds(pl.multiple_of(start, 8), rows), EVERY)]

    def phase(self, number, phase):
        piece = self.pieces[number]
        place = self.place
        at = place.at
        deep, high, wide, cores = place.sizes
        array, first, rows, order = piece
        base = number * sum(size - 1 for size in place.sizes)
        if phase == 0:
            axis, skip = "z", 0
            source = self.shards[array].at[pl.ds(first, rows), :]
            target = self.view(piece, at["z"], at["y"], at["x"])
        elif phase == 3:
            axis, skip = "c", deep + high + wide - 3
            source = target = self.view(piece, EVERY, EVERY, EVERY)
        else:
            axis = order[phase - 1]
            skip = deep - 1 + (phase - 1) * (high - 1)
            if phase == 1:
                source = self.view(piece, EVERY, at["y"], at["x"])
            elif axis == "y":
                source = self.view(piece, EVERY, at["y"], EVERY)
            else:
                source = self.view(piece, EVERY, EVERY, at["x"])
            target = source
        copies = []
        for step, other in enumerate(place.others(axis)):
            slot = base + skip + step
            copies.append(
                pltpu.make_async_remote_copy(
                    source,
                    target,
                    self.send_sem.at[slot],
                    self.recv_sem.at[slot],
                    device_id=place.device(**{axis: other}),
                    device_id_type=MESH,
                )
            )
        if phase == 0:
            copies.append(pltpu.make_async_copy(source, target, self.local_sem.at[number]))
        return copies

    def advance(self, numbers, phase):
        for number in numbers:
            if phase > 0:
                for copy in self.phase(number, phase - 1):
                    copy.wait()
            if phase < self.PHASES:
                for copy in self.phase(number, phase):
                    copy.start()


class Scatter:
    PHASES = 4

    def __init__(self, place, pieces, sources, kept, outs, buffers, load_sem, send_sem, recv_sem):
        self.place, self.pieces, self.sources, self.kept, self.outs = place, pieces, sources, kept, outs
        self.buffers, self.load_sem, self.send_sem, self.recv_sem = buffers, load_sem, send_sem, recv_sem

    @staticmethod
    def copies(sizes, pieces):
        return len(pieces) * sum(size - 1 for size in grid_of(sizes))

    @staticmethod
    def scratch(sizes, pieces, shapes, kept):
        deep, high, wide, cores = grid_of(sizes)
        buffers = []
        for source, first, columns, order in pieces:
            rows, dtype = shapes[source]
            near, far = (wide, high) if order == "xy" else (high, wide)
            block = (rows, columns)
            shapes_here = [(deep, high, wide) + block, (near - 1, deep, far) + block, (far - 1, deep) + block, (deep,) + block]
            if not kept[source]:
                shapes_here.append((deep, high, wide) + block)
            buffers += [pltpu.VMEM(shape, dtype) for shape in shapes_here]
        return buffers

    def buffer(self, number, which):
        place = sum(4 if self.kept[piece[0]] else 5 for piece in self.pieces[:number])
        return self.buffers[place + which]

    def half(self, number, core):
        source, first, columns, order = self.pieces[number]
        return self.sources[source].at[:, :, :, core, :, pl.ds(first, columns)]

    def load(self, number):
        return pltpu.make_async_copy(self.half(number, self.place.at["c"]), self.buffer(number, 4), self.load_sem.at[number])

    def phase(self, number, phase):
        place = self.place
        at = place.at
        deep, high, wide, cores = place.sizes
        order = self.pieces[number][3]
        base = number * sum(size - 1 for size in place.sizes)
        axis = ("c" + order + "z")[phase]
        skip = sum(place.size(before) - 1 for before in ("c" + order + "z")[:phase])
        sums = self.buffer(number, 0)
        copies = []
        for step, other in enumerate(place.others(axis)):
            if phase == 0:
                source, target = self.half(number, other), sums
            elif phase == 3:
                source, target = sums.at[other, at["y"], at["x"]], self.buffer(number, 3).at[at["z"]]
            else:
                target = self.buffer(number, phase).at[step]
                y, x = (other, EVERY) if axis == "y" else (EVERY, other)
                if phase == 2:
                    y, x = (other, at["x"]) if axis == "y" else (at["y"], other)
                source = sums.at[:, y, x]
            slot = base + skip + step
            copies.append(
                pltpu.make_async_remote_copy(
                    source,
                    target,
                    self.send_sem.at[slot],
                    self.recv_sem.at[slot],
                    device_id=place.device(**{axis: other}),
                    device_id_type=MESH,
                )
            )
        return copies

    def absorb(self, number, phase):
        source, first, columns, order = self.pieces[number]
        at = self.place.at
        deep = self.place.sizes[0]
        sums = self.buffer(number, 0)
        if phase == 3:
            slots = self.buffer(number, 3)
            slots[at["z"]] = sums[at["z"], at["y"], at["x"]]
            total = slots[0].astype(F32)
            for slot in range(1, deep):
                total += slots[slot].astype(F32)
            self.outs[source][:, first : first + columns] = total
            return

        @pl.loop(0, deep)
        def _(z):
            if phase == 0:
                own = self.sources[source].at[z, :, :, at["c"], :, pl.ds(first, columns)] if self.kept[source] else self.buffer(number, 4).at[z]
                view, parts = sums.at[z], [own[...]]
            else:
                came = self.buffer(number, phase)
                parts = [came[step, z] for step in range(came.shape[0])]
                if phase == 1:
                    view = sums.at[z, :, at["x"]] if order[0] == "x" else sums.at[z, at["y"]]
                else:
                    view = sums.at[z, at["y"], at["x"]]
            total = view[...].astype(F32)
            for part in parts:
                total += part.astype(F32)
            view[...] = total.astype(view.dtype)

    def advance(self, numbers, phase):
        for number in numbers:
            if phase > 0:
                for copy in self.phase(number, phase - 1):
                    copy.wait()
                if phase == 1 and not self.kept[self.pieces[number][0]]:
                    self.load(number).wait()
                self.absorb(number, phase - 1)
            elif not self.kept[self.pieces[number][0]]:
                self.load(number).start()
            if phase < self.PHASES:
                for copy in self.phase(number, phase):
                    copy.start()


class Band:
    def __init__(self, length, reach):
        self.reach = reach
        self.causal = length + reach
        self.two_way = 2 * reach
        self.width = self.causal + self.two_way
        self.query_zero = length - SUB
        self.query_zero_two = reach - SUB
        self.key_zero = reach - SUB

    def distances(self, rows):
        causal = lax.broadcasted_iota(jnp.int32, (1, self.causal), 1)
        two_way = lax.broadcasted_iota(jnp.int32, (1, self.two_way), 1)
        if rows == "queries":
            causal, two_way = self.query_zero - causal, self.query_zero_two - two_way
            return (
                jnp.where(causal <= -self.reach, causal + self.causal, causal),
                jnp.where(two_way <= -self.reach, two_way + self.two_way, two_way),
            )
        causal, two_way = causal - self.key_zero, two_way - self.key_zero
        return (
            jnp.where(causal >= self.causal - self.reach, causal - self.causal, causal),
            jnp.where(two_way >= self.reach, two_way - self.two_way, two_way),
        )


def one_hot(map_ref, band, rows):
    bucket = lax.broadcasted_iota(jnp.int32, (NB, 1), 0)

    def edges(row, number):
        entries = map_ref[row : row + 1, :]
        below = jnp.sum((entries < number).astype(jnp.int32), axis=1, keepdims=True)
        return below, below + jnp.sum((entries == number).astype(jnp.int32), axis=1, keepdims=True)

    causal, two_way = band.distances(rows)
    low, high = edges(0, bucket)
    one = (causal >= low) & (causal < high)
    ahead = bucket >= NB // 2
    low, high = edges(1, jnp.where(ahead, bucket - NB // 2, bucket))
    apart = jnp.abs(two_way)
    two = (apart >= low) & (apart < high) & ((two_way < 0) == ahead)
    return jnp.concatenate([jnp.where(one, 1.0, 0.0), jnp.where(two, 1.0, 0.0)], axis=1), causal


def spread(row, width):
    return pltpu.roll(jnp.broadcast_to(row, (SUB, width)), 0, 1, stride=1, stride_axis=0)


def fold(band):
    width = band.shape[1]
    half = SUB // 2
    while half >= 8:
        band = band[:half] + pltpu.roll(band[half:], width - half, 1)
        half //= 2
    row = lax.broadcasted_iota(jnp.int32, band.shape, 0)
    for bit in (4, 2, 1):
        band = jnp.where((row & bit) != 0, pltpu.roll(band, width - bit, 1), band)
    return jnp.sum(band, axis=0, keepdims=True)


def fill_bands(head, bias_ref, band, causal_ref, two_ref):
    row = bias_ref[pl.ds(head, 1), :]
    causal_ref[...] = spread(row[:, : band.causal], band.causal)
    two_ref[...] = spread(row[:, band.causal :], band.two_way)


def bias_rows(table_ref, map_ref, band, rows):
    hot, causal = one_hot(map_ref, band, rows)
    bias = dot(table_ref[...], hot.astype(BF16), 0, 0)
    return jnp.concatenate([jnp.where(causal < 0, NEG, bias[:, : band.causal]), bias[:, band.causal :]], axis=1)


def head_cols(head):
    group = head // 2
    return pl.ds(pl.multiple_of(group * PAIR, PAIR), PAIR), head % 2


def pick_lanes(half):
    return lax.broadcasted_iota(jnp.int32, (1, PAIR), 1) // DH == half


def soft_rows(scores):
    high = jnp.max(scores, axis=-1, keepdims=True)
    weights = jnp.exp(scores - high)
    total = jnp.sum(weights, axis=-1, keepdims=True)
    return weights.astype(BF16), total, high + jnp.log(total)


def store_head(mixed_ref, lse_ref, rows, cols, head, half, out, total, lse):
    pick = pick_lanes(half)
    mixed_ref[rows, cols] = jnp.where(pick, (out / total).astype(BF16), mixed_ref[rows, cols])
    lane = lax.broadcasted_iota(jnp.int32, (1, lse_ref.shape[1]), 1)
    lse_ref[rows, :] = jnp.where(lane == head, lse, lse_ref[rows, :])


def self_forward_head(head, limit, q_ref, k_ref, v_ref, causal_ref, two_ref, band, mixed_ref, lse_ref):
    length = q_ref.shape[0]
    cols, half = head_cols(head)
    pick = pick_lanes(half)
    block = 256
    for start in range(0, length, block):
        keys = max(start + block, band.reach)
        rows = pl.ds(start, block)
        query = jnp.where(pick, q_ref[rows, cols], 0)
        scores = dot(query, k_ref[pl.ds(0, keys), cols], 1, 1)
        parts = []
        for first in range(start, start + block, SUB):
            at = band.query_zero - first
            bias = causal_ref[:, at : at + keys]
            if start < band.reach:
                at = band.query_zero_two - first
                two = two_ref[:, at : at + keys]
                inside = (first + lax.broadcasted_iota(jnp.int32, (SUB, keys), 0) < limit) & (
                    lax.broadcasted_iota(jnp.int32, (SUB, keys), 1) < limit
                )
                bias = jnp.where(inside, two, bias)
            parts.append(bias)
        weights, total, lse = soft_rows(scores + jnp.concatenate(parts, axis=0))
        out = dot(weights, v_ref[pl.ds(0, keys), cols])
        store_head(mixed_ref, lse_ref, rows, cols, head, half, out, total, lse)


def cross_forward_head(head, q_ref, k_ref, v_ref, mixed_ref, lse_ref):
    length = q_ref.shape[0]
    cols, half = head_cols(head)
    pick = pick_lanes(half)
    block = 256
    for start in range(0, length, block):
        rows = pl.ds(start, block)
        query = jnp.where(pick, q_ref[rows, cols], 0)
        weights, total, lse = soft_rows(dot(query, k_ref[:, cols], 1, 1))
        out = dot(weights, v_ref[:, cols])
        store_head(mixed_ref, lse_ref, rows, cols, head, half, out, total, lse)


def row_blocks(count, block, step):
    @pl.loop(0, count // block)
    def _(index):
        step(pl.ds(pl.multiple_of(index * block, block), block))


def gain_rows(gathered, width):
    devices = gathered.shape[0]
    share = width // devices
    lane = lax.broadcasted_iota(jnp.int32, (SUB, width), 1)
    select = jnp.where(lax.rem(lane, share) == lax.broadcasted_iota(jnp.int32, (SUB, width), 0), 1.0, 0.0)
    first = share * lax.broadcasted_iota(jnp.int32, (devices, width), 0)
    lane = lax.broadcasted_iota(jnp.int32, (devices, width), 1)
    own = (lane >= first) & (lane < first + share)
    rows = []
    for number in range(8):
        spread_out = exact_dot(gathered[:, number, :], select)
        rows.append(jnp.sum(jnp.where(own, spread_out, 0.0), axis=0, keepdims=True))
    return jnp.concatenate(rows, axis=0)


ATTENTION = 8
SHARDS = 12


def gather_pieces(rows, down_rows):
    head, tail = rows // 3 // 8 * 8, rows - rows // 3 // 8 * 8
    first = [(0, 0, rows, "xy"), (1, 0, rows, "yx"), (2, 0, head, "xy"), (2, head, tail, "yx"), (11, 0, 8, "xy")]
    rest = [(3, 0, rows, "xy"), (4, 0, rows, "yx"), (5, 0, rows, "xy"), (6, 0, rows, "yx")]
    rest += [(7, 0, tail, "xy"), (7, tail, head, "yx")]
    feed = [(8, 0, rows, "xy"), (9, 0, rows, "yx")]
    feed += [(10, 0, down_rows // 2, "xy"), (10, down_rows // 2, down_rows // 2, "yx")]
    pieces = first + rest + feed
    numbers = list(range(len(pieces)))
    groups = numbers[: len(first)], numbers[len(first) : len(first) + len(rest)], numbers[len(first) + len(rest) :]
    return pieces, groups


def forward_kernel(
    limit_ref, tokens_ref, memory_ref, table_ref, map_ref, gain1_ref, gain2_ref, gain3_ref, *refs, band, heads, plan,
):
    count = SHARDS - 1 if plan else ATTENTION
    shards, refs = refs[:count], refs[count:]
    if plan:
        gathered, refs = refs[:SHARDS], refs[SHARDS:]
    else:
        gathered = shards
    (
        gains_ref, q1_ref, k1_ref, v1_ref, mixed1_ref, lse1_ref, first_ref,
        q2_ref, k2_ref, v2_ref, mixed2_ref, lse2_ref, second_ref,
        bias_ref, causal_ref, two_ref, weights_ref, share_ref, tile_ref, load_sem, *gather_sems,
    ) = refs
    length, width = tokens_ref.shape
    if plan:
        sizes, pieces, (soon, later, feed) = plan
        place = Place(sizes)
        gather = Gather(place, pieces, (*shards, share_ref), gathered, *gather_sems)

    def advance(*steps):
        if plan:
            for numbers, phase in steps:
                gather.advance({"soon": soon, "later": later, "feed": feed}[numbers], phase)

    def load(number):
        return pltpu.make_async_copy(gathered[number].reshape(width, width), weights_ref.at[number], load_sem.at[number])

    def load_tile():
        return pltpu.make_async_copy(gathered[SHARDS - 1].reshape(tile_ref.shape), tile_ref, load_sem.at[ATTENTION])

    gain_refs = (gain1_ref, gain2_ref, gain3_ref)
    if plan:
        share_ref[...] = jnp.zeros_like(share_ref)
        for number, gain_ref in enumerate(gain_refs):
            share_ref[number : number + 1, : gain_ref.shape[1]] = gain_ref[...].astype(F32)
        place.meet()
    advance(("soon", 0))
    bias_ref[...] = bias_rows(table_ref, map_ref, band, "queries")
    lse1_ref[...] = jnp.zeros_like(lse1_ref)
    lse2_ref[...] = jnp.zeros_like(lse2_ref)
    mixed1_ref[...] = jnp.zeros_like(mixed1_ref)
    mixed2_ref[...] = jnp.zeros_like(mixed2_ref)
    advance(("soon", 1), ("later", 0), ("feed", 0), ("soon", 2), ("soon", 3), ("later", 1), ("soon", 4))
    for number in range(3):
        load(number).start()
    if plan:
        load_tile().start()
        load_tile().wait()
        gains_ref[...] = gain_rows(tile_ref[...], width)
    else:
        gains_ref[...] = jnp.zeros_like(gains_ref)
        for number, gain_ref in enumerate(gain_refs):
            gains_ref[number : number + 1, :] = gain_ref[...].astype(F32)
    for number in range(3):
        load(number).wait()

    def project_self(rows):
        value = tokens_ref[rows, :].astype(F32)
        normed = (value * rms(value) * gains_ref[0:1, :]).astype(BF16)
        q1_ref[rows, :] = dot(normed, weights_ref[0]).astype(BF16)
        k1_ref[rows, :] = dot(normed, weights_ref[1]).astype(BF16)
        v1_ref[rows, :] = dot(normed, weights_ref[2]).astype(BF16)

    row_blocks(length, 256, project_self)
    advance(("later", 2))

    @pl.loop(0, heads)
    def _(head):
        fill_bands(head, bias_ref, band, causal_ref, two_ref)
        self_forward_head(head, limit_ref[0], q1_ref, k1_ref, v1_ref, causal_ref, two_ref, band, mixed1_ref, lse1_ref)

        @pl.when(head == heads // 4)
        def _():
            advance(("feed", 1), ("later", 3))

        @pl.when(head == heads // 2)
        def _():
            advance(("later", 4))
            for number in range(3, ATTENTION):
                load(number).start()
            advance(("feed", 2))

    for number in range(3, ATTENTION):
        load(number).wait()

    def project_memory(rows):
        k2_ref[rows, :] = dot(memory_ref[rows, :], weights_ref[5]).astype(BF16)
        v2_ref[rows, :] = dot(memory_ref[rows, :], weights_ref[6]).astype(BF16)

    row_blocks(memory_ref.shape[0], 256, project_memory)

    def project_cross(rows):
        value = tokens_ref[rows, :].astype(F32) + dot(mixed1_ref[rows, :], weights_ref[3])
        first_ref[rows, :] = value
        normed = (value * rms(value) * gains_ref[1:2, :]).astype(BF16)
        q2_ref[rows, :] = dot(normed, weights_ref[4]).astype(BF16)

    row_blocks(length, 256, project_cross)
    advance(("feed", 3))

    @pl.loop(0, heads)
    def _(head):
        cross_forward_head(head, q2_ref, k2_ref, v2_ref, mixed2_ref, lse2_ref)

    def project_second(rows):
        second_ref[rows, :] = first_ref[rows, :] + dot(mixed2_ref[rows, :], weights_ref[7])

    row_blocks(length, 256, project_second)
    advance(("feed", 4))


def norm_back_rows(value, gain, grad):
    scale = rms(value)
    unit = value * scale
    scaled = grad * gain
    back = scale * (scaled - unit * jnp.mean(scaled * unit, axis=-1, keepdims=True))
    return back, jnp.sum(grad * unit, axis=0, keepdims=True)


GELU_A = 0.7978845608028654
GELU_B = 0.044715


def feed_kernel(
    second_ref, gout_ref, gains_ref, gate_ref, up_ref, down_ref,
    output_ref, gsecond_ref, ggain_ref, dgate_ref, dup_ref, ddown_ref,
    normed_ref, flipped_ref, out_ref, back_ref, hidden_ref, ggate_ref, gup_ref,
):
    step = pl.program_id(0)
    length = second_ref.shape[0]
    block = 256

    @pl.when(step == 0)
    def _():
        def prepare(rows):
            value = second_ref[rows, :]
            normed = (value * rms(value) * gains_ref[2:3, :]).astype(BF16)
            normed_ref[rows, :] = normed
            flipped_ref[:, rows] = normed.T
            out_ref[rows, :] = value
            back_ref[rows, :] = jnp.zeros_like(value)

        row_blocks(length, block, prepare)

    def rows_step(rows):
        normed = normed_ref[rows, :]
        gate = dot(normed, gate_ref[...])
        upward = dot(normed, up_ref[...])
        square = gate * gate
        bend = jnp.tanh(GELU_A * gate * (1.0 + GELU_B * square))
        half = 0.5 * (1.0 + bend)
        active = gate * half
        hidden = (active * upward).astype(BF16)
        hidden_ref[rows, :] = hidden
        out_ref[rows, :] += dot(hidden, down_ref[...])
        ghidden = dot(gout_ref[rows, :], down_ref[...], 1, 1)
        slope = half + 0.5 * gate * (1.0 - bend * bend) * (GELU_A * (1.0 + 3.0 * GELU_B * square))
        ggate = (ghidden * upward * slope).astype(BF16)
        gup = (ghidden * active).astype(BF16)
        ggate_ref[rows, :] = ggate
        gup_ref[rows, :] = gup
        back_ref[rows, :] += dot(ggate, gate_ref[...], 1, 1) + dot(gup, up_ref[...], 1, 1)

    row_blocks(length, block, rows_step)
    ddown_ref[...] = dot(hidden_ref[...].T, gout_ref[...]).astype(BF16)
    dgate_ref[...] = dot(flipped_ref[...], ggate_ref[...]).astype(BF16)
    dup_ref[...] = dot(flipped_ref[...], gup_ref[...]).astype(BF16)

    @pl.when(step == pl.num_programs(0) - 1)
    def _():
        ggain_ref[...] = jnp.zeros_like(ggain_ref)

        def finish(rows):
            output_ref[rows, :] = out_ref[rows, :].astype(BF16)
            back, ggain = norm_back_rows(second_ref[rows, :], gains_ref[2:3, :], back_ref[rows, :])
            gsecond_ref[rows, :] = back + gout_ref[rows, :].astype(F32)
            ggain_ref[0:1, :] += ggain

        row_blocks(length, block, finish)


def backward_head_prepare(group_cols, gm_ref, mixed_ref, delta_ref):
    product = (gm_ref[:, group_cols].astype(F32) * mixed_ref[:, group_cols].astype(F32)).T
    delta_ref[0:1, :] = jnp.sum(product[:DH], axis=0, keepdims=True)
    delta_ref[1:2, :] = jnp.sum(product[DH:], axis=0, keepdims=True)


def backward_block(key_rows, cols, half, start, bias, q_ref, k_ref, v_ref, gm_ref, lse, delta, gk_ref, gv_ref, gqt_ref):
    length = q_ref.shape[0]
    pick = pick_lanes(half)
    queries = pl.ds(start, length - start)
    query = jnp.where(pick, q_ref[queries, cols], 0)
    grad = jnp.where(pick, gm_ref[queries, cols], 0)
    keys = k_ref[key_rows, cols]
    scores = dot(keys, query, 1, 1)
    if bias is not None:
        scores = scores + bias
    probs = jnp.exp(scores - lse[:, start:])
    gv = dot(probs.astype(BF16), grad)
    gprobs = dot(v_ref[key_rows, cols], grad, 1, 1)
    gscores = probs * (gprobs - delta[:, start:])
    low = gscores.astype(BF16)
    gk = dot(low, query)
    gk_ref[key_rows, cols] = jnp.where(pick, gk.astype(BF16), gk_ref[key_rows, cols])
    gv_ref[key_rows, cols] = jnp.where(pick, gv.astype(BF16), gv_ref[key_rows, cols])
    gqt_ref[:, queries] += dot(jnp.where(pick, keys, 0).T, low)
    return gscores


def self_backward_head(
    head, limit, q_ref, k_ref, v_ref, gm_ref, mixed_ref, lse_ref, delta_ref, causal_ref, two_ref, band,
    gk_ref, gv_ref, gqt_ref, causal_sum_ref, two_sum_ref,
):
    length = q_ref.shape[0]
    cols, half = head_cols(head)
    lse = lse_ref[pl.ds(head, 1), :]
    delta = delta_ref[pl.ds(half, 1), :]
    reach = band.reach
    block = 256
    for first in range(0, length, block):
        start = 0 if first < reach else first
        count = length - start
        parts = []
        for key in range(first, first + block, SUB):
            at = band.key_zero - key + start
            bias = causal_ref[:, at : at + count]
            if first < reach:
                at = band.key_zero - key
                two = two_ref[:, at : at + reach]
                inside = (key + lax.broadcasted_iota(jnp.int32, (SUB, reach), 0) < limit) & (
                    lax.broadcasted_iota(jnp.int32, (SUB, reach), 1) < limit
                )
                bias = jnp.concatenate([jnp.where(inside, two, bias[:, :reach]), bias[:, reach:]], axis=1)
            parts.append(bias)
        gscores = backward_block(
            pl.ds(first, block), cols, half, start, jnp.concatenate(parts, axis=0),
            q_ref, k_ref, v_ref, gm_ref, lse, delta, gk_ref, gv_ref, gqt_ref,
        )
        for key in range(first, first + block, SUB):
            part = gscores[key - first : key - first + SUB]
            at = band.key_zero - key + start
            if first < reach:
                inside = (key + lax.broadcasted_iota(jnp.int32, (SUB, reach), 0) < limit) & (
                    lax.broadcasted_iota(jnp.int32, (SUB, reach), 1) < limit
                )
                head_part = part[:, :reach]
                at_two = band.key_zero - key
                two_sum_ref[:, at_two : at_two + reach] += jnp.where(inside, head_part, 0.0)
                causal_sum_ref[:, at : at + reach] += jnp.where(inside, 0.0, head_part)
                causal_sum_ref[:, at + reach : at + count] += part[:, reach:]
            else:
                causal_sum_ref[:, at : at + count] += part


def split_columns(number, columns):
    half = columns // 2
    return [(number, 0, half, "xy"), (number, half, half, "yx")]


def cross_backward_kernel(
    gsecond_ref, first_ref, memory_ref, gains_ref, q_ref, k_ref, v_ref, mixed1_ref, mixed2_ref, lse_ref,
    wo_ref, cq_ref, ck_ref, cv_ref, co_ref, *refs, heads, plan,
):
    count = 2 if plan else 0
    sources, refs = refs[:count], refs[count:]
    gmem_ref, gfirst_ref, gm1_ref, ggain_ref, dwo_ref, dcq_ref, dck_ref, dcv_ref, dco_ref, *refs = refs
    outs, refs = refs[:count], refs[count:]
    gm_ref, branch_ref, flipped_ref, lse_rows_ref, delta_ref, gq_ref, gk_ref, gv_ref, gqt_ref, *refs = refs
    if plan:
        sizes, pieces = plan
        scatter = Scatter(Place(sizes), pieces, sources, [False] * count, outs, refs[:-3], *refs[-3:])
        everything = range(len(pieces))
        scatter.place.meet()
        scatter.advance(everything, 0)
    length, width = first_ref.shape
    source = memory_ref.shape[0]
    block = 256

    def prepare(rows):
        branch = gsecond_ref[rows, :].astype(BF16)
        branch_ref[rows, :] = branch
        gm_ref[rows, :] = dot(branch, co_ref[...], 1, 1).astype(BF16)
        flipped_ref[:, rows] = mixed2_ref[rows, :].T

    row_blocks(length, block, prepare)

    def out_grad(rows):
        dco_ref[rows, :] = dot(flipped_ref[rows, :], branch_ref[...]).astype(BF16)

    row_blocks(width, block, out_grad)
    lse_rows_ref[...] = lse_ref[...].T
    gk_ref[...] = jnp.zeros_like(gk_ref)
    gv_ref[...] = jnp.zeros_like(gv_ref)
    groups = heads // 2

    @pl.loop(0, groups)
    def _(group):
        if plan:
            for when, phase in ((1, 1), (groups - 2, 2), (groups - 1, 3)):

                @pl.when(group == when)
                def _(phase=phase):
                    scatter.advance(everything, phase)

        cols = pl.ds(pl.multiple_of(group * PAIR, PAIR), PAIR)
        backward_head_prepare(cols, gm_ref, mixed2_ref, delta_ref)
        gqt_ref[...] = jnp.zeros_like(gqt_ref)

        @pl.loop(0, 2)
        def _(half):
            head = group * 2 + half
            for first in range(0, source, block):
                backward_block(
                    pl.ds(first, block), cols, half, 0, None, q_ref, k_ref, v_ref, gm_ref,
                    lse_rows_ref[pl.ds(head, 1), :], delta_ref[pl.ds(half, 1), :], gk_ref, gv_ref, gqt_ref,
                )

        gq_ref[:, cols] = gqt_ref[...].T.astype(BF16)

    def memory_grad(rows):
        gmem_ref[rows, :] = dot(gk_ref[rows, :], ck_ref[...], 1, 1) + dot(gv_ref[rows, :], cv_ref[...], 1, 1)
        flipped_ref[:, rows] = memory_ref[rows, :].T

    row_blocks(source, block, memory_grad)

    def memory_weights(rows):
        flipped = flipped_ref[rows, :source]
        dck_ref[rows, :] = dot(flipped, gk_ref[...]).astype(BF16)
        dcv_ref[rows, :] = dot(flipped, gv_ref[...]).astype(BF16)

    row_blocks(width, block, memory_weights)
    ggain_ref[...] = jnp.zeros_like(ggain_ref)

    def first_grad(rows):
        value = first_ref[rows, :]
        flipped_ref[:, rows] = (value * rms(value) * gains_ref[1:2, :]).astype(BF16).T
        back, ggain = norm_back_rows(value, gains_ref[1:2, :], dot(gq_ref[rows, :], cq_ref[...], 1, 1))
        ggain_ref[0:1, :] += ggain
        gfirst = back + gsecond_ref[rows, :]
        gfirst_ref[rows, :] = gfirst
        branch = gfirst.astype(BF16)
        branch_ref[rows, :] = branch
        gm1_ref[rows, :] = dot(branch, wo_ref[...], 1, 1).astype(BF16)

    row_blocks(length, block, first_grad)

    def query_weights(rows):
        dcq_ref[rows, :] = dot(flipped_ref[rows, :], gq_ref[...]).astype(BF16)

    row_blocks(width, block, query_weights)

    def flip_mixed(rows):
        flipped_ref[:, rows] = mixed1_ref[rows, :].T

    row_blocks(length, block, flip_mixed)

    def out_weights(rows):
        dwo_ref[rows, :] = dot(flipped_ref[rows, :], branch_ref[...]).astype(BF16)

    row_blocks(width, block, out_weights)
    if plan:
        scatter.advance(everything, 4)


def store_shares(ref, cols, value, start):
    if len(ref.shape) == 2:
        ref[pl.ds(start, value.shape[0]), cols] = value.astype(BF16)
    else:
        deep, high, wide, cores, rows, columns = ref.shape
        chunk = high * wide * cores * rows
        ref[start // chunk, :, :, :, :, cols] = value.reshape(high, wide, cores, rows, value.shape[1]).astype(BF16)


TILE = 16


def fill_tiles(tiles_ref, gtable, ggains):
    deep, high, wide, cores, rows, lanes = tiles_ref.shape
    devices = deep * high * wide * cores
    width = ggains[0].shape[1]
    share = width // devices
    lane = lax.broadcasted_iota(jnp.int32, (SUB, width), 1)
    select = jnp.where(lax.rem(lane, share) == lax.broadcasted_iota(jnp.int32, (SUB, width), 0), 1.0, 0.0)
    first = share * lax.broadcasted_iota(jnp.int32, (devices, width), 0)
    lane = lax.broadcasted_iota(jnp.int32, (devices, width), 1)
    own = (lane >= first) & (lane < first + share)
    parts = [exact_dot(jnp.where(own, ggain, 0.0), select, 1, 1) for ggain in ggains]
    tiles_ref[...] = jnp.zeros_like(tiles_ref)
    heads, buckets = gtable.shape
    for device in range(devices):
        at = tuple(int(part) for part in (device // (high * wide * cores), device // (wide * cores) % high, device // cores % wide, device % cores))
        tiles_ref[(*at, slice(0, heads), slice(0, buckets))] = gtable
        for number, part in enumerate(parts):
            row = TILE - len(parts) + number
            tiles_ref[(*at, slice(row, row + 1), EVERY)] = part[device : device + 1]


REST = 6


def self_pieces(down_columns, columns):
    first = split_columns(0, down_columns) + [(1, 0, columns, "xy"), (2, 0, columns, "yx")]
    rest = [(3, 0, columns, "xy"), (4, 0, columns, "yx")] + split_columns(5, columns)
    half = columns // 2
    early = [(REST, 0, half, "xy"), (REST + 1, 0, half, "yx"), (REST + 2, 0, half, "xy")]
    late = [(REST, half, half, "yx"), (REST + 1, half, half, "xy"), (REST + 2, half, half, "yx"), (REST + 3, 0, SUB, "xy")]
    pieces, groups = [], []
    for group in (first, rest, early, late):
        groups.append(range(len(pieces), len(pieces) + len(group)))
        pieces += group
    return pieces, groups


def self_backward_kernel(
    limit_ref, tokens_ref, gains_ref, table_ref, map_ref, q_ref, k_ref, v_ref, mixed_ref, lse_ref, gm_ref, gfirst_ref,
    ggain2_ref, ggain3_ref, wq_ref, wk_ref, wv_ref, *refs, band, heads, plan,
):
    count = REST if plan else 0
    sources, refs = refs[:count], refs[count:]
    gtokens_ref, refs = refs[0], refs[1:]
    if plan:
        outs, refs = refs[: REST + 3], refs[REST + 3 :]
        gtable_ref, *ggain_refs = refs[:4]
        refs = refs[4:]
    else:
        ggain_ref, gtable_ref, dwq_ref, dwk_ref, dwv_ref, *refs = refs
    (
        bias_ref, causal_ref, two_ref, flipped_ref, lse_rows_ref, delta_ref, gq_ref, gk_ref, gv_ref, gqt_ref,
        causal_sum_ref, two_sum_ref, sums_ref, *refs,
    ) = refs
    length, width = tokens_ref.shape
    block = 256
    groups = heads // 2
    if plan:
        sizes, pieces, (first, rest, early, late) = plan
        dwq_ref, dwk_ref, dwv_ref, tiles_ref, tile_ref, ggain_ref, *refs = refs
        scatter = Scatter(
            Place(sizes), pieces, (*sources, dwq_ref, dwk_ref, dwv_ref, tiles_ref), [False] * REST + [True] * 4,
            (*outs, tile_ref), refs[:-3], *refs[-3:],
        )
        scatter.place.meet()
        scatter.advance(first, 0)
        scatter.advance(rest, 0)
    bias_ref[...] = bias_rows(table_ref, map_ref, band, "keys")
    lse_rows_ref[...] = lse_ref[...].T
    gk_ref[...] = jnp.zeros_like(gk_ref)
    gv_ref[...] = jnp.zeros_like(gv_ref)
    sums_ref[...] = jnp.zeros_like(sums_ref)

    def flip_normed(rows):
        value = tokens_ref[rows, :].astype(F32)
        flipped_ref[:, rows] = (value * rms(value) * gains_ref[0:1, :]).astype(BF16).T

    row_blocks(length, block, flip_normed)

    def group_step(group):
        cols = pl.ds(pl.multiple_of(group * PAIR, PAIR), PAIR)
        backward_head_prepare(cols, gm_ref, mixed_ref, delta_ref)
        gqt_ref[...] = jnp.zeros_like(gqt_ref)

        @pl.loop(0, 2)
        def _(half):
            head = group * 2 + half
            fill_bands(head, bias_ref, band, causal_ref, two_ref)
            causal_sum_ref[...] = jnp.zeros_like(causal_sum_ref)
            two_sum_ref[...] = jnp.zeros_like(two_sum_ref)
            self_backward_head(
                head, limit_ref[0], q_ref, k_ref, v_ref, gm_ref, mixed_ref, lse_rows_ref, delta_ref,
                causal_ref, two_ref, band, gk_ref, gv_ref, gqt_ref, causal_sum_ref, two_sum_ref,
            )
            sums_ref[pl.ds(head, 1), : band.causal] = fold(causal_sum_ref[...])
            sums_ref[pl.ds(head, 1), band.causal :] = fold(two_sum_ref[...])

        gq_ref[:, cols] = gqt_ref[...].T.astype(BF16)

    rows_each = width // (sizes["dp"] // (sizes["fsdp"] // 2)) if plan else block

    def weights(cols):
        @pl.loop(0, width // rows_each)
        def _(index):
            start = pl.multiple_of(index * rows_each, 64)
            flipped = flipped_ref[pl.ds(start, rows_each), :]
            for target, grad in ((dwq_ref, gq_ref), (dwk_ref, gk_ref), (dwv_ref, gv_ref)):
                store_shares(target, cols, dot(flipped, grad[:, cols]), start)

    half_groups = groups // 2
    low, high = pl.ds(0, width // 2), pl.ds(width // 2, width // 2)

    @pl.loop(0, groups)
    def _(group):
        if plan:

            @pl.when(group == 1)
            def _():
                scatter.advance(first, 1)

            @pl.when(group == half_groups)
            def _():
                weights(low)
                scatter.advance(early, 0)
                scatter.advance(first, 2)
                scatter.advance(rest, 1)

            @pl.when(group == half_groups + 1)
            def _():
                scatter.advance(first, 3)
                scatter.advance(early, 1)

            @pl.when(group == groups - 1)
            def _():
                scatter.advance(rest, 2)
                scatter.advance(early, 2)

        group_step(group)

    if plan:
        scatter.advance(first, 4)
        scatter.advance(rest, 3)
        weights(high)
        scatter.advance(early, 3)
        scatter.advance(late[:3], 0)
    else:
        weights(low)
        weights(high)
    hot, unused = one_hot(map_ref, band, "keys")
    gtable = exact_dot(sums_ref[...], hot, 1, 1)
    ggain_ref[...] = jnp.zeros_like(ggain_ref)

    def tokens_grad(rows):
        value = tokens_ref[rows, :].astype(F32)
        grad = dot(gq_ref[rows, :], wq_ref[...], 1, 1)
        grad += dot(gk_ref[rows, :], wk_ref[...], 1, 1)
        grad += dot(gv_ref[rows, :], wv_ref[...], 1, 1)
        back, ggain = norm_back_rows(value, gains_ref[0:1, :], grad)
        ggain_ref[0:1, :] += ggain
        gtokens_ref[rows, :] = back + gfirst_ref[rows, :]

    if plan:
        scatter.advance(late[:3], 1)
        row_blocks(length, block, tokens_grad)
        fill_tiles(tiles_ref, gtable, [ggain_ref[0:1, :], ggain2_ref[0:1, :], ggain3_ref[0:1, :]])
        scatter.advance(late[3:], 0)
        scatter.advance(late[:3], 2)
        scatter.advance(late[3:], 1)
        scatter.advance(rest, 4)
        scatter.advance(late[:3], 3)
        scatter.advance(late[3:], 2)
        scatter.advance(early, 4)
        scatter.advance(late[3:], 3)
        scatter.advance(late, 4)
        tile = tile_ref[...]
        gtable_ref[...] = tile.T[:NB, :heads]
        for number, ref in enumerate(ggain_refs):
            row = TILE - len(ggain_refs) + number
            ref[...] = tile[row : row + 1, : ref.shape[1]]
    else:
        row_blocks(length, block, tokens_grad)
        gtable_ref[...] = gtable.T


def vmem(*shapes):
    return [pltpu.VMEM(shape, dtype) for shape, dtype in shapes]


def params(**kw):
    return pltpu.CompilerParams(vmem_limit_bytes=60 * 1024 * 1024, **kw)


def per_device(
    inputs, encoded, out_grad, prefix, bucket_map, bias_table,
    norm_self, self_query, self_key, self_value, self_out,
    norm_cross, cross_query, cross_key, cross_value, cross_out,
    norm_feed, feed_gate, feed_up, feed_down,
):
    seqs, length, width = inputs.shape
    source = encoded.shape[1]
    heads = bias_table.shape[1]
    ff = feed_gate.shape[1]
    band = Band(length, length // 2)
    tokens = inputs.reshape(length, width)
    memory = encoded.reshape(source, width)
    gout = out_grad.reshape(length, width)
    gains_in = [norm_self, norm_cross, norm_feed]
    projections = [self_query, self_key, self_value, self_out, cross_query, cross_key, cross_value, cross_out]
    feeds = [feed_gate, feed_up, feed_down]
    sizes = dict(dp=lax.axis_size("dp"), fsdp=lax.axis_size("fsdp"))
    devices = sizes["dp"] * sizes["fsdp"]
    own = self_query.shape[0] % 8 == 0
    if own:
        pieces, groups = gather_pieces(self_query.shape[0], feed_down.shape[0])
        plan = (sizes, pieces, groups)
        copies = Gather.copies(sizes, pieces)
        shards = projections + feeds
    else:
        plan = None
        gains_in = [lax.all_gather(gain, AXES, axis=0, tiled=True) for gain in gains_in]
        shards = [lax.all_gather(shard, AXES, axis=0, tiled=True) for shard in projections]
        gate_full, up_full, down = [lax.all_gather(shard, AXES, axis=0, tiled=True) for shard in feeds]
    gains_in = [gain.reshape(1, -1) for gain in gains_in]

    remote = pl.BlockSpec(memory_space=pl.ANY)
    scalar = pl.BlockSpec(memory_space=pltpu.SMEM)

    def full(shape):
        return pl.BlockSpec(shape, lambda *_: (0,) * len(shape))

    def like(shape, dtype):
        return jax.ShapeDtypeStruct(shape, dtype)

    act = like((length, width), BF16)
    mem = like((source, width), BF16)
    act32 = like((length, width), F32)
    lse_shape = like((length, SUB), F32)
    gain_shape = like((8, width), F32)
    outs = [gain_shape, act, act, act, act, lse_shape, act32, act, mem, mem, act, lse_shape, act32]
    gathered_shapes = []
    if own:
        chips, cores = grid_of(sizes)[:3], grid_of(sizes)[3]
        gathered_shapes = [like(chips + (cores * shard.shape[0], shard.shape[1]), shard.dtype) for shard in shards]
        gathered_shapes.append(like(chips + (cores * 8, SUB), F32))
    forward_in = (tokens, memory, bias_table, bucket_map, *gains_in)
    results = pl.pallas_call(
        functools.partial(forward_kernel, band=band, heads=heads, plan=plan),
        out_shape=gathered_shapes + outs,
        grid=(1,),
        in_specs=[scalar] + [full(a.shape) for a in forward_in] + [remote] * len(shards),
        out_specs=[remote] * len(gathered_shapes) + [full(o.shape) for o in outs],
        scratch_shapes=vmem(
            ((heads, band.width), F32), ((SUB, band.causal), F32), ((SUB, band.two_way), F32),
            ((ATTENTION, width, width), BF16), ((8, SUB), F32), ((devices, 8, SUB), F32),
        )
        + [pltpu.SemaphoreType.DMA((ATTENTION + 1,))]
        + ([pltpu.SemaphoreType.DMA((number,)) for number in (len(pieces), copies, copies)] if own else []),
        compiler_params=params(collective_id=0, has_side_effects=True) if own else params(),
        name="forward",
    )(prefix, *forward_in, *shards)
    attention = shards
    if own:
        gathered, results = results[:SHARDS], results[SHARDS:]
        attention = [part.reshape(width, width) for part in gathered[:ATTENTION]]
        gate_full, up_full = gathered[8].reshape(width, ff), gathered[9].reshape(width, ff)
        down = gathered[10].reshape(ff, width)
    gains, q1, k1, v1, mixed1, lse1, first, q2, k2, v2, mixed2, lse2, second = results

    fblock = 256
    ggain_shape = like((8, width), F32)
    feed_out = [
        act, act32, ggain_shape, like((width, ff), BF16), like((width, ff), BF16), like((ff, width), BF16)
    ]
    output, gsecond, ggain_feed, dgate, dup, ddown = pl.pallas_call(
        feed_kernel,
        out_shape=feed_out,
        grid=(ff // fblock,),
        in_specs=[full(second.shape), full(gout.shape), full(gains.shape)]
        + [
            pl.BlockSpec((width, fblock), lambda i: (0, i)),
            pl.BlockSpec((width, fblock), lambda i: (0, i)),
            pl.BlockSpec((fblock, width), lambda i: (i, 0)),
        ],
        out_specs=[full(o.shape) for o in feed_out[:3]]
        + [
            pl.BlockSpec((width, fblock), lambda i: (0, i)),
            pl.BlockSpec((width, fblock), lambda i: (0, i)),
            pl.BlockSpec((fblock, width), lambda i: (i, 0)),
        ],
        scratch_shapes=vmem(
            ((length, width), BF16), ((width, length), BF16), ((length, width), F32), ((length, width), F32),
            ((length, fblock), BF16), ((length, fblock), BF16), ((length, fblock), BF16),
        ),
        compiler_params=params(),
        name="feed",
    )(second, gout, gains, gate_full, up_full, down)

    square = like((width, width), BF16)
    cross_shapes = [like((source, width), F32), act32, act, ggain_shape] + [square] * 5
    cross_in = (gsecond, first, memory, gains, q2, k2, v2, mixed1, mixed2, lse2)
    cross_scratch = vmem(
        ((length, width), BF16), ((length, width), BF16), ((width, length), BF16), ((SUB, length), F32),
        ((8, length), F32), ((length, width), BF16), ((source, width), BF16), ((source, width), BF16),
        ((PAIR, length), F32),
    )
    grid = grid_of(sizes)

    def shares(grads):
        return [grad.reshape(grid + (grad.shape[0] // devices, grad.shape[1])) for grad in grads]

    def scatter_scratch(pieces, shapes, kept):
        count = Scatter.copies(sizes, pieces)
        return Scatter.scratch(sizes, pieces, shapes, kept) + [
            pltpu.SemaphoreType.DMA((number,)) for number in (len(pieces), count, count)
        ]

    plan, sources, gate_shapes, scratch = None, [], [], []
    if own:
        sources = shares([dgate, dup])
        pieces = [(0, 0, ff, "xy"), (1, 0, ff, "yx")]
        plan = (sizes, pieces)
        gate_shapes = [like(part.shape[-2:], F32) for part in sources]
        scratch = scatter_scratch(pieces, [(part.shape[-2], BF16) for part in sources], [False, False])
    cross_shapes += gate_shapes
    gmem, gfirst, gm1, ggain_cross, dwo, dcq, dck, dcv, dco, *feed_grads = pl.pallas_call(
        functools.partial(cross_backward_kernel, heads=heads, plan=plan),
        out_shape=cross_shapes,
        grid=(1,),
        in_specs=[full(a.shape) for a in cross_in] + [full((width, width))] * 5 + [remote] * len(sources),
        out_specs=[full(o.shape) for o in cross_shapes],
        scratch_shapes=cross_scratch + scratch,
        compiler_params=params(collective_id=1, has_side_effects=True) if own else params(),
        name="cross_backward",
    )(*cross_in, *attention[3:], *sources)

    self_in = (tokens, gains, bias_table, bucket_map, q1, k1, v1, mixed1, lse1, gm1, gfirst, ggain_cross, ggain_feed)
    self_scratch = vmem(
        ((heads, band.width), F32), ((SUB, band.causal), F32), ((SUB, band.two_way), F32), ((width, length), BF16),
        ((SUB, length), F32), ((8, length), F32), ((length, width), BF16), ((length, width), BF16),
        ((length, width), BF16), ((PAIR, length), F32), ((SUB, band.causal), F32), ((SUB, band.two_way), F32),
        ((heads, band.width), F32),
    )
    plan, sources, scratch = None, [], []
    table_shape = like((NB, heads), F32)
    if own:
        sources = shares([ddown, dco, dwo, dcq, dck, dcv])
        pieces, groups = self_pieces(width, width)
        plan = (sizes, pieces, groups)
        share = width // devices
        kept = [False] * REST + [True] * 4
        shapes = [(part.shape[-2], BF16) for part in sources] + [(share, BF16)] * 3 + [(TILE, F32)]
        self_shapes = [act32] + [like(part.shape[-2:], F32) for part in sources] + [like((share, width), F32)] * 3
        self_shapes += [table_shape] + [like((1, share), F32)] * 3
        scratch = vmem(*[(grid + (share, width), BF16)] * 3, (grid + (TILE, SUB), F32), ((TILE, SUB), F32), ((8, width), F32))
        scratch += scatter_scratch(pieces, shapes, kept)
    else:
        self_shapes = [act32, ggain_shape, table_shape] + [square] * 3
    gtokens, *grads = pl.pallas_call(
        functools.partial(self_backward_kernel, band=band, heads=heads, plan=plan),
        out_shape=self_shapes,
        grid=(1,),
        in_specs=[scalar] + [full(a.shape) for a in self_in] + [full((width, width))] * 3 + [remote] * len(sources),
        out_specs=[full(o.shape) for o in self_shapes],
        scratch_shapes=self_scratch + scratch,
        compiler_params=params(collective_id=2, has_side_effects=True) if own else params(),
        name="self_backward",
    )(prefix, *self_in, *attention[:3], *sources)

    if own:
        ddown, dco, dwo, dcq, dck, dcv, dwq, dwk, dwv, table_grad, *ggains = grads
        ggains = [ggain.reshape(-1) for ggain in ggains]
        dgate, dup = feed_grads
    else:
        ggain_self, gtable, dwq, dwk, dwv = grads
        table_grad = lax.psum(gtable, AXES)

        def scatter(parts, axis):
            return lax.psum_scatter(jnp.concatenate(parts, axis=1 - axis), AXES, scatter_dimension=axis, tiled=True)

        ggains = scatter([ggain_self[:1], ggain_cross[:1], ggain_feed[:1]], 1)
        dgate, dup = jnp.split(scatter([dgate, dup], 0).astype(F32), 2, axis=1)
        ddown = scatter([ddown], 0).astype(F32)
        squares = scatter([dwq, dwk, dwv, dwo, dcq, dck, dcv, dco], 0).astype(F32)
        dwq, dwk, dwv, dwo, dcq, dck, dcv, dco = jnp.split(squares, 8, axis=1)
    return (
        output.reshape(inputs.shape),
        gtokens.reshape(inputs.shape),
        gmem.reshape(encoded.shape),
        table_grad,
        ggains[0], dwq, dwk, dwv, dwo,
        ggains[1], dcq, dck, dcv, dco,
        ggains[2], dgate, dup, ddown,
    )


def solution(mesh):
    rows = P(AXES, None)
    gain = P(AXES)
    block = P(AXES, None, None)
    return jax.shard_map(
        per_device,
        mesh=mesh,
        in_specs=(block, block, block, gain, P(), P())
        + (gain, rows, rows, rows, rows)
        + (gain, rows, rows, rows, rows)
        + (gain, rows, rows, rows),
        out_specs=(block, block, block, P())
        + (gain, rows, rows, rows, rows)
        + (gain, rows, rows, rows, rows)
        + (gain, rows, rows, rows),
        check_vma=False,
    )
```

```python
import functools

import jax
import jax.numpy as jnp
from jax import lax
from jax.experimental import pallas as pl
from jax.experimental.pallas import tpu as pltpu
from jax.sharding import PartitionSpec as P

DH = 64
NB = 32
PAIR = 2 * DH
SUB = 128
NEG = -1e30
F32 = jnp.float32
BF16 = jnp.bfloat16
AXES = ("dp", "fsdp")


def dot(a, b, ca=1, cb=0):
    return lax.dot_general(a, b, (((ca,), (cb,)), ((), ())), preferred_element_type=F32)


def exact_dot(a, b, ca=1, cb=0):
    return lax.dot_general(
        a,
        b,
        (((ca,), (cb,)), ((), ())),
        preferred_element_type=F32,
        precision=lax.Precision.HIGHEST,
    )


def rms(value):
    return lax.rsqrt(jnp.mean(value * value, axis=-1, keepdims=True) + 1e-06)


MESH = pl.DeviceIdType.MESH
EVERY = slice(None)


class Place:
    def __init__(self, sizes):
        self.grid = sizes
        self.sizes = grid_of(sizes)
        across, inner = lax.axis_index("dp"), lax.axis_index("fsdp")
        deep, high, wide, cores = self.sizes
        self.at = {
            "z": lax.div(across, high),
            "y": lax.rem(across, high),
            "x": lax.div(inner, cores),
            "c": lax.rem(inner, cores),
        }

    def device(self, **moved):
        at = {**self.at, **moved}
        deep, high, wide, cores = self.sizes
        return (at["z"] * high + at["y"], at["x"] * cores + at["c"])

    def size(self, axis):
        return self.sizes["zyxc".index(axis)]

    def others(self, axis):
        size = self.size(axis)
        return [lax.rem(self.at[axis] + step, size) for step in range(1, size)]

    def meet(self):
        barrier = pltpu.get_barrier_semaphore()
        peers = [self.device(**{axis: other}) for axis in "zyxc" for other in self.others(axis)]
        for peer in peers:
            pl.semaphore_signal(barrier, inc=1, device_id=peer, device_id_type=MESH)
        pl.semaphore_wait(barrier, len(peers))


def grid_of(sizes):
    wide = sizes["fsdp"] // 2
    return (sizes["dp"] // wide, wide, wide, 2)


class Gather:
    PHASES = 4

    def __init__(self, place, pieces, shards, outs, local_sem, send_sem, recv_sem):
        self.place, self.pieces, self.shards, self.outs = place, pieces, shards, outs
        self.local_sem, self.send_sem, self.recv_sem = local_sem, send_sem, recv_sem

    @staticmethod
    def each(sizes):
        grid = grid_of(sizes)
        return sum(size - 1 for size in grid[:3]) + max(grid[:3])

    @staticmethod
    def copies(sizes, pieces):
        return len(pieces) * Gather.each(sizes)

    def view(self, piece, held):
        array, first, rows, order = piece
        start = self.place.at["c"] * self.shards[array].shape[0] + first
        where = [held.get(axis, EVERY) for axis in "zyx"]
        return self.outs[array].at[(*where, pl.ds(pl.multiple_of(start, 8), rows), EVERY)]

    def phase(self, number, phase, core):
        piece = self.pieces[number]
        place, at = self.place, self.place.at
        array, first, rows, order = piece
        slot = number * self.each(place.grid) + sum(place.size(axis) - 1 for axis in order[:phase])
        copies = []

        def send(source, target, **moved):
            copies.append(
                pltpu.make_async_remote_copy(
                    source,
                    target,
                    self.send_sem.at[slot + len(copies)],
                    self.recv_sem.at[slot + len(copies)],
                    device_id=place.device(**moved),
                    device_id_type=MESH,
                )
            )

        other_core = place.others("c")[0]
        last = order[2]
        if core:
            slot = number * self.each(place.grid) + sum(place.size(axis) - 1 for axis in order)
            if phase == 2:
                part = self.view(piece, {last: at[last]})
                send(part, part, c=other_core)
            else:
                slot += 1
                for other in place.others(last):
                    part = self.view(piece, {last: other})
                    send(part, part, c=other_core)
            return copies
        axis = order[phase]
        target = self.view(piece, {later: at[later] for later in order[phase:]})
        source = self.shards[array].at[pl.ds(first, rows), :] if phase == 0 else target
        for other in place.others(axis):
            send(source, target, **{axis: other})
        if phase == 0:
            copies.append(pltpu.make_async_copy(source, target, self.local_sem.at[number]))
        return copies

    def advance(self, numbers, phase):
        for number in numbers:
            waits, starts = [], []
            if 0 < phase < 4:
                waits = self.phase(number, phase - 1, False)
            if phase < 3:
                starts = self.phase(number, phase, False)
            if phase in (2, 3):
                starts += self.phase(number, phase, True)
            if phase == 4:
                waits = self.phase(number, 2, True) + self.phase(number, 3, True)
            for copy in waits:
                copy.wait()
            for copy in starts:
                copy.start()


class Scatter:
    PHASES = 4

    def __init__(self, place, pieces, sources, kept, outs, buffers, load_sem, send_sem, recv_sem):
        self.place, self.pieces, self.sources, self.kept, self.outs = place, pieces, sources, kept, outs
        self.buffers, self.load_sem, self.send_sem, self.recv_sem = buffers, load_sem, send_sem, recv_sem

    @staticmethod
    def copies(sizes, pieces):
        return len(pieces) * sum(size - 1 for size in grid_of(sizes))

    @staticmethod
    def scratch(sizes, pieces, shapes, kept):
        deep, high, wide, cores = grid_of(sizes)
        buffers = []
        for source, first, columns, order in pieces:
            rows, dtype = shapes[source]
            near, far = (wide, high) if order == "xy" else (high, wide)
            block = (rows, columns)
            shapes_here = [(deep, high, wide) + block, (near - 1, deep, far) + block, (far - 1, deep) + block, (deep,) + block]
            if not kept[source]:
                shapes_here.append((deep, high, wide) + block)
            buffers += [pltpu.VMEM(shape, dtype) for shape in shapes_here]
        return buffers

    def buffer(self, number, which):
        place = sum(4 if self.kept[piece[0]] else 5 for piece in self.pieces[:number])
        return self.buffers[place + which]

    def half(self, number, core):
        source, first, columns, order = self.pieces[number]
        return self.sources[source].at[:, :, :, core, :, pl.ds(first, columns)]

    def load(self, number):
        return pltpu.make_async_copy(self.half(number, self.place.at["c"]), self.buffer(number, 4), self.load_sem.at[number])

    def phase(self, number, phase):
        place = self.place
        at = place.at
        deep, high, wide, cores = place.sizes
        order = self.pieces[number][3]
        base = number * sum(size - 1 for size in place.sizes)
        axis = ("c" + order + "z")[phase]
        skip = sum(place.size(before) - 1 for before in ("c" + order + "z")[:phase])
        sums = self.buffer(number, 0)
        copies = []
        for step, other in enumerate(place.others(axis)):
            if phase == 0:
                source, target = self.half(number, other), sums
            elif phase == 3:
                source, target = sums.at[other, at["y"], at["x"]], self.buffer(number, 3).at[at["z"]]
            else:
                target = self.buffer(number, phase).at[step]
                y, x = (other, EVERY) if axis == "y" else (EVERY, other)
                if phase == 2:
                    y, x = (other, at["x"]) if axis == "y" else (at["y"], other)
                source = sums.at[:, y, x]
            slot = base + skip + step
            copies.append(
                pltpu.make_async_remote_copy(
                    source,
                    target,
                    self.send_sem.at[slot],
                    self.recv_sem.at[slot],
                    device_id=place.device(**{axis: other}),
                    device_id_type=MESH,
                )
            )
        return copies

    def absorb(self, number, phase):
        source, first, columns, order = self.pieces[number]
        at = self.place.at
        deep = self.place.sizes[0]
        sums = self.buffer(number, 0)
        if phase == 3:
            slots = self.buffer(number, 3)
            slots[at["z"]] = sums[at["z"], at["y"], at["x"]]
            total = slots[0].astype(F32)
            for slot in range(1, deep):
                total += slots[slot].astype(F32)
            self.outs[source][:, first : first + columns] = total
            return

        @pl.loop(0, deep)
        def _(z):
            if phase == 0:
                own = self.sources[source].at[z, :, :, at["c"], :, pl.ds(first, columns)] if self.kept[source] else self.buffer(number, 4).at[z]
                view, parts = sums.at[z], [own[...]]
            else:
                came = self.buffer(number, phase)
                parts = [came[step, z] for step in range(came.shape[0])]
                if phase == 1:
                    view = sums.at[z, :, at["x"]] if order[0] == "x" else sums.at[z, at["y"]]
                else:
                    view = sums.at[z, at["y"], at["x"]]
            total = view[...].astype(F32)
            for part in parts:
                total += part.astype(F32)
            view[...] = total.astype(view.dtype)

    def advance(self, numbers, phase):
        for number in numbers:
            if phase > 0:
                for copy in self.phase(number, phase - 1):
                    copy.wait()
                if phase == 1 and not self.kept[self.pieces[number][0]]:
                    self.load(number).wait()
                self.absorb(number, phase - 1)
            elif not self.kept[self.pieces[number][0]]:
                self.load(number).start()
            if phase < self.PHASES:
                for copy in self.phase(number, phase):
                    copy.start()


class Band:
    def __init__(self, length, reach):
        self.reach = reach
        self.causal = length + reach
        self.two_way = 2 * reach
        self.width = self.causal + self.two_way
        self.query_zero = length - SUB
        self.query_zero_two = reach - SUB
        self.key_zero = reach - SUB

    def distances(self, rows):
        causal = lax.broadcasted_iota(jnp.int32, (1, self.causal), 1)
        two_way = lax.broadcasted_iota(jnp.int32, (1, self.two_way), 1)
        if rows == "queries":
            causal, two_way = self.query_zero - causal, self.query_zero_two - two_way
            return (
                jnp.where(causal <= -self.reach, causal + self.causal, causal),
                jnp.where(two_way <= -self.reach, two_way + self.two_way, two_way),
            )
        causal, two_way = causal - self.key_zero, two_way - self.key_zero
        return (
            jnp.where(causal >= self.causal - self.reach, causal - self.causal, causal),
            jnp.where(two_way >= self.reach, two_way - self.two_way, two_way),
        )


def one_hot(map_ref, band, rows):
    bucket = lax.broadcasted_iota(jnp.int32, (NB, 1), 0)

    def edges(row, number):
        entries = map_ref[row : row + 1, :]
        below = jnp.sum((entries < number).astype(jnp.int32), axis=1, keepdims=True)
        return below, below + jnp.sum((entries == number).astype(jnp.int32), axis=1, keepdims=True)

    causal, two_way = band.distances(rows)
    low, high = edges(0, bucket)
    one = (causal >= low) & (causal < high)
    ahead = bucket >= NB // 2
    low, high = edges(1, jnp.where(ahead, bucket - NB // 2, bucket))
    apart = jnp.abs(two_way)
    two = (apart >= low) & (apart < high) & ((two_way < 0) == ahead)
    return jnp.concatenate([jnp.where(one, 1.0, 0.0), jnp.where(two, 1.0, 0.0)], axis=1), causal


def spread(row, width):
    return pltpu.roll(jnp.broadcast_to(row, (SUB, width)), 0, 1, stride=1, stride_axis=0)


def fold(band):
    width = band.shape[1]
    half = SUB // 2
    while half >= 8:
        band = band[:half] + pltpu.roll(band[half:], width - half, 1)
        half //= 2
    row = lax.broadcasted_iota(jnp.int32, band.shape, 0)
    for bit in (4, 2, 1):
        band = jnp.where((row & bit) != 0, pltpu.roll(band, width - bit, 1), band)
    return jnp.sum(band, axis=0, keepdims=True)


def fill_bands(head, bias_ref, band, causal_ref, two_ref):
    row = bias_ref[pl.ds(head, 1), :]
    causal_ref[...] = spread(row[:, : band.causal], band.causal)
    two_ref[...] = spread(row[:, band.causal :], band.two_way)


def bias_rows(table_ref, map_ref, band, rows):
    hot, causal = one_hot(map_ref, band, rows)
    bias = dot(table_ref[...], hot.astype(BF16), 0, 0)
    return jnp.concatenate([jnp.where(causal < 0, NEG, bias[:, : band.causal]), bias[:, band.causal :]], axis=1)


def head_cols(head):
    group = head // 2
    return pl.ds(pl.multiple_of(group * PAIR, PAIR), PAIR), head % 2


def pick_lanes(half):
    return lax.broadcasted_iota(jnp.int32, (1, PAIR), 1) // DH == half


def soft_rows(scores):
    high = jnp.max(scores, axis=-1, keepdims=True)
    weights = jnp.exp(scores - high)
    total = jnp.sum(weights, axis=-1, keepdims=True)
    return weights.astype(BF16), total, high + jnp.log(total)


def store_head(mixed_ref, lse_ref, rows, cols, head, half, out, total, lse):
    pick = pick_lanes(half)
    mixed_ref[rows, cols] = jnp.where(pick, (out / total).astype(BF16), mixed_ref[rows, cols])
    lane = lax.broadcasted_iota(jnp.int32, (1, lse_ref.shape[1]), 1)
    lse_ref[rows, :] = jnp.where(lane == head, lse, lse_ref[rows, :])


def self_forward_head(head, limit, q_ref, k_ref, v_ref, causal_ref, two_ref, band, mixed_ref, lse_ref):
    length = q_ref.shape[0]
    cols, half = head_cols(head)
    pick = pick_lanes(half)
    block = 256
    for start in range(0, length, block):
        keys = max(start + block, band.reach)
        rows = pl.ds(start, block)
        query = jnp.where(pick, q_ref[rows, cols], 0)
        scores = dot(query, k_ref[pl.ds(0, keys), cols], 1, 1)
        parts = []
        for first in range(start, start + block, SUB):
            at = band.query_zero - first
            bias = causal_ref[:, at : at + keys]
            if start < band.reach:
                at = band.query_zero_two - first
                two = two_ref[:, at : at + keys]
                inside = (first + lax.broadcasted_iota(jnp.int32, (SUB, keys), 0) < limit) & (
                    lax.broadcasted_iota(jnp.int32, (SUB, keys), 1) < limit
                )
                bias = jnp.where(inside, two, bias)
            parts.append(bias)
        weights, total, lse = soft_rows(scores + jnp.concatenate(parts, axis=0))
        out = dot(weights, v_ref[pl.ds(0, keys), cols])
        store_head(mixed_ref, lse_ref, rows, cols, head, half, out, total, lse)


def cross_forward_head(head, q_ref, k_ref, v_ref, mixed_ref, lse_ref):
    length = q_ref.shape[0]
    cols, half = head_cols(head)
    pick = pick_lanes(half)
    block = 256
    for start in range(0, length, block):
        rows = pl.ds(start, block)
        query = jnp.where(pick, q_ref[rows, cols], 0)
        weights, total, lse = soft_rows(dot(query, k_ref[:, cols], 1, 1))
        out = dot(weights, v_ref[:, cols])
        store_head(mixed_ref, lse_ref, rows, cols, head, half, out, total, lse)


def row_blocks(count, block, step):
    @pl.loop(0, count // block)
    def _(index):
        step(pl.ds(pl.multiple_of(index * block, block), block))


def gain_rows(gathered, width):
    devices = gathered.shape[0]
    share = width // devices
    lane = lax.broadcasted_iota(jnp.int32, (SUB, width), 1)
    select = jnp.where(lax.rem(lane, share) == lax.broadcasted_iota(jnp.int32, (SUB, width), 0), 1.0, 0.0)
    first = share * lax.broadcasted_iota(jnp.int32, (devices, width), 0)
    lane = lax.broadcasted_iota(jnp.int32, (devices, width), 1)
    own = (lane >= first) & (lane < first + share)
    rows = []
    for number in range(8):
        spread_out = exact_dot(gathered[:, number, :], select)
        rows.append(jnp.sum(jnp.where(own, spread_out, 0.0), axis=0, keepdims=True))
    return jnp.concatenate(rows, axis=0)


ATTENTION = 8
SHARDS = 12


def gather_pieces(rows, down_rows):
    head, tail = rows // 3 // 8 * 8, rows - rows // 3 // 8 * 8
    half = down_rows // 2
    table = {
        "qk": [(0, 0, rows, "zxy"), (1, 0, rows, "zyx"), (11, 0, 8, "zxy")],
        "v": [(2, 0, head, "xzy"), (2, head, tail, "yzx")],
        "out": [(3, 0, rows, "zxy"), (4, 0, rows, "zyx"), (7, 0, tail, "zxy"), (7, tail, head, "zyx")],
        "memory": [(5, 0, rows, "xzy"), (6, 0, rows, "yzx")],
        "gate": [(8, 0, rows, "zxy"), (9, 0, rows, "zyx")],
        "down": [(10, 0, half, "xzy"), (10, half, half, "yzx")],
    }
    pieces, groups = [], {}
    for name, group in table.items():
        groups[name] = range(len(pieces), len(pieces) + len(group))
        pieces += group
    return pieces, groups


def forward_kernel(
    limit_ref, tokens_ref, memory_ref, table_ref, map_ref, gain1_ref, gain2_ref, gain3_ref, *refs, band, heads, plan,
):
    count = SHARDS - 1 if plan else ATTENTION
    shards, refs = refs[:count], refs[count:]
    if plan:
        gathered, refs = refs[:SHARDS], refs[SHARDS:]
    else:
        gathered = shards
    (
        gains_ref, q1_ref, k1_ref, v1_ref, mixed1_ref, lse1_ref, first_ref,
        q2_ref, k2_ref, v2_ref, mixed2_ref, lse2_ref, second_ref,
        bias_ref, causal_ref, two_ref, weights_ref, share_ref, tile_ref, load_sem, *gather_sems,
    ) = refs
    length, width = tokens_ref.shape
    if plan:
        sizes, pieces, groups = plan
        place = Place(sizes)
        gather = Gather(place, pieces, (*shards, share_ref), gathered, *gather_sems)

    def advance(*steps):
        if plan:
            for numbers, phase in steps:
                gather.advance(groups[numbers], phase)

    def load(number):
        return pltpu.make_async_copy(gathered[number].reshape(width, width), weights_ref.at[number], load_sem.at[number])

    def load_tile():
        return pltpu.make_async_copy(gathered[SHARDS - 1].reshape(tile_ref.shape), tile_ref, load_sem.at[ATTENTION])

    gain_refs = (gain1_ref, gain2_ref, gain3_ref)
    if plan:
        share_ref[...] = jnp.zeros_like(share_ref)
        for number, gain_ref in enumerate(gain_refs):
            share_ref[number : number + 1, : gain_ref.shape[1]] = gain_ref[...].astype(F32)
        place.meet()
    advance(("qk", 0), ("v", 0), ("memory", 0))
    bias_ref[...] = bias_rows(table_ref, map_ref, band, "queries")
    lse1_ref[...] = jnp.zeros_like(lse1_ref)
    lse2_ref[...] = jnp.zeros_like(lse2_ref)
    mixed1_ref[...] = jnp.zeros_like(mixed1_ref)
    mixed2_ref[...] = jnp.zeros_like(mixed2_ref)
    advance(("v", 1), ("out", 0), ("memory", 1), ("qk", 1), ("gate", 0), ("down", 0), ("qk", 2), ("v", 2))
    advance(("qk", 3), ("v", 3), ("out", 1), ("qk", 4), ("v", 4))
    for number in range(3):
        load(number).start()
    if plan:
        load_tile().start()
        load_tile().wait()
        gains_ref[...] = gain_rows(tile_ref[...], width)
    else:
        gains_ref[...] = jnp.zeros_like(gains_ref)
        for number, gain_ref in enumerate(gain_refs):
            gains_ref[number : number + 1, :] = gain_ref[...].astype(F32)
    for number in range(3):
        load(number).wait()

    def project_self(rows):
        value = tokens_ref[rows, :].astype(F32)
        normed = (value * rms(value) * gains_ref[0:1, :]).astype(BF16)
        q1_ref[rows, :] = dot(normed, weights_ref[0]).astype(BF16)
        k1_ref[rows, :] = dot(normed, weights_ref[1]).astype(BF16)
        v1_ref[rows, :] = dot(normed, weights_ref[2]).astype(BF16)

    for start in range(0, length, length // 2):
        project_self(pl.ds(start, length // 2))
        if start == 0:
            advance(("out", 2))

    @pl.loop(0, heads)
    def _(head):
        fill_bands(head, bias_ref, band, causal_ref, two_ref)
        self_forward_head(head, limit_ref[0], q1_ref, k1_ref, v1_ref, causal_ref, two_ref, band, mixed1_ref, lse1_ref)

        for when, steps in (
            (1, (("out", 3), ("memory", 2))),
            (4, (("out", 4), ("down", 1))),
            (6, (("memory", 3),)),
            (8, (("memory", 4), ("gate", 1))),
        ):

            @pl.when(head == when * heads // 12)
            def _(when=when, steps=steps):
                advance(*steps)
                for number in {4: (3, 4, 7), 8: (5, 6)}.get(when, ()):
                    load(number).start()

    advance(("gate", 2))
    for number in range(3, ATTENTION):
        load(number).wait()

    def project_memory(rows):
        k2_ref[rows, :] = dot(memory_ref[rows, :], weights_ref[5]).astype(BF16)
        v2_ref[rows, :] = dot(memory_ref[rows, :], weights_ref[6]).astype(BF16)

    row_blocks(memory_ref.shape[0], 512, project_memory)

    def project_cross(rows):
        value = tokens_ref[rows, :].astype(F32) + dot(mixed1_ref[rows, :], weights_ref[3])
        first_ref[rows, :] = value
        normed = (value * rms(value) * gains_ref[1:2, :]).astype(BF16)
        q2_ref[rows, :] = dot(normed, weights_ref[4]).astype(BF16)

    row_blocks(length, 512, project_cross)

    @pl.loop(0, heads)
    def _(head):
        cross_forward_head(head, q2_ref, k2_ref, v2_ref, mixed2_ref, lse2_ref)

        @pl.when(head == heads // 4)
        def _():
            advance(("down", 2))

        @pl.when(head == heads * 2 // 3)
        def _():
            advance(("gate", 3))

    advance(("down", 3))

    def project_second(rows):
        second_ref[rows, :] = first_ref[rows, :] + dot(mixed2_ref[rows, :], weights_ref[7])

    row_blocks(length, 512, project_second)
    advance(("gate", 4), ("down", 4))


def norm_back_rows(value, gain, grad):
    scale = rms(value)
    unit = value * scale
    scaled = grad * gain
    back = scale * (scaled - unit * jnp.mean(scaled * unit, axis=-1, keepdims=True))
    return back, jnp.sum(grad * unit, axis=0, keepdims=True)


GELU_A = 0.7978845608028654
GELU_B = 0.044715


def feed_kernel(
    second_ref, gout_ref, gains_ref, gate_ref, up_ref, down_ref,
    output_ref, gsecond_ref, ggain_ref, dgate_ref, dup_ref, ddown_ref,
    normed_ref, flipped_ref, out_ref, back_ref, hidden_ref, ggate_ref, gup_ref,
):
    step = pl.program_id(0)
    length = second_ref.shape[0]
    block = 256

    @pl.when(step == 0)
    def _():
        def prepare(rows):
            value = second_ref[rows, :]
            normed = (value * rms(value) * gains_ref[2:3, :]).astype(BF16)
            normed_ref[rows, :] = normed
            flipped_ref[:, rows] = normed.T
            out_ref[rows, :] = value
            back_ref[rows, :] = jnp.zeros_like(value)

        row_blocks(length, block, prepare)

    def rows_step(rows):
        normed = normed_ref[rows, :]
        gate = dot(normed, gate_ref[...])
        upward = dot(normed, up_ref[...])
        square = gate * gate
        bend = jnp.tanh(GELU_A * gate * (1.0 + GELU_B * square))
        half = 0.5 * (1.0 + bend)
        active = gate * half
        hidden = (active * upward).astype(BF16)
        hidden_ref[rows, :] = hidden
        out_ref[rows, :] += dot(hidden, down_ref[...])
        ghidden = dot(gout_ref[rows, :], down_ref[...], 1, 1)
        slope = half + 0.5 * gate * (1.0 - bend * bend) * (GELU_A * (1.0 + 3.0 * GELU_B * square))
        ggate = (ghidden * upward * slope).astype(BF16)
        gup = (ghidden * active).astype(BF16)
        ggate_ref[rows, :] = ggate
        gup_ref[rows, :] = gup
        back_ref[rows, :] += dot(ggate, gate_ref[...], 1, 1) + dot(gup, up_ref[...], 1, 1)

    row_blocks(length, 512, rows_step)
    ddown_ref[...] = dot(hidden_ref[...].T, gout_ref[...]).astype(BF16)
    dgate_ref[...] = dot(flipped_ref[...], ggate_ref[...]).astype(BF16)
    dup_ref[...] = dot(flipped_ref[...], gup_ref[...]).astype(BF16)

    @pl.when(step == pl.num_programs(0) - 1)
    def _():
        ggain_ref[...] = jnp.zeros_like(ggain_ref)

        def finish(rows):
            output_ref[rows, :] = out_ref[rows, :].astype(BF16)
            back, ggain = norm_back_rows(second_ref[rows, :], gains_ref[2:3, :], back_ref[rows, :])
            gsecond_ref[rows, :] = back + gout_ref[rows, :].astype(F32)
            ggain_ref[0:1, :] += ggain

        row_blocks(length, block, finish)


def backward_head_prepare(group_cols, gm_ref, mixed_ref, delta_ref):
    product = (gm_ref[:, group_cols].astype(F32) * mixed_ref[:, group_cols].astype(F32)).T
    delta_ref[0:1, :] = jnp.sum(product[:DH], axis=0, keepdims=True)
    delta_ref[1:2, :] = jnp.sum(product[DH:], axis=0, keepdims=True)


def backward_block(key_rows, cols, half, start, bias, q_ref, k_ref, v_ref, gm_ref, lse, delta, gk_ref, gv_ref, gqt_ref):
    length = q_ref.shape[0]
    pick = pick_lanes(half)
    queries = pl.ds(start, length - start)
    query = jnp.where(pick, q_ref[queries, cols], 0)
    grad = jnp.where(pick, gm_ref[queries, cols], 0)
    keys = k_ref[key_rows, cols]
    scores = dot(keys, query, 1, 1)
    if bias is not None:
        scores = scores + bias
    probs = jnp.exp(scores - lse[:, start:])
    gv = dot(probs.astype(BF16), grad)
    gprobs = dot(v_ref[key_rows, cols], grad, 1, 1)
    gscores = probs * (gprobs - delta[:, start:])
    low = gscores.astype(BF16)
    gk = dot(low, query)
    gk_ref[key_rows, cols] = jnp.where(pick, gk.astype(BF16), gk_ref[key_rows, cols])
    gv_ref[key_rows, cols] = jnp.where(pick, gv.astype(BF16), gv_ref[key_rows, cols])
    gqt_ref[:, queries] += dot(jnp.where(pick, keys, 0).T, low)
    return gscores


def self_backward_head(
    head, limit, q_ref, k_ref, v_ref, gm_ref, mixed_ref, lse_ref, delta_ref, causal_ref, two_ref, band,
    gk_ref, gv_ref, gqt_ref, causal_sum_ref, two_sum_ref,
):
    length = q_ref.shape[0]
    cols, half = head_cols(head)
    lse = lse_ref[pl.ds(head, 1), :]
    delta = delta_ref[pl.ds(half, 1), :]
    reach = band.reach
    block = 256
    for first in range(0, length, block):
        start = 0 if first < reach else first
        count = length - start
        parts = []
        for key in range(first, first + block, SUB):
            at = band.key_zero - key + start
            bias = causal_ref[:, at : at + count]
            if first < reach:
                at = band.key_zero - key
                two = two_ref[:, at : at + reach]
                inside = (key + lax.broadcasted_iota(jnp.int32, (SUB, reach), 0) < limit) & (
                    lax.broadcasted_iota(jnp.int32, (SUB, reach), 1) < limit
                )
                bias = jnp.concatenate([jnp.where(inside, two, bias[:, :reach]), bias[:, reach:]], axis=1)
            parts.append(bias)
        gscores = backward_block(
            pl.ds(first, block), cols, half, start, jnp.concatenate(parts, axis=0),
            q_ref, k_ref, v_ref, gm_ref, lse, delta, gk_ref, gv_ref, gqt_ref,
        )
        for key in range(first, first + block, SUB):
            part = gscores[key - first : key - first + SUB]
            at = band.key_zero - key + start
            if first < reach:
                inside = (key + lax.broadcasted_iota(jnp.int32, (SUB, reach), 0) < limit) & (
                    lax.broadcasted_iota(jnp.int32, (SUB, reach), 1) < limit
                )
                head_part = part[:, :reach]
                at_two = band.key_zero - key
                two_sum_ref[:, at_two : at_two + reach] += jnp.where(inside, head_part, 0.0)
                causal_sum_ref[:, at : at + reach] += jnp.where(inside, 0.0, head_part)
                causal_sum_ref[:, at + reach : at + count] += part[:, reach:]
            else:
                causal_sum_ref[:, at : at + count] += part


def split_columns(number, columns):
    half = columns // 2
    return [(number, 0, half, "xy"), (number, half, half, "yx")]


def cross_backward_kernel(
    gsecond_ref, first_ref, memory_ref, gains_ref, q_ref, k_ref, v_ref, mixed1_ref, mixed2_ref, lse_ref,
    wo_ref, cq_ref, ck_ref, cv_ref, co_ref, *refs, heads, plan,
):
    count = 2 if plan else 0
    sources, refs = refs[:count], refs[count:]
    gmem_ref, gfirst_ref, gm1_ref, ggain_ref, dwo_ref, dcq_ref, dck_ref, dcv_ref, dco_ref, *refs = refs
    outs, refs = refs[:count], refs[count:]
    gm_ref, branch_ref, flipped_ref, lse_rows_ref, delta_ref, gq_ref, gk_ref, gv_ref, gqt_ref, *refs = refs
    if plan:
        sizes, pieces = plan
        scatter = Scatter(Place(sizes), pieces, sources, [False] * count, outs, refs[:-3], *refs[-3:])
        soon, later = range(len(pieces) // 2), range(len(pieces) // 2, len(pieces))
        scatter.place.meet()
        scatter.advance(soon, 0)
        scatter.advance(later, 0)
    length, width = first_ref.shape
    source = memory_ref.shape[0]
    block = 256

    def prepare(rows):
        branch = gsecond_ref[rows, :].astype(BF16)
        branch_ref[rows, :] = branch
        gm_ref[rows, :] = dot(branch, co_ref[...], 1, 1).astype(BF16)
        flipped_ref[:, rows] = mixed2_ref[rows, :].T

    row_blocks(length, 512, prepare)

    def out_grad(rows):
        dco_ref[rows, :] = dot(flipped_ref[rows, :], branch_ref[...]).astype(BF16)

    row_blocks(width, 384, out_grad)
    if plan:
        scatter.advance(soon, 1)
    lse_rows_ref[...] = lse_ref[...].T
    gk_ref[...] = jnp.zeros_like(gk_ref)
    gv_ref[...] = jnp.zeros_like(gv_ref)
    groups = heads // 2

    @pl.loop(0, groups)
    def _(group):
        if plan:

            @pl.when(group == groups // 3)
            def _():
                scatter.advance(soon, 2)
                scatter.advance(later, 1)

            @pl.when(group == groups - 2)
            def _():
                scatter.advance(soon, 3)

        cols = pl.ds(pl.multiple_of(group * PAIR, PAIR), PAIR)
        backward_head_prepare(cols, gm_ref, mixed2_ref, delta_ref)
        gqt_ref[...] = jnp.zeros_like(gqt_ref)

        @pl.loop(0, 2)
        def _(half):
            head = group * 2 + half
            for first in range(0, source, block):
                backward_block(
                    pl.ds(first, block), cols, half, 0, None, q_ref, k_ref, v_ref, gm_ref,
                    lse_rows_ref[pl.ds(head, 1), :], delta_ref[pl.ds(half, 1), :], gk_ref, gv_ref, gqt_ref,
                )

        gq_ref[:, cols] = gqt_ref[...].T.astype(BF16)

    if plan:
        scatter.advance(later, 2)

    def memory_grad(rows):
        gmem_ref[rows, :] = dot(gk_ref[rows, :], ck_ref[...], 1, 1) + dot(gv_ref[rows, :], cv_ref[...], 1, 1)
        flipped_ref[:, rows] = memory_ref[rows, :].T

    row_blocks(source, 512, memory_grad)

    def memory_weights(rows):
        flipped = flipped_ref[rows, :source]
        dck_ref[rows, :] = dot(flipped, gk_ref[...]).astype(BF16)
        dcv_ref[rows, :] = dot(flipped, gv_ref[...]).astype(BF16)

    row_blocks(width, 384, memory_weights)
    if plan:
        scatter.advance(later, 3)
        scatter.advance(soon, 4)
    ggain_ref[...] = jnp.zeros_like(ggain_ref)

    def first_grad(rows):
        value = first_ref[rows, :]
        flipped_ref[:, rows] = (value * rms(value) * gains_ref[1:2, :]).astype(BF16).T
        back, ggain = norm_back_rows(value, gains_ref[1:2, :], dot(gq_ref[rows, :], cq_ref[...], 1, 1))
        ggain_ref[0:1, :] += ggain
        gfirst = back + gsecond_ref[rows, :]
        gfirst_ref[rows, :] = gfirst
        branch = gfirst.astype(BF16)
        branch_ref[rows, :] = branch
        gm1_ref[rows, :] = dot(branch, wo_ref[...], 1, 1).astype(BF16)

    row_blocks(length, 512, first_grad)

    def query_weights(rows):
        dcq_ref[rows, :] = dot(flipped_ref[rows, :], gq_ref[...]).astype(BF16)

    row_blocks(width, 384, query_weights)

    def flip_mixed(rows):
        flipped_ref[:, rows] = mixed1_ref[rows, :].T

    row_blocks(length, block, flip_mixed)

    def out_weights(rows):
        dwo_ref[rows, :] = dot(flipped_ref[rows, :], branch_ref[...]).astype(BF16)

    row_blocks(width, 384, out_weights)
    if plan:
        scatter.advance(later, 4)


def store_shares(ref, cols, value, start):
    if len(ref.shape) == 2:
        ref[pl.ds(start, value.shape[0]), cols] = value.astype(BF16)
    else:
        deep, high, wide, cores, rows, columns = ref.shape
        chunk = high * wide * cores * rows
        ref[start // chunk, :, :, :, :, cols] = value.reshape(high, wide, cores, rows, value.shape[1]).astype(BF16)


TILE = 16


def fill_tiles(tiles_ref, gtable, ggains):
    deep, high, wide, cores, rows, lanes = tiles_ref.shape
    devices = deep * high * wide * cores
    width = ggains[0].shape[1]
    share = width // devices
    lane = lax.broadcasted_iota(jnp.int32, (SUB, width), 1)
    select = jnp.where(lax.rem(lane, share) == lax.broadcasted_iota(jnp.int32, (SUB, width), 0), 1.0, 0.0)
    first = share * lax.broadcasted_iota(jnp.int32, (devices, width), 0)
    lane = lax.broadcasted_iota(jnp.int32, (devices, width), 1)
    own = (lane >= first) & (lane < first + share)
    parts = [exact_dot(jnp.where(own, ggain, 0.0), select, 1, 1) for ggain in ggains]
    tiles_ref[...] = jnp.zeros_like(tiles_ref)
    heads, buckets = gtable.shape
    for device in range(devices):
        at = tuple(int(part) for part in (device // (high * wide * cores), device // (wide * cores) % high, device // cores % wide, device % cores))
        tiles_ref[(*at, slice(0, heads), slice(0, buckets))] = gtable
        for number, part in enumerate(parts):
            row = TILE - len(parts) + number
            tiles_ref[(*at, slice(row, row + 1), EVERY)] = part[device : device + 1]


REST = 6


def self_pieces(down_columns, columns):
    first = split_columns(0, down_columns) + [(1, 0, columns, "xy"), (2, 0, columns, "yx")]
    rest = [(3, 0, columns, "xy"), (4, 0, columns, "yx")] + split_columns(5, columns)
    half = columns // 2
    early = [(REST, 0, half, "xy"), (REST + 1, 0, half, "yx"), (REST + 2, 0, half, "xy")]
    late = [(REST, half, half, "yx"), (REST + 1, half, half, "xy"), (REST + 2, half, half, "yx"), (REST + 3, 0, SUB, "xy")]
    pieces, groups = [], []
    for group in (first, rest, early, late):
        groups.append(range(len(pieces), len(pieces) + len(group)))
        pieces += group
    return pieces, groups


def self_backward_kernel(
    limit_ref, tokens_ref, gains_ref, table_ref, map_ref, q_ref, k_ref, v_ref, mixed_ref, lse_ref, gm_ref, gfirst_ref,
    ggain2_ref, ggain3_ref, wq_ref, wk_ref, wv_ref, *refs, band, heads, plan,
):
    count = REST if plan else 0
    sources, refs = refs[:count], refs[count:]
    gtokens_ref, refs = refs[0], refs[1:]
    if plan:
        outs, refs = refs[: REST + 3], refs[REST + 3 :]
        gtable_ref, *ggain_refs = refs[:4]
        refs = refs[4:]
    else:
        ggain_ref, gtable_ref, dwq_ref, dwk_ref, dwv_ref, *refs = refs
    (
        bias_ref, causal_ref, two_ref, flipped_ref, lse_rows_ref, delta_ref, gq_ref, gk_ref, gv_ref, gqt_ref,
        causal_sum_ref, two_sum_ref, sums_ref, *refs,
    ) = refs
    length, width = tokens_ref.shape
    block = 256
    groups = heads // 2
    if plan:
        sizes, pieces, (first, rest, early, late) = plan
        dwq_ref, dwk_ref, dwv_ref, tiles_ref, tile_ref, ggain_ref, *refs = refs
        scatter = Scatter(
            Place(sizes), pieces, (*sources, dwq_ref, dwk_ref, dwv_ref, tiles_ref), [False] * REST + [True] * 4,
            (*outs, tile_ref), refs[:-3], *refs[-3:],
        )
        scatter.place.meet()
        scatter.advance(first, 0)
        scatter.advance(rest, 0)
    bias_ref[...] = bias_rows(table_ref, map_ref, band, "keys")
    lse_rows_ref[...] = lse_ref[...].T
    gk_ref[...] = jnp.zeros_like(gk_ref)
    gv_ref[...] = jnp.zeros_like(gv_ref)
    sums_ref[...] = jnp.zeros_like(sums_ref)

    def flip_normed(rows):
        value = tokens_ref[rows, :].astype(F32)
        flipped_ref[:, rows] = (value * rms(value) * gains_ref[0:1, :]).astype(BF16).T

    row_blocks(length, block, flip_normed)

    def group_step(group):
        cols = pl.ds(pl.multiple_of(group * PAIR, PAIR), PAIR)
        backward_head_prepare(cols, gm_ref, mixed_ref, delta_ref)
        gqt_ref[...] = jnp.zeros_like(gqt_ref)

        @pl.loop(0, 2)
        def _(half):
            head = group * 2 + half
            fill_bands(head, bias_ref, band, causal_ref, two_ref)
            causal_sum_ref[...] = jnp.zeros_like(causal_sum_ref)
            two_sum_ref[...] = jnp.zeros_like(two_sum_ref)
            self_backward_head(
                head, limit_ref[0], q_ref, k_ref, v_ref, gm_ref, mixed_ref, lse_rows_ref, delta_ref,
                causal_ref, two_ref, band, gk_ref, gv_ref, gqt_ref, causal_sum_ref, two_sum_ref,
            )
            sums_ref[pl.ds(head, 1), : band.causal] = fold(causal_sum_ref[...])
            sums_ref[pl.ds(head, 1), band.causal :] = fold(two_sum_ref[...])

        gq_ref[:, cols] = gqt_ref[...].T.astype(BF16)

    rows_each = width // (sizes["dp"] // (sizes["fsdp"] // 2)) if plan else block

    def weights(cols):
        @pl.loop(0, width // rows_each)
        def _(index):
            start = pl.multiple_of(index * rows_each, 64)
            flipped = flipped_ref[pl.ds(start, rows_each), :]
            for target, grad in ((dwq_ref, gq_ref), (dwk_ref, gk_ref), (dwv_ref, gv_ref)):
                store_shares(target, cols, dot(flipped, grad[:, cols]), start)

    half_groups = groups // 2
    low, high = pl.ds(0, width // 2), pl.ds(width // 2, width // 2)

    @pl.loop(0, groups)
    def _(group):
        if plan:

            @pl.when(group == 1)
            def _():
                scatter.advance(first, 1)

            @pl.when(group == half_groups)
            def _():
                weights(low)
                scatter.advance(early, 0)
                scatter.advance(first, 2)
                scatter.advance(rest, 1)

            @pl.when(group == half_groups + 1)
            def _():
                scatter.advance(first, 3)
                scatter.advance(early, 1)

            @pl.when(group == groups - 1)
            def _():
                scatter.advance(rest, 2)

        group_step(group)

    if plan:
        weights(high)
        scatter.advance(late[:3], 0)
        scatter.advance(early, 2)
        scatter.advance(rest, 3)
    else:
        weights(low)
        weights(high)
    hot, unused = one_hot(map_ref, band, "keys")
    gtable = exact_dot(sums_ref[...], hot, 1, 1)
    ggain_ref[...] = jnp.zeros_like(ggain_ref)

    def tokens_grad(rows):
        value = tokens_ref[rows, :].astype(F32)
        grad = dot(gq_ref[rows, :], wq_ref[...], 1, 1)
        grad += dot(gk_ref[rows, :], wk_ref[...], 1, 1)
        grad += dot(gv_ref[rows, :], wv_ref[...], 1, 1)
        back, ggain = norm_back_rows(value, gains_ref[0:1, :], grad)
        ggain_ref[0:1, :] += ggain
        gtokens_ref[rows, :] = back + gfirst_ref[rows, :]

    if plan:
        scatter.advance(late[:3], 1)
        steps = (first, 4), (early, 3), (late[:3], 2), (rest, 4)
        for number, step in enumerate(steps):
            for start in range(number * length // 4, (number + 1) * length // 4, block):
                tokens_grad(pl.ds(start, block))
            scatter.advance(*step)
        fill_tiles(tiles_ref, gtable, [ggain_ref[0:1, :], ggain2_ref[0:1, :], ggain3_ref[0:1, :]])
        scatter.advance(late[3:], 0)
        scatter.advance(late[:3], 3)
        scatter.advance(late[3:], 1)
        scatter.advance(early, 4)
        scatter.advance(late[3:], 2)
        scatter.advance(late[3:], 3)
        scatter.advance(late, 4)
        tile = tile_ref[...]
        gtable_ref[...] = tile.T[:NB, :heads]
        for number, ref in enumerate(ggain_refs):
            row = TILE - len(ggain_refs) + number
            ref[...] = tile[row : row + 1, : ref.shape[1]]
    else:
        row_blocks(length, block, tokens_grad)
        gtable_ref[...] = gtable.T


def hand_on_kernel(*refs):
    count = (len(refs) - 2) // 3
    ins, outs, held, (in_sem, out_sem) = refs[:count], refs[count : 2 * count], refs[2 * count : 3 * count], refs[3 * count :]
    loads = [pltpu.make_async_copy(ins[i], held[i], in_sem.at[i]) for i in range(count)]
    stores = [pltpu.make_async_copy(held[i], outs[i], out_sem.at[i]) for i in range(count)]
    for load in loads:
        load.start()
    for load, store in zip(loads, stores):
        load.wait()
        store.start()
    for store in stores:
        store.wait()


def hand_on(arrays):
    spec = pl.BlockSpec(memory_space=pl.ANY)
    return pl.pallas_call(
        hand_on_kernel,
        out_shape=[jax.ShapeDtypeStruct(a.shape, a.dtype) for a in arrays],
        in_specs=[spec] * len(arrays),
        out_specs=[spec] * len(arrays),
        scratch_shapes=[pltpu.VMEM(a.shape, a.dtype) for a in arrays] + [pltpu.SemaphoreType.DMA((len(arrays),))] * 2,
        compiler_params=params(),
        name="hand_on",
    )(*arrays)


def vmem(*shapes):
    return [pltpu.VMEM(shape, dtype) for shape, dtype in shapes]


def params(**kw):
    return pltpu.CompilerParams(vmem_limit_bytes=60 * 1024 * 1024, **kw)


def per_device(
    inputs, encoded, out_grad, prefix, bucket_map, bias_table,
    norm_self, self_query, self_key, self_value, self_out,
    norm_cross, cross_query, cross_key, cross_value, cross_out,
    norm_feed, feed_gate, feed_up, feed_down,
):
    seqs, length, width = inputs.shape
    source = encoded.shape[1]
    heads = bias_table.shape[1]
    ff = feed_gate.shape[1]
    band = Band(length, length // 2)
    tokens = inputs.reshape(length, width)
    memory = encoded.reshape(source, width)
    gout = out_grad.reshape(length, width)
    gains_in = [norm_self, norm_cross, norm_feed]
    projections = [self_query, self_key, self_value, self_out, cross_query, cross_key, cross_value, cross_out]
    feeds = [feed_gate, feed_up, feed_down]
    sizes = dict(dp=lax.axis_size("dp"), fsdp=lax.axis_size("fsdp"))
    devices = sizes["dp"] * sizes["fsdp"]
    own = self_query.shape[0] % 8 == 0
    if own:
        pieces, groups = gather_pieces(self_query.shape[0], feed_down.shape[0])
        plan = (sizes, pieces, groups)
        copies = Gather.copies(sizes, pieces)
        shards = projections + feeds
    else:
        plan = None
        gains_in = [lax.all_gather(gain, AXES, axis=0, tiled=True) for gain in gains_in]
        shards = [lax.all_gather(shard, AXES, axis=0, tiled=True) for shard in projections]
        gate_full, up_full, down = [lax.all_gather(shard, AXES, axis=0, tiled=True) for shard in feeds]
    gains_in = [gain.reshape(1, -1) for gain in gains_in]

    remote = pl.BlockSpec(memory_space=pl.ANY)
    scalar = pl.BlockSpec(memory_space=pltpu.SMEM)

    def full(shape):
        return pl.BlockSpec(shape, lambda *_: (0,) * len(shape))

    def like(shape, dtype):
        return jax.ShapeDtypeStruct(shape, dtype)

    act = like((length, width), BF16)
    mem = like((source, width), BF16)
    act32 = like((length, width), F32)
    lse_shape = like((length, SUB), F32)
    gain_shape = like((8, width), F32)
    outs = [gain_shape, act, act, act, act, lse_shape, act32, act, mem, mem, act, lse_shape, act32]
    gathered_shapes = []
    if own:
        chips, cores = grid_of(sizes)[:3], grid_of(sizes)[3]
        gathered_shapes = [like(chips + (cores * shard.shape[0], shard.shape[1]), shard.dtype) for shard in shards]
        gathered_shapes.append(like(chips + (cores * 8, SUB), F32))
    forward_in = (tokens, memory, bias_table, bucket_map, *gains_in)
    results = pl.pallas_call(
        functools.partial(forward_kernel, band=band, heads=heads, plan=plan),
        out_shape=gathered_shapes + outs,
        grid=(1,),
        in_specs=[scalar] + [full(a.shape) for a in forward_in]
        + ([full(a.shape) for a in shards] if own else [remote] * len(shards)),
        out_specs=[remote] * len(gathered_shapes) + [full(o.shape) for o in outs],
        scratch_shapes=vmem(
            ((heads, band.width), F32), ((SUB, band.causal), F32), ((SUB, band.two_way), F32),
            ((ATTENTION, width, width), BF16), ((8, SUB), F32), ((devices, 8, SUB), F32),
        )
        + [pltpu.SemaphoreType.DMA((ATTENTION + 1,))]
        + ([pltpu.SemaphoreType.DMA((number,)) for number in (len(pieces), copies, copies)] if own else []),
        compiler_params=params(collective_id=0, has_side_effects=True) if own else params(),
        name="forward",
    )(prefix, *forward_in, *shards)
    attention = shards
    if own:
        gathered, results = results[:SHARDS], results[SHARDS:]
        attention = [part.reshape(width, width) for part in gathered[:ATTENTION]]
        gate_full, up_full = gathered[8].reshape(width, ff), gathered[9].reshape(width, ff)
        down = gathered[10].reshape(ff, width)
    gains, q1, k1, v1, mixed1, lse1, first, q2, k2, v2, mixed2, lse2, second = results

    fblock = min(1024, ff)
    ggain_shape = like((8, width), F32)
    feed_out = [
        act, act32, ggain_shape, like((width, ff), BF16), like((width, ff), BF16), like((ff, width), BF16)
    ]
    output, gsecond, ggain_feed, dgate, dup, ddown = pl.pallas_call(
        feed_kernel,
        out_shape=feed_out,
        grid=(ff // fblock,),
        in_specs=[full(second.shape), full(gout.shape), full(gains.shape)]
        + [
            pl.BlockSpec((width, fblock), lambda i: (0, i)),
            pl.BlockSpec((width, fblock), lambda i: (0, i)),
            pl.BlockSpec((fblock, width), lambda i: (i, 0)),
        ],
        out_specs=[full(o.shape) for o in feed_out[:3]]
        + [
            pl.BlockSpec((width, fblock), lambda i: (0, i)),
            pl.BlockSpec((width, fblock), lambda i: (0, i)),
            pl.BlockSpec((fblock, width), lambda i: (i, 0)),
        ],
        scratch_shapes=vmem(
            ((length, width), BF16), ((width, length), BF16), ((length, width), F32), ((length, width), F32),
            ((length, fblock), BF16), ((length, fblock), BF16), ((length, fblock), BF16),
        ),
        compiler_params=params(),
        name="feed",
    )(second, gout, gains, gate_full, up_full, down)

    square = like((width, width), BF16)
    cross_shapes = [like((source, width), F32), act32, act, ggain_shape] + [square] * 5
    cross_in = (gsecond, first, memory, gains, q2, k2, v2, mixed1, mixed2, lse2)
    cross_scratch = vmem(
        ((length, width), BF16), ((length, width), BF16), ((width, length), BF16), ((SUB, length), F32),
        ((8, length), F32), ((length, width), BF16), ((source, width), BF16), ((source, width), BF16),
        ((PAIR, length), F32),
    )
    grid = grid_of(sizes)

    def shares(grads):
        return [grad.reshape(grid + (grad.shape[0] // devices, grad.shape[1])) for grad in grads]

    def scatter_scratch(pieces, shapes, kept):
        count = Scatter.copies(sizes, pieces)
        return Scatter.scratch(sizes, pieces, shapes, kept) + [
            pltpu.SemaphoreType.DMA((number,)) for number in (len(pieces), count, count)
        ]

    plan, sources, gate_shapes, scratch = None, [], [], []
    if own:
        sources = shares([dgate, dup])
        half = ff // 2
        pieces = [(0, 0, half, "xy"), (1, 0, half, "yx"), (0, half, half, "xy"), (1, half, half, "yx")]
        plan = (sizes, pieces)
        gate_shapes = [like(part.shape[-2:], F32) for part in sources]
        scratch = scatter_scratch(pieces, [(part.shape[-2], BF16) for part in sources], [False, False])
    cross_shapes += gate_shapes
    gmem, gfirst, gm1, ggain_cross, dwo, dcq, dck, dcv, dco, *feed_grads = pl.pallas_call(
        functools.partial(cross_backward_kernel, heads=heads, plan=plan),
        out_shape=cross_shapes,
        grid=(1,),
        in_specs=[full(a.shape) for a in cross_in] + [full((width, width))] * 5 + [remote] * len(sources),
        out_specs=[full(o.shape) for o in cross_shapes],
        scratch_shapes=cross_scratch + scratch,
        compiler_params=params(collective_id=1, has_side_effects=True) if own else params(),
        name="cross_backward",
    )(*cross_in, *attention[3:], *sources)

    self_in = (tokens, gains, bias_table, bucket_map, q1, k1, v1, mixed1, lse1, gm1, gfirst, ggain_cross, ggain_feed)
    self_scratch = vmem(
        ((heads, band.width), F32), ((SUB, band.causal), F32), ((SUB, band.two_way), F32), ((width, length), BF16),
        ((SUB, length), F32), ((8, length), F32), ((length, width), BF16), ((length, width), BF16),
        ((length, width), BF16), ((PAIR, length), F32), ((SUB, band.causal), F32), ((SUB, band.two_way), F32),
        ((heads, band.width), F32),
    )
    plan, sources, scratch = None, [], []
    table_shape = like((NB, heads), F32)
    if own:
        sources = shares([ddown, dco, dwo, dcq, dck, dcv])
        pieces, groups = self_pieces(width, width)
        plan = (sizes, pieces, groups)
        share = width // devices
        kept = [False] * REST + [True] * 4
        shapes = [(part.shape[-2], BF16) for part in sources] + [(share, BF16)] * 3 + [(TILE, F32)]
        self_shapes = [act32] + [like(part.shape[-2:], F32) for part in sources] + [like((share, width), F32)] * 3
        self_shapes += [table_shape] + [like((1, share), F32)] * 3
        scratch = vmem(*[(grid + (share, width), BF16)] * 3, (grid + (TILE, SUB), F32), ((TILE, SUB), F32), ((8, width), F32))
        scratch += scatter_scratch(pieces, shapes, kept)
    else:
        self_shapes = [act32, ggain_shape, table_shape] + [square] * 3
    gtokens, *grads = pl.pallas_call(
        functools.partial(self_backward_kernel, band=band, heads=heads, plan=plan),
        out_shape=self_shapes,
        grid=(1,),
        in_specs=[scalar] + [full(a.shape) for a in self_in] + [full((width, width))] * 3 + [remote] * len(sources),
        out_specs=[full(o.shape) for o in self_shapes],
        scratch_shapes=self_scratch + scratch,
        compiler_params=params(collective_id=2, has_side_effects=True) if own else params(),
        name="self_backward",
    )(prefix, *self_in, *attention[:3], *sources)

    if own:
        gtokens, gmem, dgate, dup, *grads = hand_on([gtokens, gmem, *feed_grads, *grads])
        ddown, dco, dwo, dcq, dck, dcv, dwq, dwk, dwv, table_grad, *ggains = grads
        ggains = [ggain.reshape(-1) for ggain in ggains]
    else:
        ggain_self, gtable, dwq, dwk, dwv = grads
        table_grad = lax.psum(gtable, AXES)

        def scatter(parts, axis):
            return lax.psum_scatter(jnp.concatenate(parts, axis=1 - axis), AXES, scatter_dimension=axis, tiled=True)

        ggains = scatter([ggain_self[:1], ggain_cross[:1], ggain_feed[:1]], 1)
        dgate, dup = jnp.split(scatter([dgate, dup], 0).astype(F32), 2, axis=1)
        ddown = scatter([ddown], 0).astype(F32)
        squares = scatter([dwq, dwk, dwv, dwo, dcq, dck, dcv, dco], 0).astype(F32)
        dwq, dwk, dwv, dwo, dcq, dck, dcv, dco = jnp.split(squares, 8, axis=1)
    return (
        output.reshape(inputs.shape),
        gtokens.reshape(inputs.shape),
        gmem.reshape(encoded.shape),
        table_grad,
        ggains[0], dwq, dwk, dwv, dwo,
        ggains[1], dcq, dck, dcv, dco,
        ggains[2], dgate, dup, ddown,
    )


def solution(mesh):
    rows = P(AXES, None)
    gain = P(AXES)
    block = P(AXES, None, None)
    return jax.shard_map(
        per_device,
        mesh=mesh,
        in_specs=(block, block, block, gain, P(), P())
        + (gain, rows, rows, rows, rows)
        + (gain, rows, rows, rows, rows)
        + (gain, rows, rows, rows),
        out_specs=(block, block, block, P())
        + (gain, rows, rows, rows, rows)
        + (gain, rows, rows, rows, rows)
        + (gain, rows, rows, rows),
        check_vma=False,
    )
```

```python
import functools

import jax
import jax.numpy as jnp
from jax import lax
from jax.experimental import pallas as pl
from jax.experimental.pallas import tpu as pltpu
from jax.sharding import PartitionSpec as P

DH = 64
NB = 32
PAIR = 2 * DH
SUB = 128
NEG = -1e30
F32 = jnp.float32
BF16 = jnp.bfloat16
AXES = ("dp", "fsdp")


def dot(a, b, ca=1, cb=0):
    return lax.dot_general(a, b, (((ca,), (cb,)), ((), ())), preferred_element_type=F32)


def exact_dot(a, b, ca=1, cb=0):
    return lax.dot_general(
        a,
        b,
        (((ca,), (cb,)), ((), ())),
        preferred_element_type=F32,
        precision=lax.Precision.HIGHEST,
    )


def rms(value):
    return lax.rsqrt(jnp.mean(value * value, axis=-1, keepdims=True) + 1e-06)


MESH = pl.DeviceIdType.MESH
EVERY = slice(None)


class Place:
    def __init__(self, sizes):
        self.grid = sizes
        self.sizes = grid_of(sizes)
        across, inner = lax.axis_index("dp"), lax.axis_index("fsdp")
        deep, high, wide, cores = self.sizes
        self.at = {
            "z": lax.div(across, high),
            "y": lax.rem(across, high),
            "x": lax.div(inner, cores),
            "c": lax.rem(inner, cores),
        }

    def device(self, **moved):
        at = {**self.at, **moved}
        deep, high, wide, cores = self.sizes
        return (at["z"] * high + at["y"], at["x"] * cores + at["c"])

    def size(self, axis):
        return self.sizes["zyxc".index(axis)]

    def others(self, axis):
        size = self.size(axis)
        return [lax.rem(self.at[axis] + step, size) for step in range(1, size)]

    def greet(self):
        barrier = pltpu.get_barrier_semaphore()
        for peer in self.peers():
            pl.semaphore_signal(barrier, inc=1, device_id=peer, device_id_type=MESH)

    def meet(self):
        pl.semaphore_wait(pltpu.get_barrier_semaphore(), len(self.peers()))

    def peers(self):
        return [self.device(**{axis: other}) for axis in "zyxc" for other in self.others(axis)]


def grid_of(sizes):
    wide = sizes["fsdp"] // 2
    return (sizes["dp"] // wide, wide, wide, 2)


class Moves:
    def __init__(self, ins, outs, refs):
        count = len(ins) + len(outs)
        self.ins, self.outs = ins, outs
        self.held, self.sem, self.rest = refs[:count], refs[count], refs[count + 1 :]
        self.held_ins, self.held_outs = self.held[: len(ins)], self.held[len(ins) :]
        self.stored = []

    @staticmethod
    def scratch(arrays):
        return [pltpu.VMEM(a.shape, a.dtype) for a in arrays] + [pltpu.SemaphoreType.DMA((len(arrays),))]

    def copy(self, number):
        if number < len(self.ins):
            return pltpu.make_async_copy(self.ins[number], self.held[number], self.sem.at[number])
        return pltpu.make_async_copy(self.held[number], self.outs[number - len(self.ins)], self.sem.at[number])

    def load(self, *numbers):
        for number in numbers:
            self.copy(number).start()

    def need(self, *numbers):
        for number in numbers:
            self.copy(number).wait()

    def store(self, *numbers):
        for number in numbers:
            self.copy(len(self.ins) + number).start()
            self.stored.append(len(self.ins) + number)

    def finish(self):
        for number in self.stored:
            self.copy(number).wait()


class Gather:
    PHASES = 4

    def __init__(self, place, pieces, shards, outs, local_sem, send_sem, recv_sem):
        self.place, self.pieces, self.shards, self.outs = place, pieces, shards, outs
        self.local_sem, self.send_sem, self.recv_sem = local_sem, send_sem, recv_sem

    @staticmethod
    def each(sizes):
        grid = grid_of(sizes)
        return sum(size - 1 for size in grid[:3]) + max(grid[:3])

    @staticmethod
    def copies(sizes, pieces):
        return len(pieces) * Gather.each(sizes)

    def view(self, piece, held):
        array, first, rows, order = piece
        start = self.place.at["c"] * (self.outs[array].shape[3] // 2) + first
        where = [held.get(axis, EVERY) for axis in "zyx"]
        return self.outs[array].at[(*where, pl.ds(pl.multiple_of(start, 8), rows), EVERY)]

    def phase(self, number, phase, core):
        piece = self.pieces[number]
        place, at = self.place, self.place.at
        array, first, rows, order = piece
        slot = number * self.each(place.grid) + sum(place.size(axis) - 1 for axis in order[:phase])
        copies = []

        def send(source, target, **moved):
            copies.append(
                pltpu.make_async_remote_copy(
                    source,
                    target,
                    self.send_sem.at[slot + len(copies)],
                    self.recv_sem.at[slot + len(copies)],
                    device_id=place.device(**moved),
                    device_id_type=MESH,
                )
            )

        other_core = place.others("c")[0]
        last = order[2]
        if core:
            slot = number * self.each(place.grid) + sum(place.size(axis) - 1 for axis in order)
            if phase == 2:
                part = self.view(piece, {last: at[last]})
                send(part, part, c=other_core)
            else:
                slot += 1
                for other in place.others(last):
                    part = self.view(piece, {last: other})
                    send(part, part, c=other_core)
            return copies
        axis = order[phase]
        target = self.view(piece, {later: at[later] for later in order[phase:]})
        source = self.shards[array].at[pl.ds(first, rows), :] if phase == 0 else target
        for other in place.others(axis):
            send(source, target, **{axis: other})
        if phase == 0:
            copies.append(pltpu.make_async_copy(source, target, self.local_sem.at[number]))
        return copies

    def advance(self, numbers, phase):
        for number in numbers:
            waits, starts = [], []
            if 0 < phase < 4:
                waits = self.phase(number, phase - 1, False)
            if phase < 3:
                starts = self.phase(number, phase, False)
            if phase in (2, 3):
                starts += self.phase(number, phase, True)
            if phase == 4:
                waits = self.phase(number, 2, True) + self.phase(number, 3, True)
            for copy in waits:
                copy.wait()
            for copy in starts:
                copy.start()

    def settle(self, numbers):
        for number in numbers:
            for copy in self.phase(number, 0, False):
                copy.wait()

    def resume(self, numbers):
        for number in numbers:
            for copy in self.phase(number, 1, False):
                copy.start()


class Scatter:
    PHASES = 4

    def __init__(self, place, pieces, sources, kept, outs, buffers, load_sem, send_sem, recv_sem):
        self.place, self.pieces, self.sources, self.kept, self.outs = place, pieces, sources, kept, outs
        self.buffers, self.load_sem, self.send_sem, self.recv_sem = buffers, load_sem, send_sem, recv_sem

    @staticmethod
    def copies(sizes, pieces):
        return len(pieces) * sum(size - 1 for size in grid_of(sizes))

    @staticmethod
    def scratch(sizes, pieces, shapes, kept):
        deep, high, wide, cores = grid_of(sizes)
        buffers = []
        for source, first, columns, order in pieces:
            rows, dtype = shapes[source]
            near, far = (wide, high) if order == "xy" else (high, wide)
            block = (rows, columns)
            shapes_here = [(deep, high, wide) + block, (near - 1, deep, far) + block, (far - 1, deep) + block, (deep,) + block]
            if not kept[source]:
                shapes_here.append((deep, high, wide) + block)
            buffers += [pltpu.VMEM(shape, dtype) for shape in shapes_here]
        return buffers

    def buffer(self, number, which):
        place = sum(4 if self.kept[piece[0]] else 5 for piece in self.pieces[:number])
        return self.buffers[place + which]

    def half(self, number, core):
        source, first, columns, order = self.pieces[number]
        return self.sources[source].at[:, :, :, core, :, pl.ds(first, columns)]

    def load(self, number):
        return pltpu.make_async_copy(self.half(number, self.place.at["c"]), self.buffer(number, 4), self.load_sem.at[number])

    def phase(self, number, phase):
        place = self.place
        at = place.at
        deep, high, wide, cores = place.sizes
        order = self.pieces[number][3]
        base = number * sum(size - 1 for size in place.sizes)
        axis = ("c" + order + "z")[phase]
        skip = sum(place.size(before) - 1 for before in ("c" + order + "z")[:phase])
        sums = self.buffer(number, 0)
        copies = []
        for step, other in enumerate(place.others(axis)):
            if phase == 0:
                source, target = self.half(number, other), sums
            elif phase == 3:
                source, target = sums.at[other, at["y"], at["x"]], self.buffer(number, 3).at[at["z"]]
            else:
                target = self.buffer(number, phase).at[step]
                y, x = (other, EVERY) if axis == "y" else (EVERY, other)
                if phase == 2:
                    y, x = (other, at["x"]) if axis == "y" else (at["y"], other)
                source = sums.at[:, y, x]
            slot = base + skip + step
            copies.append(
                pltpu.make_async_remote_copy(
                    source,
                    target,
                    self.send_sem.at[slot],
                    self.recv_sem.at[slot],
                    device_id=place.device(**{axis: other}),
                    device_id_type=MESH,
                )
            )
        return copies

    def absorb(self, number, phase):
        source, first, columns, order = self.pieces[number]
        at = self.place.at
        deep = self.place.sizes[0]
        sums = self.buffer(number, 0)
        if phase == 3:
            slots = self.buffer(number, 3)
            slots[at["z"]] = sums[at["z"], at["y"], at["x"]]
            total = slots[0].astype(F32)
            for slot in range(1, deep):
                total += slots[slot].astype(F32)
            self.outs[source][:, first : first + columns] = total
            return

        @pl.loop(0, deep)
        def _(z):
            if phase == 0:
                own = self.sources[source].at[z, :, :, at["c"], :, pl.ds(first, columns)] if self.kept[source] else self.buffer(number, 4).at[z]
                view, parts = sums.at[z], [own[...]]
            else:
                came = self.buffer(number, phase)
                parts = [came[step, z] for step in range(came.shape[0])]
                if phase == 1:
                    view = sums.at[z, :, at["x"]] if order[0] == "x" else sums.at[z, at["y"]]
                else:
                    view = sums.at[z, at["y"], at["x"]]
            total = view[...].astype(F32)
            for part in parts:
                total += part.astype(F32)
            view[...] = total.astype(view.dtype)

    def advance(self, numbers, phase):
        for number in numbers:
            if phase > 0:
                for copy in self.phase(number, phase - 1):
                    copy.wait()
                if phase == 1 and not self.kept[self.pieces[number][0]]:
                    self.load(number).wait()
                self.absorb(number, phase - 1)
            elif not self.kept[self.pieces[number][0]]:
                self.load(number).start()
            if phase < self.PHASES:
                for copy in self.phase(number, phase):
                    copy.start()


class Band:
    def __init__(self, length, reach):
        self.reach = reach
        self.causal = length + reach
        self.two_way = 2 * reach
        self.width = self.causal + self.two_way
        self.query_zero = length - SUB
        self.query_zero_two = reach - SUB
        self.key_zero = reach - SUB

    def distances(self, rows):
        causal = lax.broadcasted_iota(jnp.int32, (1, self.causal), 1)
        two_way = lax.broadcasted_iota(jnp.int32, (1, self.two_way), 1)
        if rows == "queries":
            causal, two_way = self.query_zero - causal, self.query_zero_two - two_way
            return (
                jnp.where(causal <= -self.reach, causal + self.causal, causal),
                jnp.where(two_way <= -self.reach, two_way + self.two_way, two_way),
            )
        causal, two_way = causal - self.key_zero, two_way - self.key_zero
        return (
            jnp.where(causal >= self.causal - self.reach, causal - self.causal, causal),
            jnp.where(two_way >= self.reach, two_way - self.two_way, two_way),
        )


def one_hot(map_ref, band, rows):
    bucket = lax.broadcasted_iota(jnp.int32, (NB, 1), 0)

    def edges(row, number):
        entries = map_ref[row : row + 1, :]
        below = jnp.sum((entries < number).astype(jnp.int32), axis=1, keepdims=True)
        return below, below + jnp.sum((entries == number).astype(jnp.int32), axis=1, keepdims=True)

    causal, two_way = band.distances(rows)
    low, high = edges(0, bucket)
    one = (causal >= low) & (causal < high)
    ahead = bucket >= NB // 2
    low, high = edges(1, jnp.where(ahead, bucket - NB // 2, bucket))
    apart = jnp.abs(two_way)
    two = (apart >= low) & (apart < high) & ((two_way < 0) == ahead)
    return jnp.concatenate([jnp.where(one, 1.0, 0.0), jnp.where(two, 1.0, 0.0)], axis=1), causal


def spread(row, width):
    return pltpu.roll(jnp.broadcast_to(row, (SUB, width)), 0, 1, stride=1, stride_axis=0)


def fold(band):
    width = band.shape[1]
    half = SUB // 2
    while half >= 8:
        band = band[:half] + pltpu.roll(band[half:], width - half, 1)
        half //= 2
    row = lax.broadcasted_iota(jnp.int32, band.shape, 0)
    for bit in (4, 2, 1):
        band = jnp.where((row & bit) != 0, pltpu.roll(band, width - bit, 1), band)
    return jnp.sum(band, axis=0, keepdims=True)


def fill_bands(head, bias_ref, band, causal_ref, two_ref):
    row = bias_ref[pl.ds(head, 1), :]
    causal_ref[...] = spread(row[:, : band.causal], band.causal)
    two_ref[...] = spread(row[:, band.causal :], band.two_way)


def bias_rows(table_ref, map_ref, band, rows):
    hot, causal = one_hot(map_ref, band, rows)
    bias = dot(table_ref[...], hot.astype(BF16), 0, 0)
    return jnp.concatenate([jnp.where(causal < 0, NEG, bias[:, : band.causal]), bias[:, band.causal :]], axis=1)


def head_cols(head):
    group = head // 2
    return pl.ds(pl.multiple_of(group * PAIR, PAIR), PAIR), head % 2


def pick_lanes(half):
    return lax.broadcasted_iota(jnp.int32, (1, PAIR), 1) // DH == half


def soft_rows(scores):
    high = jnp.max(scores, axis=-1, keepdims=True)
    weights = jnp.exp(scores - high)
    total = jnp.sum(weights, axis=-1, keepdims=True)
    return weights.astype(BF16), total, high + jnp.log(total)


def store_head(mixed_ref, lse_ref, rows, cols, head, half, out, total, lse):
    pick = pick_lanes(half)
    mixed_ref[rows, cols] = jnp.where(pick, (out / total).astype(BF16), mixed_ref[rows, cols])
    lane = lax.broadcasted_iota(jnp.int32, (1, lse_ref.shape[1]), 1)
    lse_ref[rows, :] = jnp.where(lane == head, lse, lse_ref[rows, :])


def self_forward_head(head, limit, q_ref, k_ref, v_ref, causal_ref, two_ref, band, mixed_ref, lse_ref):
    length = q_ref.shape[0]
    cols, half = head_cols(head)
    pick = pick_lanes(half)
    block = 256
    for start in range(0, length, block):
        keys = max(start + block, band.reach)
        rows = pl.ds(start, block)
        query = jnp.where(pick, q_ref[rows, cols], 0)
        scores = dot(query, k_ref[pl.ds(0, keys), cols], 1, 1)
        parts = []
        for first in range(start, start + block, SUB):
            at = band.query_zero - first
            bias = causal_ref[:, at : at + keys]
            if start < band.reach:
                at = band.query_zero_two - first
                two = two_ref[:, at : at + keys]
                inside = (first + lax.broadcasted_iota(jnp.int32, (SUB, keys), 0) < limit) & (
                    lax.broadcasted_iota(jnp.int32, (SUB, keys), 1) < limit
                )
                bias = jnp.where(inside, two, bias)
            parts.append(bias)
        weights, total, lse = soft_rows(scores + jnp.concatenate(parts, axis=0))
        out = dot(weights, v_ref[pl.ds(0, keys), cols])
        store_head(mixed_ref, lse_ref, rows, cols, head, half, out, total, lse)


def cross_forward_head(head, q_ref, k_ref, v_ref, mixed_ref, lse_ref):
    length = q_ref.shape[0]
    cols, half = head_cols(head)
    pick = pick_lanes(half)
    block = 256
    for start in range(0, length, block):
        rows = pl.ds(start, block)
        query = jnp.where(pick, q_ref[rows, cols], 0)
        weights, total, lse = soft_rows(dot(query, k_ref[:, cols], 1, 1))
        out = dot(weights, v_ref[:, cols])
        store_head(mixed_ref, lse_ref, rows, cols, head, half, out, total, lse)


def row_blocks(count, block, step):
    @pl.loop(0, count // block)
    def _(index):
        step(pl.ds(pl.multiple_of(index * block, block), block))


def gain_rows(gathered, width):
    devices = gathered.shape[0]
    share = width // devices
    lane = lax.broadcasted_iota(jnp.int32, (SUB, width), 1)
    select = jnp.where(lax.rem(lane, share) == lax.broadcasted_iota(jnp.int32, (SUB, width), 0), 1.0, 0.0)
    first = share * lax.broadcasted_iota(jnp.int32, (devices, width), 0)
    lane = lax.broadcasted_iota(jnp.int32, (devices, width), 1)
    own = (lane >= first) & (lane < first + share)
    rows = []
    for number in range(8):
        spread_out = exact_dot(gathered[:, number, :], select)
        rows.append(jnp.sum(jnp.where(own, spread_out, 0.0), axis=0, keepdims=True))
    return jnp.concatenate(rows, axis=0)


ATTENTION = 8
SHARDS = 14


def gather_pieces(rows, down_rows):
    head, tail = rows // 3 // 8 * 8, rows - rows // 3 // 8 * 8
    half = down_rows // 2
    table = {
        "qk": [(0, 0, rows, "zxy"), (1, 0, rows, "zyx"), (13, 0, 8, "zxy")],
        "v": [(2, 0, head, "xzy"), (2, head, tail, "yzx")],
        "out": [(3, 0, rows, "zxy"), (4, 0, rows, "zyx"), (7, 0, tail, "zxy"), (7, tail, head, "zyx")],
        "memory": [(5, 0, rows, "xzy"), (6, 0, rows, "yzx")],
        "gate": [(8, 0, rows, "zxy"), (9, 0, rows, "zyx")],
        "down": [(10, 0, half, "xzy"), (10, half, half, "yzx")],
        "upper": [(11, 0, rows, "zxy"), (12, 0, rows, "zyx")],
    }
    pieces, groups = [], {}
    for name, group in table.items():
        groups[name] = range(len(pieces), len(pieces) + len(group))
        pieces += group
    return pieces, groups


FORWARD_OUTS = 13


def forward_kernel(
    limit_ref, tokens_ref, memory_ref, table_ref, map_ref, gain1_ref, gain2_ref, gain3_ref, *refs, band, heads, plan,
):
    count = ATTENTION + 3 if plan else ATTENTION
    shards, refs = refs[:count], refs[count:]
    if plan:
        gathered, refs = refs[:SHARDS], refs[SHARDS:]
    else:
        gathered = shards
    moves = Moves((), refs[:FORWARD_OUTS], refs[FORWARD_OUTS:])
    (
        gains_ref, q1_ref, k1_ref, v1_ref, mixed1_ref, lse1_ref, first_ref,
        q2_ref, k2_ref, v2_ref, mixed2_ref, lse2_ref, second_ref,
    ) = moves.held_outs
    bias_ref, causal_ref, two_ref, weights_ref, share_ref, tile_ref, load_sem, *gather_sems = moves.rest
    length, width = tokens_ref.shape
    if plan:
        sizes, pieces, groups = plan
        place = Place(sizes)
        columns = gathered[8].shape[-1]
        halves = [[ref.at[:, start : start + columns] for ref in shards[8:10]] for start in (0, columns)]
        parts = (*shards[:8], *halves[0], shards[10], *halves[1], share_ref)
        gather = Gather(place, pieces, parts, gathered, *gather_sems)

    def advance(*steps):
        if plan:
            for numbers, phase in steps:
                gather.advance(groups[numbers], phase)

    def load(number):
        return pltpu.make_async_copy(gathered[number].reshape(width, width), weights_ref.at[number], load_sem.at[number])

    def load_tile():
        return pltpu.make_async_copy(gathered[SHARDS - 1].reshape(tile_ref.shape), tile_ref, load_sem.at[ATTENTION])

    gain_refs = (gain1_ref, gain2_ref, gain3_ref)
    if plan:
        share_ref[...] = jnp.zeros_like(share_ref)
        for number, gain_ref in enumerate(gain_refs):
            share_ref[number : number + 1, : gain_ref.shape[1]] = gain_ref[...].astype(F32)
        place.greet()
    bias_ref[...] = bias_rows(table_ref, map_ref, band, "queries")
    lse1_ref[...] = jnp.zeros_like(lse1_ref)
    lse2_ref[...] = jnp.zeros_like(lse2_ref)
    mixed1_ref[...] = jnp.zeros_like(mixed1_ref)
    mixed2_ref[...] = jnp.zeros_like(mixed2_ref)
    if plan:
        place.meet()
    advance(("qk", 0), ("v", 0), ("memory", 0))
    advance(("v", 1), ("qk", 1), ("qk", 2), ("v", 2), ("out", 0))
    advance(("qk", 3), ("v", 3), ("qk", 4), ("v", 4), ("memory", 1), ("out", 1), ("gate", 0), ("down", 0), ("upper", 0))
    for number in range(3):
        load(number).start()
    if plan:
        load_tile().start()
        load_tile().wait()
        gains_ref[...] = gain_rows(tile_ref[...], width)
    else:
        gains_ref[...] = jnp.zeros_like(gains_ref)
        for number, gain_ref in enumerate(gain_refs):
            gains_ref[number : number + 1, :] = gain_ref[...].astype(F32)
    for number in range(3):
        load(number).wait()

    def project_self(rows):
        value = tokens_ref[rows, :].astype(F32)
        normed = (value * rms(value) * gains_ref[0:1, :]).astype(BF16)
        q1_ref[rows, :] = dot(normed, weights_ref[0]).astype(BF16)
        k1_ref[rows, :] = dot(normed, weights_ref[1]).astype(BF16)
        v1_ref[rows, :] = dot(normed, weights_ref[2]).astype(BF16)

    for start in range(0, length, length // 2):
        project_self(pl.ds(start, length // 2))
        if start == 0:
            advance(("out", 2))
    moves.store(0, 1, 2, 3)

    @pl.loop(0, heads)
    def _(head):
        fill_bands(head, bias_ref, band, causal_ref, two_ref)
        self_forward_head(head, limit_ref[0], q1_ref, k1_ref, v1_ref, causal_ref, two_ref, band, mixed1_ref, lse1_ref)

        for when, steps in (
            (1, (("out", 3), ("memory", 2))),
            (4, (("out", 4), ("down", 1))),
            (6, (("memory", 3),)),
            (8, (("memory", 4), ("gate", 1))),
        ):

            @pl.when(head == when * heads // 12)
            def _(when=when, steps=steps):
                advance(*steps)
                for number in {4: (3, 4, 7), 8: (5, 6)}.get(when, ()):
                    load(number).start()

    advance(("gate", 2))
    moves.store(4, 5)
    for number in range(3, ATTENTION):
        load(number).wait()

    def project_memory(rows):
        k2_ref[rows, :] = dot(memory_ref[rows, :], weights_ref[5]).astype(BF16)
        v2_ref[rows, :] = dot(memory_ref[rows, :], weights_ref[6]).astype(BF16)

    row_blocks(memory_ref.shape[0], 512, project_memory)

    def project_cross(rows):
        value = tokens_ref[rows, :].astype(F32) + dot(mixed1_ref[rows, :], weights_ref[3])
        first_ref[rows, :] = value
        normed = (value * rms(value) * gains_ref[1:2, :]).astype(BF16)
        q2_ref[rows, :] = dot(normed, weights_ref[4]).astype(BF16)

    row_blocks(length, 512, project_cross)
    moves.store(6, 7, 8, 9)

    @pl.loop(0, heads)
    def _(head):
        cross_forward_head(head, q2_ref, k2_ref, v2_ref, mixed2_ref, lse2_ref)

        @pl.when(head == heads // 4)
        def _():
            advance(("down", 2))

        @pl.when(head == heads * 2 // 3)
        def _():
            advance(("gate", 3))

    advance(("down", 3))
    moves.store(10, 11)

    def project_second(rows):
        second_ref[rows, :] = first_ref[rows, :] + dot(mixed2_ref[rows, :], weights_ref[7])

    row_blocks(length, 512, project_second)
    moves.store(12)
    advance(("gate", 4), ("down", 4))
    if plan:
        gather.settle(groups["upper"])
    moves.finish()


def norm_back_rows(value, gain, grad):
    scale = rms(value)
    unit = value * scale
    scaled = grad * gain
    return scale * (scaled - unit * jnp.mean(scaled * unit, axis=-1, keepdims=True))


GELU_A = 0.7978845608028654
GELU_B = 0.044715


def feed_rows(
    rows, gate_ref, up_ref, down_ref, gout_ref, normed_ref, out_ref, back_ref, hidden_ref, ggate_ref, gup_ref
):
    normed = normed_ref[rows, :]
    gate = dot(normed, gate_ref[...])
    upward = dot(normed, up_ref[...])
    square = gate * gate
    bend = jnp.tanh(GELU_A * gate * (1.0 + GELU_B * square))
    half = 0.5 * (1.0 + bend)
    active = gate * half
    hidden = (active * upward).astype(BF16)
    hidden_ref[rows, :] = hidden
    out_ref[rows, :] += dot(hidden, down_ref[...])
    ghidden = dot(gout_ref[rows, :], down_ref[...], 1, 1)
    slope = half + 0.5 * gate * (1.0 - bend * bend) * (GELU_A * (1.0 + 3.0 * GELU_B * square))
    ggate = (ghidden * upward * slope).astype(BF16)
    gup = (ghidden * active).astype(BF16)
    ggate_ref[rows, :] = ggate
    gup_ref[rows, :] = gup
    back_ref[rows, :] += dot(ggate, gate_ref[...], 1, 1) + dot(gup, up_ref[...], 1, 1)


def feed_kernel(
    second_ref, gout_ref, gains_ref, gate_ref, up_ref, down_ref,
    output_ref, gsecond_ref, dgate_ref, dup_ref, ddown_ref,
    normed_ref, flipped_ref, out_ref, back_ref, hidden_ref, ggate_ref, gup_ref,
):
    step = pl.program_id(0)
    length = second_ref.shape[0]
    block = 256

    @pl.when(step == 0)
    def _():
        def prepare(rows):
            value = second_ref[rows, :]
            normed = (value * rms(value) * gains_ref[2:3, :]).astype(BF16)
            normed_ref[rows, :] = normed
            flipped_ref[:, rows] = normed.T
            out_ref[rows, :] = value
            back_ref[rows, :] = jnp.zeros_like(value)

        row_blocks(length, block, prepare)

    def rows_step(rows):
        feed_rows(
            rows, gate_ref, up_ref, down_ref, gout_ref, normed_ref, out_ref, back_ref, hidden_ref, ggate_ref, gup_ref
        )

    row_blocks(length, 512, rows_step)
    ddown_ref[...] = dot(hidden_ref[...].T, gout_ref[...]).astype(BF16)
    dgate_ref[...] = dot(flipped_ref[...], ggate_ref[...]).astype(BF16)
    dup_ref[...] = dot(flipped_ref[...], gup_ref[...]).astype(BF16)

    @pl.when(step == pl.num_programs(0) - 1)
    def _():
        def finish(rows):
            output_ref[rows, :] = out_ref[rows, :].astype(BF16)
            back = norm_back_rows(second_ref[rows, :], gains_ref[2:3, :], back_ref[rows, :])
            gsecond_ref[rows, :] = back + gout_ref[rows, :].astype(F32)

        row_blocks(length, block, finish)


FEED_INS, FEED_OUTS = 6, 3


def feed_exchange_kernel(*refs, plan):
    ins, refs = refs[:FEED_INS], refs[FEED_INS + 2 :]
    results, refs = refs[:FEED_OUTS], refs[FEED_OUTS:]
    shares, outs, gathered, refs = refs[:2], refs[2:4], refs[4:6], refs[6:]
    moves = Moves(ins, results, refs)
    second_ref, gout_ref, gains_ref, gate_low_ref, up_low_ref, down_ref = moves.held_ins
    output_ref, gsecond_ref, ddown_ref = moves.held_outs
    (
        normed_ref, flipped_ref, out_ref, back_ref, hidden_ref, ggate_ref, gup_ref, gate_ref, up_ref,
        dgate_ref, dup_ref, load_sem, share_sem, *refs,
    ) = moves.rest
    sizes, gather_plan, scatter_plan = plan
    place = Place(sizes)
    gather = Gather(place, gather_plan, (), gathered, *refs[:3])
    lower = [dgate_ref.at[0], dup_ref.at[0]]
    scatter = Scatter(place, scatter_plan, lower, [True, True], outs, refs[3:-3], *refs[-3:])
    upper, every = range(len(gather_plan)), range(len(scatter_plan))
    length, width = second_ref.shape
    columns = gate_low_ref.shape[1]
    block = 256

    def load(number):
        target = (gate_ref, up_ref)[number].at[1]
        return pltpu.make_async_copy(gathered[number].reshape(width, columns), target, load_sem.at[number])

    def low(number):
        target = (gate_ref, up_ref)[number].at[0]
        return pltpu.make_async_copy((ins[3], ins[4])[number], target, load_sem.at[2 + number])

    place.greet()
    moves.load(0, 2, 1)
    for number in (0, 1):
        low(number).start()
    moves.load(5)
    place.meet()
    gather.resume(upper)
    moves.need(0, 2)

    def prepare(rows):
        value = second_ref[rows, :]
        normed = (value * rms(value) * gains_ref[2:3, :]).astype(BF16)
        normed_ref[rows, :] = normed
        flipped_ref[:, rows] = normed.T
        out_ref[rows, :] = value
        back_ref[rows, :] = jnp.zeros_like(value)

    row_blocks(length, block, prepare)
    moves.need(1, 5)
    for number in (0, 1):
        low(number).wait()

    @pl.loop(0, 2)
    def _(half):
        units = pl.ds(pl.multiple_of(half * columns, columns), columns)
        gate, up, down = gate_ref.at[half], up_ref.at[half], down_ref.at[units]

        @pl.loop(0, 2)
        def _(index):
            rows = pl.ds(pl.multiple_of(index * (length // 2), length // 2), length // 2)
            feed_rows(rows, gate, up, down, gout_ref, normed_ref, out_ref, back_ref, hidden_ref, ggate_ref, gup_ref)

            @pl.when((half == 0) & (index == 0))
            def _():
                gather.advance(upper, 2)

            @pl.when((half == 1) & (index == 0))
            def _():
                scatter.advance(every, 2)

            @pl.when((half == 1) & (index == 1))
            def _():
                scatter.advance(every, 3)

        rows_each = width // place.sizes[0]

        @pl.loop(0, place.sizes[0])
        def _(index):
            start = pl.multiple_of(index * rows_each, 64)
            flipped = flipped_ref[pl.ds(start, rows_each), :]
            for target, grad in ((dgate_ref, ggate_ref), (dup_ref, gup_ref)):
                store_shares(target.at[half], EVERY, dot(flipped, grad[...]), start)

        @pl.when(half == 0)
        def _():
            scatter.advance(every, 0)
            gather.advance(upper, 3)

        ddown_ref[units, :] = dot(hidden_ref[...].T, gout_ref[...]).astype(BF16)

        @pl.when(half == 0)
        def _():
            gather.advance(upper, 4)
            for number in upper:
                load(number).start()
            scatter.advance(every, 1)
            for number in upper:
                load(number).wait()

    share = [pltpu.make_async_copy(ref.at[1], shares[i], share_sem.at[i]) for i, ref in enumerate((dgate_ref, dup_ref))]
    for copy in share:
        copy.start()
    moves.store(2)

    def finish(rows):
        output_ref[rows, :] = out_ref[rows, :].astype(BF16)
        back = norm_back_rows(second_ref[rows, :], gains_ref[2:3, :], back_ref[rows, :])
        gsecond_ref[rows, :] = back + gout_ref[rows, :].astype(F32)

    row_blocks(length, block, finish)
    moves.store(0, 1)
    scatter.advance(every, 4)
    for copy in share:
        copy.wait()
    moves.finish()


def backward_head_prepare(group_cols, gm_ref, mixed_ref, delta_ref):
    product = (gm_ref[:, group_cols].astype(F32) * mixed_ref[:, group_cols].astype(F32)).T
    delta_ref[0:1, :] = jnp.sum(product[:DH], axis=0, keepdims=True)
    delta_ref[1:2, :] = jnp.sum(product[DH:], axis=0, keepdims=True)


def backward_block(key_rows, cols, half, start, bias, q_ref, k_ref, v_ref, gm_ref, lse, delta, gk_ref, gv_ref, gqt_ref):
    length = q_ref.shape[0]
    pick = pick_lanes(half)
    queries = pl.ds(start, length - start)
    query = jnp.where(pick, q_ref[queries, cols], 0)
    grad = jnp.where(pick, gm_ref[queries, cols], 0)
    keys = k_ref[key_rows, cols]
    scores = dot(keys, query, 1, 1)
    if bias is not None:
        scores = scores + bias
    probs = jnp.exp(scores - lse[:, start:])
    gv = dot(probs.astype(BF16), grad)
    gprobs = dot(v_ref[key_rows, cols], grad, 1, 1)
    gscores = probs * (gprobs - delta[:, start:])
    low = gscores.astype(BF16)
    gk = dot(low, query)
    gk_ref[key_rows, cols] = jnp.where(pick, gk.astype(BF16), gk_ref[key_rows, cols])
    gv_ref[key_rows, cols] = jnp.where(pick, gv.astype(BF16), gv_ref[key_rows, cols])
    gqt_ref[:, queries] += dot(jnp.where(pick, keys, 0).T, low)
    return gscores


def self_backward_head(
    head, limit, q_ref, k_ref, v_ref, gm_ref, mixed_ref, lse_ref, delta_ref, causal_ref, two_ref, band,
    gk_ref, gv_ref, gqt_ref, causal_sum_ref, two_sum_ref,
):
    length = q_ref.shape[0]
    cols, half = head_cols(head)
    lse = lse_ref[pl.ds(head, 1), :]
    delta = delta_ref[pl.ds(half, 1), :]
    reach = band.reach
    block = 256
    for first in range(0, length, block):
        start = 0 if first < reach else first
        count = length - start
        parts = []
        for key in range(first, first + block, SUB):
            at = band.key_zero - key + start
            bias = causal_ref[:, at : at + count]
            if first < reach:
                at = band.key_zero - key
                two = two_ref[:, at : at + reach]
                inside = (key + lax.broadcasted_iota(jnp.int32, (SUB, reach), 0) < limit) & (
                    lax.broadcasted_iota(jnp.int32, (SUB, reach), 1) < limit
                )
                bias = jnp.concatenate([jnp.where(inside, two, bias[:, :reach]), bias[:, reach:]], axis=1)
            parts.append(bias)
        gscores = backward_block(
            pl.ds(first, block), cols, half, start, jnp.concatenate(parts, axis=0),
            q_ref, k_ref, v_ref, gm_ref, lse, delta, gk_ref, gv_ref, gqt_ref,
        )
        for key in range(first, first + block, SUB):
            part = gscores[key - first : key - first + SUB]
            at = band.key_zero - key + start
            if first < reach:
                inside = (key + lax.broadcasted_iota(jnp.int32, (SUB, reach), 0) < limit) & (
                    lax.broadcasted_iota(jnp.int32, (SUB, reach), 1) < limit
                )
                head_part = part[:, :reach]
                at_two = band.key_zero - key
                two_sum_ref[:, at_two : at_two + reach] += jnp.where(inside, head_part, 0.0)
                causal_sum_ref[:, at : at + reach] += jnp.where(inside, 0.0, head_part)
                causal_sum_ref[:, at + reach : at + count] += part[:, reach:]
            else:
                causal_sum_ref[:, at : at + count] += part


def split_columns(number, columns):
    half = columns // 2
    return [(number, 0, half, "xy"), (number, half, half, "yx")]


CROSS_INS, CROSS_OUTS = 15, 8


def cross_backward_kernel(*refs, heads, plan):
    count = 3 if plan else 0
    ins, refs = refs[:CROSS_INS], refs[CROSS_INS:]
    sources, refs = refs[:count], refs[count:]
    results, refs = refs[:CROSS_OUTS], refs[CROSS_OUTS:]
    outs, refs = refs[:count], refs[count:]
    moves = Moves(ins, results, refs)
    (
        gsecond_ref, first_ref, memory_ref, gains_ref, q_ref, k_ref, v_ref, mixed1_ref, mixed2_ref, lse_ref,
        wo_ref, cq_ref, ck_ref, cv_ref, co_ref,
    ) = moves.held_ins
    gmem_ref, gfirst_ref, gm1_ref, dwo_ref, dcq_ref, dck_ref, dcv_ref, dco_ref = moves.held_outs
    gm_ref, branch_ref, flipped_ref, lse_rows_ref, delta_ref, gq_ref, gk_ref, gv_ref, gqt_ref, *refs = moves.rest
    if plan:
        sizes, pieces = plan
        scatter = Scatter(Place(sizes), pieces, sources, [False] * count, outs, refs[:-3], *refs[-3:])
        soon, later = range(len(pieces) // 2), range(len(pieces) // 2, len(pieces))
        scatter.place.greet()
    moves.load(0, 14, 8, 4, 5, 6, 9, 2, 12, 13, 1, 3, 11, 10, 7)
    if plan:
        scatter.place.meet()
        scatter.advance(soon, 0)
        scatter.advance(later, 0)
    length, width = first_ref.shape
    source = memory_ref.shape[0]
    block = 256

    def prepare(rows):
        branch = gsecond_ref[rows, :].astype(BF16)
        branch_ref[rows, :] = branch
        gm_ref[rows, :] = dot(branch, co_ref[...], 1, 1).astype(BF16)
        flipped_ref[:, rows] = mixed2_ref[rows, :].T

    moves.need(0, 14, 8)
    row_blocks(length, 512, prepare)

    def out_grad(rows):
        dco_ref[rows, :] = dot(flipped_ref[rows, :], branch_ref[...]).astype(BF16)

    row_blocks(width, 384, out_grad)
    moves.store(7)
    moves.need(4, 5, 6, 9)
    if plan:
        scatter.advance(soon, 1)
    lse_rows_ref[...] = lse_ref[...].T
    gk_ref[...] = jnp.zeros_like(gk_ref)
    gv_ref[...] = jnp.zeros_like(gv_ref)
    groups = heads // 2

    @pl.loop(0, groups)
    def _(group):
        if plan:

            @pl.when(group == groups // 3)
            def _():
                scatter.advance(soon, 2)
                scatter.advance(later, 1)

            @pl.when(group == groups - 2)
            def _():
                scatter.advance(soon, 3)

        cols = pl.ds(pl.multiple_of(group * PAIR, PAIR), PAIR)
        backward_head_prepare(cols, gm_ref, mixed2_ref, delta_ref)
        gqt_ref[...] = jnp.zeros_like(gqt_ref)

        @pl.loop(0, 2)
        def _(half):
            head = group * 2 + half
            for first in range(0, source, block):
                backward_block(
                    pl.ds(first, block), cols, half, 0, None, q_ref, k_ref, v_ref, gm_ref,
                    lse_rows_ref[pl.ds(head, 1), :], delta_ref[pl.ds(half, 1), :], gk_ref, gv_ref, gqt_ref,
                )

        gq_ref[:, cols] = gqt_ref[...].T.astype(BF16)

    if plan:
        scatter.advance(later, 2)

    def memory_grad(rows):
        gmem_ref[rows, :] = dot(gk_ref[rows, :], ck_ref[...], 1, 1) + dot(gv_ref[rows, :], cv_ref[...], 1, 1)
        flipped_ref[:, rows] = memory_ref[rows, :].T

    moves.need(2, 12, 13)
    row_blocks(source, 512, memory_grad)
    moves.store(0)

    def memory_weights(rows):
        flipped = flipped_ref[rows, :source]
        dck_ref[rows, :] = dot(flipped, gk_ref[...]).astype(BF16)
        dcv_ref[rows, :] = dot(flipped, gv_ref[...]).astype(BF16)

    row_blocks(width, 384, memory_weights)
    moves.store(5, 6)
    moves.need(1, 3, 11, 10, 7)
    if plan:
        scatter.advance(later, 3)
        scatter.advance(soon, 4)

    def first_grad(rows):
        value = first_ref[rows, :]
        flipped_ref[:, rows] = (value * rms(value) * gains_ref[1:2, :]).astype(BF16).T
        back = norm_back_rows(value, gains_ref[1:2, :], dot(gq_ref[rows, :], cq_ref[...], 1, 1))
        gfirst = back + gsecond_ref[rows, :]
        gfirst_ref[rows, :] = gfirst
        branch = gfirst.astype(BF16)
        branch_ref[rows, :] = branch
        gm1_ref[rows, :] = dot(branch, wo_ref[...], 1, 1).astype(BF16)

    row_blocks(length, 512, first_grad)
    moves.store(1, 2)

    def query_weights(rows):
        dcq_ref[rows, :] = dot(flipped_ref[rows, :], gq_ref[...]).astype(BF16)

    row_blocks(width, 384, query_weights)
    moves.store(4)

    def flip_mixed(rows):
        flipped_ref[:, rows] = mixed1_ref[rows, :].T

    row_blocks(length, block, flip_mixed)

    def out_weights(rows):
        dwo_ref[rows, :] = dot(flipped_ref[rows, :], branch_ref[...]).astype(BF16)

    row_blocks(width, 384, out_weights)
    moves.store(3)
    if plan:
        scatter.advance(later, 4)
    moves.finish()


def store_shares(ref, cols, value, start):
    if len(ref.shape) == 2:
        ref[pl.ds(start, value.shape[0]), cols] = value.astype(BF16)
    else:
        deep, high, wide, cores, rows, columns = ref.shape
        chunk = high * wide * cores * rows
        ref[lax.div(start, chunk), :, :, :, :, cols] = value.reshape(high, wide, cores, rows, value.shape[1]).astype(BF16)


TILE = 16


def fill_tiles(tiles_ref, gtable):
    deep, high, wide, cores, rows, lanes = tiles_ref.shape
    heads, buckets = gtable.shape
    tiles_ref[...] = jnp.zeros_like(tiles_ref)

    @pl.loop(0, deep)
    def _(z):
        shape = (high, wide, cores, heads, buckets)
        tiles_ref[z, :, :, :, :heads, :buckets] = jnp.broadcast_to(gtable, shape)


REST = 5


def self_parts(columns):
    half, third = columns // 2, columns // 3
    return (0, half), (half, third), (half + third, columns - half - third)


def self_pieces(columns):
    first = [(0, 0, columns, "xy"), (1, 0, columns, "yx")]
    rest = [(2, 0, columns, "xy"), (3, 0, columns, "yx")] + split_columns(4, columns)
    parts = []
    for number, (start, count) in enumerate(self_parts(columns)):
        orders = ("xy", "yx", "xy") if number % 2 else ("yx", "xy", "yx")
        parts.append([(REST + array, start, count, orders[array]) for array in range(3)])
    pieces, groups = [], []
    for group in (first, rest, *parts, [(REST + 3, 0, SUB, "xy")]):
        groups.append(range(len(pieces), len(pieces) + len(group)))
        pieces += group
    return pieces, groups


SELF_INS = 12


def self_backward_kernel(limit_ref, table_ref, map_ref, *refs, band, heads, plan):
    count = REST if plan else 0
    ins, refs = refs[:SELF_INS], refs[SELF_INS:]
    sources, refs = refs[:count], refs[count:]
    gtokens_ref, refs = refs[0], refs[1:]
    if plan:
        outs, refs = refs[: REST + 3], refs[REST + 3 :]
        gtable_ref, refs = refs[0], refs[1:]
    else:
        gtable_ref, dwq_ref, dwk_ref, dwv_ref, *refs = refs
    moves = Moves(ins, (), refs)
    (
        tokens_ref, gains_ref, lse_ref, q_ref, k_ref, v_ref, mixed_ref, gm_ref, gfirst_ref, wq_ref, wk_ref, wv_ref,
    ) = moves.held_ins
    refs = moves.rest
    (
        bias_ref, causal_ref, two_ref, flipped_ref, lse_rows_ref, delta_ref, gq_ref, gk_ref, gv_ref, gqt_ref,
        causal_sum_ref, two_sum_ref, sums_ref, *refs,
    ) = refs
    length, width = tokens_ref.shape
    block = 256
    groups = heads // 2
    if plan:
        sizes, pieces, (first, rest, early, middle, late, table) = plan
        dwq_ref, dwk_ref, dwv_ref, tiles_ref, tile_ref, *refs = refs
        scatter = Scatter(
            Place(sizes), pieces, (*sources, dwq_ref, dwk_ref, dwv_ref, tiles_ref), [False] * REST + [True] * 4,
            (*outs, tile_ref), refs[:-3], *refs[-3:],
        )
        scatter.place.greet()
    moves.load(*range(SELF_INS))
    bias_ref[...] = bias_rows(table_ref, map_ref, band, "keys")
    if plan:
        scatter.place.meet()
        scatter.advance(first, 0)
        scatter.advance(rest, 0)
    moves.need(0, 1, 2)
    lse_rows_ref[...] = lse_ref[...].T
    gk_ref[...] = jnp.zeros_like(gk_ref)
    gv_ref[...] = jnp.zeros_like(gv_ref)
    sums_ref[...] = jnp.zeros_like(sums_ref)

    def flip_normed(rows):
        value = tokens_ref[rows, :].astype(F32)
        flipped_ref[:, rows] = (value * rms(value) * gains_ref[0:1, :]).astype(BF16).T

    row_blocks(length, block, flip_normed)
    moves.need(*range(3, SELF_INS))

    def group_step(group):
        cols = pl.ds(pl.multiple_of(group * PAIR, PAIR), PAIR)
        backward_head_prepare(cols, gm_ref, mixed_ref, delta_ref)
        gqt_ref[...] = jnp.zeros_like(gqt_ref)

        @pl.loop(0, 2)
        def _(half):
            head = group * 2 + half
            if plan:
                for when, numbers, phase in ((1, first, 1), (4, rest, 1), (5, first, 2), (8, first, 3), (9, early, 1), (11, rest, 2)):

                    @pl.when(head == when * heads // 12)
                    def _(numbers=numbers, phase=phase):
                        scatter.advance(numbers, phase)

            fill_bands(head, bias_ref, band, causal_ref, two_ref)
            causal_sum_ref[...] = jnp.zeros_like(causal_sum_ref)
            two_sum_ref[...] = jnp.zeros_like(two_sum_ref)
            self_backward_head(
                head, limit_ref[0], q_ref, k_ref, v_ref, gm_ref, mixed_ref, lse_rows_ref, delta_ref,
                causal_ref, two_ref, band, gk_ref, gv_ref, gqt_ref, causal_sum_ref, two_sum_ref,
            )
            sums_ref[pl.ds(head, 1), : band.causal] = fold(causal_sum_ref[...])
            sums_ref[pl.ds(head, 1), band.causal :] = fold(two_sum_ref[...])

        gq_ref[:, cols] = gqt_ref[...].T.astype(BF16)

    rows_each = width // (sizes["dp"] // (sizes["fsdp"] // 2)) if plan else block

    def weights(cols):
        @pl.loop(0, width // rows_each)
        def _(index):
            start = pl.multiple_of(index * rows_each, 64)
            flipped = flipped_ref[pl.ds(start, rows_each), :]
            for target, grad in ((dwq_ref, gq_ref), (dwk_ref, gk_ref), (dwv_ref, gv_ref)):
                store_shares(target, cols, dot(flipped, grad[:, cols]), start)

    parts = [pl.ds(start, count) for start, count in self_parts(width)]

    @pl.loop(0, groups)
    def _(group):
        if plan:

            @pl.when(group == groups // 2)
            def _():
                weights(parts[0])
                scatter.advance(early, 0)

            @pl.when(group == groups - 1)
            def _():
                weights(parts[1])
                scatter.advance(middle, 0)

        group_step(group)

    if plan:
        weights(parts[2])
        scatter.advance(late, 0)
        scatter.advance(early, 2)
        scatter.advance(rest, 3)
    else:
        for part in parts:
            weights(part)
    hot, unused = one_hot(map_ref, band, "keys")
    gtable = exact_dot(sums_ref[...], hot, 1, 1)
    if plan:
        fill_tiles(tiles_ref, gtable)
        scatter.advance(table, 0)
        scatter.advance(middle, 1)
        scatter.advance(late, 1)

    def tokens_grad(rows):
        value = tokens_ref[rows, :].astype(F32)
        grad = dot(gq_ref[rows, :], wq_ref[...], 1, 1)
        grad += dot(gk_ref[rows, :], wk_ref[...], 1, 1)
        grad += dot(gv_ref[rows, :], wv_ref[...], 1, 1)
        gtokens_ref[rows, :] = norm_back_rows(value, gains_ref[0:1, :], grad) + gfirst_ref[rows, :]

    if plan:
        steps = (
            ((table, 1), (early, 3), (first, 4)),
            ((middle, 2), (late, 2), (table, 2)),
            ((middle, 3), (rest, 4)),
            ((late, 3), (table, 3)),
        )

        @pl.loop(0, len(steps))
        def _(step):
            for start in range(0, length // len(steps), block):
                start = step * (length // len(steps)) + start
                tokens_grad(pl.ds(pl.multiple_of(start, block), block))
            for number, advances in enumerate(steps):

                @pl.when(step == number)
                def _(advances=advances):
                    for numbers, phase in advances:
                        scatter.advance(numbers, phase)

        scatter.advance(early, 4)
        scatter.advance(middle, 4)
        scatter.advance(late, 4)
        scatter.advance(table, 4)
        gtable_ref[...] = tile_ref[...].T[:NB, :heads]
    else:
        row_blocks(length, block, tokens_grad)
        gtable_ref[...] = gtable.T


def gain_grads(gains, weights, grads):
    results = []
    for gain, parts in zip(gains, ((0, 1, 2), (3,), (4, 5))):
        total = 0.0
        for part in parts:
            product = weights[part][...].astype(F32) * grads[part][...]
            total += exact_dot(jnp.ones((8, product.shape[1]), F32), product, 1, 1)
        results.append(total[0:1] / gain[...].astype(F32))
    return results


def hand_on_kernel(*refs, places, norms):
    count = len(places)
    shards, refs = refs[: len(norms) + 3], refs[len(norms) + 3 :]
    ins, (in_sem, out_sem) = refs[:count], refs[-2:]
    refs = refs[count:-2]
    held, outs, ggain_refs = refs[-count:], refs[: -count - 3], refs[-count - 3 : -count]
    loads = [pltpu.make_async_copy(ins[i], held[i], in_sem.at[i]) for i in range(count)]
    stores = []
    for i, (out, start) in enumerate(places):
        target = outs[out] if start is None else outs[out].at[:, start : start + ins[i].shape[1]]
        stores.append(pltpu.make_async_copy(held[i], target, out_sem.at[i]))
    for load in loads:
        load.start()
    for load, store in zip(loads, stores):
        load.wait()
        store.start()
    grads = []
    for number in norms:
        parts = [held[i][...] for i, (out, start) in enumerate(places) if out == number]
        grads.append(jnp.concatenate(parts, axis=1))
    for ref, value in zip(ggain_refs, gain_grads(shards[:3], shards[3:], grads)):
        ref[...] = value
    for store in stores:
        store.wait()


def hand_on(results, norms, gains, weights):
    arrays, places, shapes = [], [], []
    for number, result in enumerate(results):
        parts = result if isinstance(result, tuple) else (result,)
        start = 0
        for part in parts:
            arrays.append(part)
            places.append((number, start if len(parts) > 1 else None))
            start += part.shape[-1]
        shapes.append(jax.ShapeDtypeStruct(parts[0].shape[:-1] + (start,), parts[0].dtype))
    spec = pl.BlockSpec(memory_space=pl.ANY)
    here = pl.BlockSpec(memory_space=pltpu.VMEM)
    shards = [*[gain.reshape(1, -1) for gain in gains], *weights]
    *results, first, second, third = pl.pallas_call(
        functools.partial(hand_on_kernel, places=places, norms=norms),
        out_shape=shapes + [jax.ShapeDtypeStruct((1, gain.shape[0]), F32) for gain in gains],
        in_specs=[here] * len(shards) + [spec] * len(arrays),
        out_specs=[spec] * len(shapes) + [here] * 3,
        scratch_shapes=[pltpu.VMEM(a.shape, a.dtype) for a in arrays] + [pltpu.SemaphoreType.DMA((len(arrays),))] * 2,
        compiler_params=params(),
        name="hand_on",
    )(*shards, *arrays)
    return results, [ggain.reshape(-1) for ggain in (first, second, third)]


def upper_shapes(arrays):
    return [jax.ShapeDtypeStruct(a.shape, a.dtype) for a in arrays]


def vmem(*shapes):
    return [pltpu.VMEM(shape, dtype) for shape, dtype in shapes]


def params(**kw):
    return pltpu.CompilerParams(vmem_limit_bytes=60 * 1024 * 1024, **kw)


def per_device(
    inputs, encoded, out_grad, prefix, bucket_map, bias_table,
    norm_self, self_query, self_key, self_value, self_out,
    norm_cross, cross_query, cross_key, cross_value, cross_out,
    norm_feed, feed_gate, feed_up, feed_down,
):
    seqs, length, width = inputs.shape
    source = encoded.shape[1]
    heads = bias_table.shape[1]
    ff = feed_gate.shape[1]
    band = Band(length, length // 2)
    tokens = inputs.reshape(length, width)
    memory = encoded.reshape(source, width)
    gout = out_grad.reshape(length, width)
    gains_in = [norm_self, norm_cross, norm_feed]
    projections = [self_query, self_key, self_value, self_out, cross_query, cross_key, cross_value, cross_out]
    feeds = [feed_gate, feed_up, feed_down]
    sizes = dict(dp=lax.axis_size("dp"), fsdp=lax.axis_size("fsdp"))
    devices = sizes["dp"] * sizes["fsdp"]
    own = self_query.shape[0] % 8 == 0
    if own:
        pieces, groups = gather_pieces(self_query.shape[0], feed_down.shape[0])
        plan = (sizes, pieces, groups)
        copies = Gather.copies(sizes, pieces)
        shards = projections + feeds
    else:
        plan = None
        gains_in = [lax.all_gather(gain, AXES, axis=0, tiled=True) for gain in gains_in]
        shards = [lax.all_gather(shard, AXES, axis=0, tiled=True) for shard in projections]
        gate_full, up_full, down = [lax.all_gather(shard, AXES, axis=0, tiled=True) for shard in feeds]
    gains_in = [gain.reshape(1, -1) for gain in gains_in]

    remote = pl.BlockSpec(memory_space=pl.ANY)
    scalar = pl.BlockSpec(memory_space=pltpu.SMEM)

    def full(shape):
        return pl.BlockSpec(shape, lambda *_: (0,) * len(shape))

    def like(shape, dtype):
        return jax.ShapeDtypeStruct(shape, dtype)

    act = like((length, width), BF16)
    mem = like((source, width), BF16)
    act32 = like((length, width), F32)
    lse_shape = like((length, SUB), F32)
    gain_shape = like((8, width), F32)
    outs = [gain_shape, act, act, act, act, lse_shape, act32, act, mem, mem, act, lse_shape, act32]
    gathered_shapes = []
    if own:
        chips, cores = grid_of(sizes)[:3], grid_of(sizes)[3]
        shapes = [shard.shape for shard in projections]
        shapes += [(feed_gate.shape[0], ff // 2)] * 2 + [feed_down.shape] + [(feed_gate.shape[0], ff // 2)] * 2
        gathered_shapes = [like(chips + (cores * shape[0], shape[1]), BF16) for shape in shapes]
        gathered_shapes.append(like(chips + (cores * 8, SUB), F32))
    forward_in = (tokens, memory, bias_table, bucket_map, *gains_in)
    results = pl.pallas_call(
        functools.partial(forward_kernel, band=band, heads=heads, plan=plan),
        out_shape=gathered_shapes + outs,
        grid=(1,),
        in_specs=[scalar] + [full(a.shape) for a in forward_in]
        + ([full(a.shape) for a in shards] if own else [remote] * len(shards)),
        out_specs=[remote] * (len(gathered_shapes) + len(outs)),
        scratch_shapes=Moves.scratch(outs)
        + vmem(
            ((heads, band.width), F32), ((SUB, band.causal), F32), ((SUB, band.two_way), F32),
            ((ATTENTION, width, width), BF16), ((8, SUB), F32), ((devices, 8, SUB), F32),
        )
        + [pltpu.SemaphoreType.DMA((ATTENTION + 1,))]
        + ([pltpu.SemaphoreType.DMA((number,)) for number in (len(pieces), copies, copies)] if own else []),
        compiler_params=params(collective_id=0, has_side_effects=True) if own else params(),
        name="forward",
    )(prefix, *forward_in, *shards)
    attention = shards
    if own:
        gathered, results = results[:SHARDS], results[SHARDS:]
        attention = [part.reshape(width, width) for part in gathered[:ATTENTION]]
        gate_low, up_low = gathered[8].reshape(width, ff // 2), gathered[9].reshape(width, ff // 2)
        down = gathered[10].reshape(ff, width)
    gains, q1, k1, v1, mixed1, lse1, first, q2, k2, v2, mixed2, lse2, second = results

    grid = grid_of(sizes)

    def shares(grads):
        return [grad.reshape(grid + (grad.shape[0] // devices, grad.shape[1])) for grad in grads]

    def scatter_scratch(pieces, shapes, kept):
        count = Scatter.copies(sizes, pieces)
        return Scatter.scratch(sizes, pieces, shapes, kept) + [
            pltpu.SemaphoreType.DMA((number,)) for number in (len(pieces), count, count)
        ]

    if own:
        half = ff // 2
        share = feed_gate.shape[0]
        upper = gathered[11:13]
        gather_plan = [(0, 0, share, "zxy"), (1, 0, share, "zyx")]
        scatter_plan = [(0, 0, half, "xy"), (1, 0, half, "yx")]
        feed_in = (second, gout, gains, gate_low, up_low, down)
        feed_out = [act, act32, like((ff, width), BF16)]
        share_shapes = [like(grid + (share, half), BF16)] * 2
        grad_shapes = [like((share, half), F32)] * 2
        copies = Gather.copies(sizes, gather_plan)
        output, gsecond, ddown, *halves = pl.pallas_call(
            functools.partial(feed_exchange_kernel, plan=(sizes, gather_plan, scatter_plan)),
            out_shape=feed_out + share_shapes + grad_shapes + upper_shapes(upper),
            grid=(1,),
            in_specs=[remote] * (FEED_INS + 2),
            out_specs=[remote] * (FEED_OUTS + 2) + [full(o.shape) for o in grad_shapes] + [remote] * 2,
            scratch_shapes=Moves.scratch([*feed_in, *feed_out])
            + vmem(
                ((length, width), BF16), ((width, length), BF16), ((length, width), F32), ((length, width), F32),
                ((length, half), BF16), ((length, half), BF16), ((length, half), BF16),
                ((2, width, half), BF16), ((2, width, half), BF16),
                ((2,) + grid + (share, half), BF16), ((2,) + grid + (share, half), BF16),
            )
            + [pltpu.SemaphoreType.DMA((number,)) for number in (4, 2, len(gather_plan), copies, copies)]
            + scatter_scratch(scatter_plan, [(share, BF16)] * 2, [True, True]),
            input_output_aliases={FEED_INS: FEED_OUTS + 4, FEED_INS + 1: FEED_OUTS + 5},
            compiler_params=params(collective_id=3, has_side_effects=True),
            name="feed",
        )(*feed_in, *upper)
        high_shares, low_grads = halves[:2], halves[2:4]
    else:
        fblock = min(1024, ff)
        feed_out = [
            act, act32, like((width, ff), BF16), like((width, ff), BF16), like((ff, width), BF16)
        ]
        output, gsecond, dgate, dup, ddown = pl.pallas_call(
            feed_kernel,
            out_shape=feed_out,
            grid=(ff // fblock,),
            in_specs=[full(second.shape), full(gout.shape), full(gains.shape)]
            + [
                pl.BlockSpec((width, fblock), lambda i: (0, i)),
                pl.BlockSpec((width, fblock), lambda i: (0, i)),
                pl.BlockSpec((fblock, width), lambda i: (i, 0)),
            ],
            out_specs=[full(o.shape) for o in feed_out[:2]]
            + [
                pl.BlockSpec((width, fblock), lambda i: (0, i)),
                pl.BlockSpec((width, fblock), lambda i: (0, i)),
                pl.BlockSpec((fblock, width), lambda i: (i, 0)),
            ],
            scratch_shapes=vmem(
                ((length, width), BF16), ((width, length), BF16), ((length, width), F32), ((length, width), F32),
                ((length, fblock), BF16), ((length, fblock), BF16), ((length, fblock), BF16),
            ),
            compiler_params=params(),
            name="feed",
        )(second, gout, gains, gate_full, up_full, down)

    square = like((width, width), BF16)
    cross_shapes = [like((source, width), F32), act32, act] + [square] * 5
    cross_in = (gsecond, first, memory, gains, q2, k2, v2, mixed1, mixed2, lse2)
    cross_scratch = vmem(
        ((length, width), BF16), ((length, width), BF16), ((width, length), BF16), ((SUB, length), F32),
        ((8, length), F32), ((length, width), BF16), ((source, width), BF16), ((source, width), BF16),
        ((PAIR, length), F32),
    )
    plan, sources, gate_shapes, scratch = None, [], [], []
    if own:
        sources = high_shares + shares([ddown])
        pieces = [(0, 0, half, "xy"), (1, 0, half, "yx")] + split_columns(2, width)
        plan = (sizes, pieces)
        gate_shapes = [like(part.shape[-2:], F32) for part in sources]
        scratch = scatter_scratch(pieces, [(part.shape[-2], BF16) for part in sources], [False] * 3)
    moved = Moves.scratch([*cross_in, *attention[3:], *cross_shapes])
    gmem, gfirst, gm1, dwo, dcq, dck, dcv, dco, *feed_grads = pl.pallas_call(
        functools.partial(cross_backward_kernel, heads=heads, plan=plan),
        out_shape=cross_shapes + gate_shapes,
        grid=(1,),
        in_specs=[remote] * (CROSS_INS + len(sources)),
        out_specs=[remote] * CROSS_OUTS + [full(o.shape) for o in gate_shapes],
        scratch_shapes=moved + cross_scratch + scratch,
        compiler_params=params(collective_id=1, has_side_effects=True) if own else params(),
        name="cross_backward",
    )(*cross_in, *attention[3:], *sources)

    self_in = (bias_table, bucket_map)
    self_moved = (tokens, gains, lse1, q1, k1, v1, mixed1, gm1, gfirst, *attention[:3])
    self_scratch = vmem(
        ((heads, band.width), F32), ((SUB, band.causal), F32), ((SUB, band.two_way), F32), ((width, length), BF16),
        ((SUB, length), F32), ((8, length), F32), ((length, width), BF16), ((length, width), BF16),
        ((length, width), BF16), ((PAIR, length), F32), ((SUB, band.causal), F32), ((SUB, band.two_way), F32),
        ((heads, band.width), F32),
    )
    plan, sources, scratch = None, [], []
    table_shape = like((NB, heads), F32)
    if own:
        sources = shares([dco, dwo, dcq, dck, dcv])
        pieces, groups = self_pieces(width)
        plan = (sizes, pieces, groups)
        share = width // devices
        kept = [False] * REST + [True] * 4
        shapes = [(part.shape[-2], BF16) for part in sources] + [(share, BF16)] * 3 + [(TILE, F32)]
        self_shapes = [act32] + [like(part.shape[-2:], F32) for part in sources] + [like((share, width), F32)] * 3
        self_shapes += [table_shape]
        scratch = vmem(*[(grid + (share, width), BF16)] * 3, (grid + (TILE, SUB), F32), ((TILE, SUB), F32))
        scratch += scatter_scratch(pieces, shapes, kept)
    else:
        self_shapes = [act32, table_shape] + [square] * 3
    gtokens, *grads = pl.pallas_call(
        functools.partial(self_backward_kernel, band=band, heads=heads, plan=plan),
        out_shape=self_shapes,
        grid=(1,),
        in_specs=[scalar] + [full(a.shape) for a in self_in] + [remote] * (SELF_INS + len(sources)),
        out_specs=[full(o.shape) for o in self_shapes],
        scratch_shapes=Moves.scratch(self_moved) + self_scratch + scratch,
        compiler_params=params(collective_id=2, has_side_effects=True) if own else params(),
        name="self_backward",
    )(prefix, *self_in, *self_moved, *sources)

    gain_parts = (norm_self, norm_cross, norm_feed)
    weight_parts = (self_query, self_key, self_value, cross_query, feed_gate, feed_up)
    if own:
        results = [gtokens, output, gmem, (low_grads[0], feed_grads[0]), (low_grads[1], feed_grads[1]), feed_grads[2]]
        results, ggains = hand_on([*results, *grads], (11, 12, 13, 8, 3, 4), gain_parts, weight_parts)
        gtokens, output, gmem, dgate, dup, ddown, dco, dwo, dcq, dck, dcv, dwq, dwk, dwv, table_grad = results
    else:
        gtable, dwq, dwk, dwv = grads
        table_grad = lax.psum(gtable, AXES)

        def scatter(parts):
            return lax.psum_scatter(jnp.concatenate(parts, axis=1), AXES, scatter_dimension=0, tiled=True).astype(F32)

        dgate, dup = jnp.split(scatter([dgate, dup]), 2, axis=1)
        ddown = scatter([ddown])
        squares = scatter([dwq, dwk, dwv, dwo, dcq, dck, dcv, dco])
        dwq, dwk, dwv, dwo, dcq, dck, dcv, dco = jnp.split(squares, 8, axis=1)
        parts = gain_grads([gain.reshape(1, -1) for gain in gain_parts], weight_parts, (dwq, dwk, dwv, dcq, dgate, dup))
        ggains = [part.reshape(-1) for part in parts]
    return (
        output.reshape(inputs.shape),
        gtokens.reshape(inputs.shape),
        gmem.reshape(encoded.shape),
        table_grad,
        ggains[0], dwq, dwk, dwv, dwo,
        ggains[1], dcq, dck, dcv, dco,
        ggains[2], dgate, dup, ddown,
    )


def solution(mesh):
    rows = P(AXES, None)
    gain = P(AXES)
    block = P(AXES, None, None)
    return jax.shard_map(
        per_device,
        mesh=mesh,
        in_specs=(block, block, block, gain, P(), P())
        + (gain, rows, rows, rows, rows)
        + (gain, rows, rows, rows, rows)
        + (gain, rows, rows, rows),
        out_specs=(block, block, block, P())
        + (gain, rows, rows, rows, rows)
        + (gain, rows, rows, rows, rows)
        + (gain, rows, rows, rows),
        check_vma=False,
    )
```

```python
import functools

import jax
import jax.numpy as jnp
from jax import lax
from jax.experimental import pallas as pl
from jax.experimental.pallas import tpu as pltpu
from jax.sharding import PartitionSpec as P

DH = 64
NB = 32
PAIR = 2 * DH
SUB = 128
NEG = -1e30
F32 = jnp.float32
BF16 = jnp.bfloat16
AXES = ("dp", "fsdp")


def dot(a, b, ca=1, cb=0):
    return lax.dot_general(a, b, (((ca,), (cb,)), ((), ())), preferred_element_type=F32)


def exact_dot(a, b, ca=1, cb=0):
    return lax.dot_general(
        a,
        b,
        (((ca,), (cb,)), ((), ())),
        preferred_element_type=F32,
        precision=lax.Precision.HIGHEST,
    )


def rms(value):
    return lax.rsqrt(jnp.mean(value * value, axis=-1, keepdims=True) + 1e-06)


MESH = pl.DeviceIdType.MESH
EVERY = slice(None)


class Place:
    def __init__(self, sizes):
        self.grid = sizes
        self.sizes = grid_of(sizes)
        across, inner = lax.axis_index("dp"), lax.axis_index("fsdp")
        deep, high, wide, cores = self.sizes
        self.at = {
            "z": lax.div(across, high),
            "y": lax.rem(across, high),
            "x": lax.div(inner, cores),
            "c": lax.rem(inner, cores),
        }

    def device(self, **moved):
        at = {**self.at, **moved}
        deep, high, wide, cores = self.sizes
        return (at["z"] * high + at["y"], at["x"] * cores + at["c"])

    def size(self, axis):
        return self.sizes["zyxc".index(axis)]

    def others(self, axis):
        size = self.size(axis)
        return [lax.rem(self.at[axis] + step, size) for step in range(1, size)]

    def greet(self):
        barrier = pltpu.get_barrier_semaphore()
        for peer in self.peers():
            pl.semaphore_signal(barrier, inc=1, device_id=peer, device_id_type=MESH)

    def meet(self):
        pl.semaphore_wait(pltpu.get_barrier_semaphore(), len(self.peers()))

    def peers(self):
        return [self.device(**{axis: other}) for axis in "zyxc" for other in self.others(axis)]


def grid_of(sizes):
    wide = sizes["fsdp"] // 2
    return (sizes["dp"] // wide, wide, wide, 2)


class Moves:
    def __init__(self, ins, outs, refs):
        count = len(ins) + len(outs)
        self.ins, self.outs = ins, outs
        self.held, self.sem, self.rest = refs[:count], refs[count], refs[count + 1 :]
        self.held_ins, self.held_outs = self.held[: len(ins)], self.held[len(ins) :]
        self.stored = []

    @staticmethod
    def scratch(arrays):
        return [pltpu.VMEM(a.shape, a.dtype) for a in arrays] + [pltpu.SemaphoreType.DMA((len(arrays),))]

    def copy(self, number):
        if number < len(self.ins):
            return pltpu.make_async_copy(self.ins[number], self.held[number], self.sem.at[number])
        return pltpu.make_async_copy(self.held[number], self.outs[number - len(self.ins)], self.sem.at[number])

    def load(self, *numbers):
        for number in numbers:
            self.copy(number).start()

    def need(self, *numbers):
        for number in numbers:
            self.copy(number).wait()

    def store(self, *numbers):
        for number in numbers:
            self.copy(len(self.ins) + number).start()
            self.stored.append(len(self.ins) + number)

    def finish(self):
        for number in self.stored:
            self.copy(number).wait()


class Gather:
    PHASES = 4

    def __init__(self, place, pieces, shards, outs, local_sem, send_sem, recv_sem):
        self.place, self.pieces, self.shards, self.outs = place, pieces, shards, outs
        self.local_sem, self.send_sem, self.recv_sem = local_sem, send_sem, recv_sem

    @staticmethod
    def each(sizes):
        grid = grid_of(sizes)
        return sum(size - 1 for size in grid[:3]) + max(grid[:3])

    @staticmethod
    def copies(sizes, pieces):
        return len(pieces) * Gather.each(sizes)

    def view(self, piece, held):
        array, first, rows, order = piece
        start = self.place.at["c"] * (self.outs[array].shape[3] // 2) + first
        where = [held.get(axis, EVERY) for axis in "zyx"]
        return self.outs[array].at[(*where, pl.ds(pl.multiple_of(start, 8), rows), EVERY)]

    def phase(self, number, phase, core):
        piece = self.pieces[number]
        place, at = self.place, self.place.at
        array, first, rows, order = piece
        slot = number * self.each(place.grid) + sum(place.size(axis) - 1 for axis in order[:phase])
        copies = []

        def send(source, target, **moved):
            copies.append(
                pltpu.make_async_remote_copy(
                    source,
                    target,
                    self.send_sem.at[slot + len(copies)],
                    self.recv_sem.at[slot + len(copies)],
                    device_id=place.device(**moved),
                    device_id_type=MESH,
                )
            )

        other_core = place.others("c")[0]
        last = order[2]
        if core:
            slot = number * self.each(place.grid) + sum(place.size(axis) - 1 for axis in order)
            if phase == 2:
                part = self.view(piece, {last: at[last]})
                send(part, part, c=other_core)
            else:
                slot += 1
                for other in place.others(last):
                    part = self.view(piece, {last: other})
                    send(part, part, c=other_core)
            return copies
        axis = order[phase]
        target = self.view(piece, {later: at[later] for later in order[phase:]})
        source = self.shards[array].at[pl.ds(first, rows), :] if phase == 0 else target
        for other in place.others(axis):
            send(source, target, **{axis: other})
        if phase == 0:
            copies.append(pltpu.make_async_copy(source, target, self.local_sem.at[number]))
        return copies

    def advance(self, numbers, phase):
        for number in numbers:
            waits, starts = [], []
            if 0 < phase < 4:
                waits = self.phase(number, phase - 1, False)
            if phase < 3:
                starts = self.phase(number, phase, False)
            if phase in (2, 3):
                starts += self.phase(number, phase, True)
            if phase == 4:
                waits = self.phase(number, 2, True) + self.phase(number, 3, True)
            for copy in waits:
                copy.wait()
            for copy in starts:
                copy.start()

    def settle(self, numbers):
        for number in numbers:
            for copy in self.phase(number, 0, False):
                copy.wait()

    def resume(self, numbers):
        for number in numbers:
            for copy in self.phase(number, 1, False):
                copy.start()


class Scatter:
    PHASES = 4

    def __init__(self, place, pieces, sources, kept, outs, buffers, load_sem, send_sem, recv_sem):
        self.place, self.pieces, self.sources, self.kept, self.outs = place, pieces, sources, kept, outs
        self.buffers, self.load_sem, self.send_sem, self.recv_sem = buffers, load_sem, send_sem, recv_sem

    @staticmethod
    def copies(sizes, pieces):
        return len(pieces) * sum(size - 1 for size in grid_of(sizes))

    @staticmethod
    def scratch(sizes, pieces, shapes, kept):
        deep, high, wide, cores = grid_of(sizes)
        buffers = []
        for source, first, columns, order in pieces:
            rows, dtype = shapes[source]
            near, far = (wide, high) if order == "xy" else (high, wide)
            block = (rows, columns)
            shapes_here = [(deep, high, wide) + block, (near - 1, deep, far) + block, (far - 1, deep) + block, (deep,) + block]
            if not kept[source]:
                shapes_here.append((deep, high, wide) + block)
            buffers += [pltpu.VMEM(shape, dtype) for shape in shapes_here]
        return buffers

    def buffer(self, number, which):
        place = sum(4 if self.kept[piece[0]] else 5 for piece in self.pieces[:number])
        return self.buffers[place + which]

    def half(self, number, core):
        source, first, columns, order = self.pieces[number]
        return self.sources[source].at[:, :, :, core, :, pl.ds(first, columns)]

    def load(self, number):
        return pltpu.make_async_copy(self.half(number, self.place.at["c"]), self.buffer(number, 4), self.load_sem.at[number])

    def phase(self, number, phase):
        place = self.place
        at = place.at
        deep, high, wide, cores = place.sizes
        order = self.pieces[number][3]
        base = number * sum(size - 1 for size in place.sizes)
        axis = ("c" + order + "z")[phase]
        skip = sum(place.size(before) - 1 for before in ("c" + order + "z")[:phase])
        sums = self.buffer(number, 0)
        copies = []
        for step, other in enumerate(place.others(axis)):
            if phase == 0:
                source, target = self.half(number, other), sums
            elif phase == 3:
                source, target = sums.at[other, at["y"], at["x"]], self.buffer(number, 3).at[at["z"]]
            else:
                target = self.buffer(number, phase).at[step]
                y, x = (other, EVERY) if axis == "y" else (EVERY, other)
                if phase == 2:
                    y, x = (other, at["x"]) if axis == "y" else (at["y"], other)
                source = sums.at[:, y, x]
            slot = base + skip + step
            copies.append(
                pltpu.make_async_remote_copy(
                    source,
                    target,
                    self.send_sem.at[slot],
                    self.recv_sem.at[slot],
                    device_id=place.device(**{axis: other}),
                    device_id_type=MESH,
                )
            )
        return copies

    def absorb(self, number, phase):
        source, first, columns, order = self.pieces[number]
        at = self.place.at
        deep = self.place.sizes[0]
        sums = self.buffer(number, 0)
        if phase == 3:
            slots = self.buffer(number, 3)
            slots[at["z"]] = sums[at["z"], at["y"], at["x"]]
            total = slots[0].astype(F32)
            for slot in range(1, deep):
                total += slots[slot].astype(F32)
            self.outs[source][:, first : first + columns] = total
            return

        @pl.loop(0, deep)
        def _(z):
            if phase == 0:
                own = self.sources[source].at[z, :, :, at["c"], :, pl.ds(first, columns)] if self.kept[source] else self.buffer(number, 4).at[z]
                view, parts = sums.at[z], [own[...]]
            else:
                came = self.buffer(number, phase)
                parts = [came[step, z] for step in range(came.shape[0])]
                if phase == 1:
                    view = sums.at[z, :, at["x"]] if order[0] == "x" else sums.at[z, at["y"]]
                else:
                    view = sums.at[z, at["y"], at["x"]]
            if len(parts) == 1:
                view[...] = view[...] + parts[0]
            else:
                total = view[...].astype(F32)
                for part in parts:
                    total += part.astype(F32)
                view[...] = total.astype(view.dtype)

    def advance(self, numbers, phase):
        for number in numbers:
            if phase > 0:
                for copy in self.phase(number, phase - 1):
                    copy.wait()
                if phase == 1 and not self.kept[self.pieces[number][0]]:
                    self.load(number).wait()
                self.absorb(number, phase - 1)
            elif not self.kept[self.pieces[number][0]]:
                self.load(number).start()
            if phase < self.PHASES:
                for copy in self.phase(number, phase):
                    copy.start()


class Band:
    def __init__(self, length, reach):
        self.reach = reach
        self.causal = length + reach
        self.two_way = 2 * reach
        self.width = self.causal + self.two_way
        self.query_zero = length - SUB
        self.query_zero_two = reach - SUB
        self.key_zero = reach - SUB

    def distances(self, rows):
        causal = lax.broadcasted_iota(jnp.int32, (1, self.causal), 1)
        two_way = lax.broadcasted_iota(jnp.int32, (1, self.two_way), 1)
        if rows == "queries":
            causal, two_way = self.query_zero - causal, self.query_zero_two - two_way
            return (
                jnp.where(causal <= -self.reach, causal + self.causal, causal),
                jnp.where(two_way <= -self.reach, two_way + self.two_way, two_way),
            )
        causal, two_way = causal - self.key_zero, two_way - self.key_zero
        return (
            jnp.where(causal >= self.causal - self.reach, causal - self.causal, causal),
            jnp.where(two_way >= self.reach, two_way - self.two_way, two_way),
        )


def one_hot(map_ref, band, rows):
    bucket = lax.broadcasted_iota(jnp.int32, (NB, 1), 0)

    def edges(row, number):
        entries = map_ref[row : row + 1, :]
        below = jnp.sum((entries < number).astype(jnp.int32), axis=1, keepdims=True)
        return below, below + jnp.sum((entries == number).astype(jnp.int32), axis=1, keepdims=True)

    causal, two_way = band.distances(rows)
    low, high = edges(0, bucket)
    one = (causal >= low) & (causal < high)
    ahead = bucket >= NB // 2
    low, high = edges(1, jnp.where(ahead, bucket - NB // 2, bucket))
    apart = jnp.abs(two_way)
    two = (apart >= low) & (apart < high) & ((two_way < 0) == ahead)
    return jnp.concatenate([jnp.where(one, 1.0, 0.0), jnp.where(two, 1.0, 0.0)], axis=1), causal


def spread(row, width):
    return pltpu.roll(jnp.broadcast_to(row, (SUB, width)), 0, 1, stride=1, stride_axis=0)


def fold(band):
    width = band.shape[1]
    half = SUB // 2
    while half >= 8:
        band = band[:half] + pltpu.roll(band[half:], width - half, 1)
        half //= 2
    row = lax.broadcasted_iota(jnp.int32, band.shape, 0)
    for bit in (4, 2, 1):
        band = jnp.where((row & bit) != 0, pltpu.roll(band, width - bit, 1), band)
    return jnp.sum(band, axis=0, keepdims=True)


def fill_bands(head, bias_ref, band, causal_ref, two_ref):
    row = bias_ref[pl.ds(head, 1), :]
    causal_ref[...] = spread(row[:, : band.causal], band.causal)
    two_ref[...] = spread(row[:, band.causal :], band.two_way)


def bias_rows(table_ref, map_ref, band, rows):
    hot, causal = one_hot(map_ref, band, rows)
    bias = dot(table_ref[...], hot.astype(BF16))
    return jnp.concatenate([jnp.where(causal < 0, NEG, bias[:, : band.causal]), bias[:, band.causal :]], axis=1)


def head_cols(head):
    group = head // 2
    return pl.ds(pl.multiple_of(group * PAIR, PAIR), PAIR), head % 2


def pick_lanes(half):
    return lax.broadcasted_iota(jnp.int32, (1, PAIR), 1) // DH == half


def soft_rows(scores):
    high = jnp.max(scores, axis=-1, keepdims=True)
    weights = jnp.exp(scores - high)
    total = jnp.sum(weights, axis=-1, keepdims=True)
    return weights.astype(BF16), total, high + jnp.log(total)


def store_head(mixed_ref, lse_ref, rows, cols, head, half, out, total, lse):
    pick = pick_lanes(half)
    mixed_ref[rows, cols] = jnp.where(pick, (out / total).astype(BF16), mixed_ref[rows, cols])
    lane = lax.broadcasted_iota(jnp.int32, (1, lse_ref.shape[1]), 1)
    lse_ref[rows, :] = jnp.where(lane == head, lse, lse_ref[rows, :])


def self_forward_head(head, limit, q_ref, k_ref, v_ref, causal_ref, two_ref, band, mixed_ref, lse_ref):
    length = q_ref.shape[0]
    cols, half = head_cols(head)
    pick = pick_lanes(half)
    block = 256
    for start in range(0, length, block):
        keys = max(start + block, band.reach)
        rows = pl.ds(start, block)
        query = jnp.where(pick, q_ref[rows, cols], 0)
        scores = dot(query, k_ref[pl.ds(0, keys), cols], 1, 1)
        parts = []
        for first in range(start, start + block, SUB):
            at = band.query_zero - first
            bias = causal_ref[:, at : at + keys]
            if start < band.reach:
                at = band.query_zero_two - first
                two = two_ref[:, at : at + keys]
                inside = (first + lax.broadcasted_iota(jnp.int32, (SUB, keys), 0) < limit) & (
                    lax.broadcasted_iota(jnp.int32, (SUB, keys), 1) < limit
                )
                bias = jnp.where(inside, two, bias)
            parts.append(bias)
        weights, total, lse = soft_rows(scores + jnp.concatenate(parts, axis=0))
        out = dot(weights, v_ref[pl.ds(0, keys), cols])
        store_head(mixed_ref, lse_ref, rows, cols, head, half, out, total, lse)


def cross_forward_head(head, q_ref, k_ref, v_ref, mixed_ref, lse_ref):
    length = q_ref.shape[0]
    cols, half = head_cols(head)
    pick = pick_lanes(half)
    block = 256
    for start in range(0, length, block):
        rows = pl.ds(start, block)
        query = jnp.where(pick, q_ref[rows, cols], 0)
        weights, total, lse = soft_rows(dot(query, k_ref[:, cols], 1, 1))
        out = dot(weights, v_ref[:, cols])
        store_head(mixed_ref, lse_ref, rows, cols, head, half, out, total, lse)


def row_blocks(count, block, step):
    @pl.loop(0, count // block)
    def _(index):
        step(pl.ds(pl.multiple_of(index * block, block), block))


def gain_rows(gathered, width):
    devices = gathered.shape[0]
    share = width // devices
    lane = lax.broadcasted_iota(jnp.int32, (SUB, width), 1)
    select = jnp.where(lax.rem(lane, share) == lax.broadcasted_iota(jnp.int32, (SUB, width), 0), 1.0, 0.0)
    first = share * lax.broadcasted_iota(jnp.int32, (devices, width), 0)
    lane = lax.broadcasted_iota(jnp.int32, (devices, width), 1)
    own = (lane >= first) & (lane < first + share)
    rows = []
    for number in range(8):
        spread_out = exact_dot(gathered[:, number, :], select)
        rows.append(jnp.sum(jnp.where(own, spread_out, 0.0), axis=0, keepdims=True))
    return jnp.concatenate(rows, axis=0)


ATTENTION = 8
SHARDS = 14


def gather_pieces(rows, down_rows):
    head, tail = rows // 3 // 8 * 8, rows - rows // 3 // 8 * 8
    half = down_rows // 2
    table = {
        "qk": [(0, 0, rows, "zxy"), (1, 0, rows, "zyx"), (13, 0, 8, "zxy")],
        "v": [(2, 0, head, "xzy"), (2, head, tail, "yzx")],
        "out": [(3, 0, rows, "zxy"), (4, 0, rows, "zyx"), (7, 0, tail, "zxy"), (7, tail, head, "zyx")],
        "memory": [(5, 0, rows, "xzy"), (6, 0, rows, "yzx")],
        "gate": [(8, 0, rows, "zxy"), (9, 0, rows, "zyx")],
        "down": [(10, 0, half, "xzy"), (10, half, half, "yzx")],
        "upper": [(11, 0, rows, "zxy"), (12, 0, rows, "zyx")],
    }
    pieces, groups = [], {}
    for name, group in table.items():
        groups[name] = range(len(pieces), len(pieces) + len(group))
        pieces += group
    return pieces, groups


FORWARD_OUTS = 13


def forward_kernel(
    limit_ref, tokens_ref, memory_ref, table_ref, map_ref, gain1_ref, gain2_ref, gain3_ref, *refs, band, heads, plan,
):
    count = ATTENTION + 3 if plan else ATTENTION
    shards, refs = refs[:count], refs[count:]
    if plan:
        gathered, refs = refs[:SHARDS], refs[SHARDS:]
    else:
        gathered = shards
    moves = Moves((), refs[:FORWARD_OUTS], refs[FORWARD_OUTS:])
    (
        gains_ref, q1_ref, k1_ref, v1_ref, mixed1_ref, lse1_ref, first_ref,
        q2_ref, k2_ref, v2_ref, mixed2_ref, lse2_ref, second_ref,
    ) = moves.held_outs
    bias_ref, causal_ref, two_ref, weights_ref, share_ref, tile_ref, load_sem, *gather_sems = moves.rest
    length, width = tokens_ref.shape
    if plan:
        sizes, pieces, groups = plan
        place = Place(sizes)
        columns = gathered[8].shape[-1]
        halves = [[ref.at[:, start : start + columns] for ref in shards[8:10]] for start in (0, columns)]
        parts = (*shards[:8], *halves[0], shards[10], *halves[1], share_ref)
        gather = Gather(place, pieces, parts, gathered, *gather_sems)

    def advance(*steps):
        if plan:
            for numbers, phase in steps:
                gather.advance(groups[numbers], phase)

    def load(number):
        return pltpu.make_async_copy(gathered[number].reshape(width, width), weights_ref.at[number], load_sem.at[number])

    def load_tile():
        return pltpu.make_async_copy(gathered[SHARDS - 1].reshape(tile_ref.shape), tile_ref, load_sem.at[ATTENTION])

    gain_refs = (gain1_ref, gain2_ref, gain3_ref)
    if plan:
        share_ref[...] = jnp.zeros_like(share_ref)
        for number, gain_ref in enumerate(gain_refs):
            share_ref[number : number + 1, : gain_ref.shape[1]] = gain_ref[...].astype(F32)
        place.greet()
    bias_ref[...] = bias_rows(table_ref, map_ref, band, "queries")
    lse1_ref[...] = jnp.zeros_like(lse1_ref)
    lse2_ref[...] = jnp.zeros_like(lse2_ref)
    mixed1_ref[...] = jnp.zeros_like(mixed1_ref)
    mixed2_ref[...] = jnp.zeros_like(mixed2_ref)
    if plan:
        place.meet()
    advance(("qk", 0), ("v", 0), ("memory", 0))
    advance(("v", 1), ("qk", 1), ("qk", 2), ("v", 2), ("out", 0))
    advance(("qk", 3), ("v", 3), ("qk", 4), ("v", 4), ("memory", 1), ("out", 1), ("gate", 0), ("down", 0), ("upper", 0))
    for number in range(3):
        load(number).start()
    if plan:
        load_tile().start()
        load_tile().wait()
        gains_ref[...] = gain_rows(tile_ref[...], width)
    else:
        gains_ref[...] = jnp.zeros_like(gains_ref)
        for number, gain_ref in enumerate(gain_refs):
            gains_ref[number : number + 1, :] = gain_ref[...].astype(F32)
    for number in range(3):
        load(number).wait()

    def project_self(rows):
        value = tokens_ref[rows, :].astype(F32)
        normed = (value * rms(value) * gains_ref[0:1, :]).astype(BF16)
        q1_ref[rows, :] = dot(normed, weights_ref[0]).astype(BF16)
        k1_ref[rows, :] = dot(normed, weights_ref[1]).astype(BF16)
        v1_ref[rows, :] = dot(normed, weights_ref[2]).astype(BF16)

    for start in range(0, length, length // 2):
        project_self(pl.ds(start, length // 2))
        if start == 0:
            advance(("out", 2))
    moves.store(0, 1, 2, 3)

    @pl.loop(0, heads)
    def _(head):
        fill_bands(head, bias_ref, band, causal_ref, two_ref)
        self_forward_head(head, limit_ref[0], q1_ref, k1_ref, v1_ref, causal_ref, two_ref, band, mixed1_ref, lse1_ref)

        for when, steps in (
            (1, (("out", 3), ("memory", 2))),
            (4, (("out", 4), ("down", 1))),
            (6, (("memory", 3),)),
            (8, (("memory", 4), ("gate", 1))),
        ):

            @pl.when(head == when * heads // 12)
            def _(when=when, steps=steps):
                advance(*steps)
                for number in {4: (3, 4, 7), 8: (5, 6)}.get(when, ()):
                    load(number).start()

    advance(("gate", 2))
    moves.store(4, 5)
    for number in range(3, ATTENTION):
        load(number).wait()

    def project_memory(rows):
        k2_ref[rows, :] = dot(memory_ref[rows, :], weights_ref[5]).astype(BF16)
        v2_ref[rows, :] = dot(memory_ref[rows, :], weights_ref[6]).astype(BF16)

    row_blocks(memory_ref.shape[0], 512, project_memory)

    def project_cross(rows):
        value = tokens_ref[rows, :].astype(F32) + dot(mixed1_ref[rows, :], weights_ref[3])
        first_ref[rows, :] = value
        normed = (value * rms(value) * gains_ref[1:2, :]).astype(BF16)
        q2_ref[rows, :] = dot(normed, weights_ref[4]).astype(BF16)

    row_blocks(length, 512, project_cross)
    moves.store(6, 7, 8, 9)

    @pl.loop(0, heads)
    def _(head):
        cross_forward_head(head, q2_ref, k2_ref, v2_ref, mixed2_ref, lse2_ref)

        @pl.when(head == heads // 4)
        def _():
            advance(("down", 2))

        @pl.when(head == heads * 2 // 3)
        def _():
            advance(("gate", 3))

    advance(("down", 3))
    moves.store(10, 11)

    def project_second(rows):
        second_ref[rows, :] = first_ref[rows, :] + dot(mixed2_ref[rows, :], weights_ref[7])

    row_blocks(length, 512, project_second)
    moves.store(12)
    advance(("gate", 4), ("down", 4))
    if plan:
        gather.settle(groups["upper"])
    moves.finish()


def norm_back_rows(value, gain, grad):
    scale = rms(value)
    unit = value * scale
    scaled = grad * gain
    return scale * (scaled - unit * jnp.mean(scaled * unit, axis=-1, keepdims=True))


GELU_A = 0.7978845608028654
GELU_B = 0.044715


def feed_rows(
    rows, gate_ref, up_ref, down_ref, gout_ref, normed_ref, out_ref, back_ref, hidden_ref, ggate_ref, gup_ref
):
    normed = normed_ref[rows, :]
    gate = dot(normed, gate_ref[...])
    upward = dot(normed, up_ref[...])
    square = gate * gate
    bend = jnp.tanh(GELU_A * gate * (1.0 + GELU_B * square))
    half = 0.5 * (1.0 + bend)
    active = gate * half
    hidden = (active * upward).astype(BF16)
    hidden_ref[rows, :] = hidden
    out_ref[rows, :] += dot(hidden, down_ref[...])
    ghidden = dot(gout_ref[rows, :], down_ref[...], 1, 1)
    slope = half + 0.5 * gate * (1.0 - bend * bend) * (GELU_A * (1.0 + 3.0 * GELU_B * square))
    ggate = (ghidden * upward * slope).astype(BF16)
    gup = (ghidden * active).astype(BF16)
    ggate_ref[rows, :] = ggate
    gup_ref[rows, :] = gup
    back_ref[rows, :] += dot(ggate, gate_ref[...], 1, 1) + dot(gup, up_ref[...], 1, 1)


def feed_kernel(
    second_ref, gout_ref, gains_ref, gate_ref, up_ref, down_ref,
    output_ref, gsecond_ref, dgate_ref, dup_ref, ddown_ref,
    normed_ref, flipped_ref, out_ref, back_ref, hidden_ref, ggate_ref, gup_ref,
):
    step = pl.program_id(0)
    length = second_ref.shape[0]
    block = 256

    @pl.when(step == 0)
    def _():
        def prepare(rows):
            value = second_ref[rows, :]
            normed = (value * rms(value) * gains_ref[2:3, :]).astype(BF16)
            normed_ref[rows, :] = normed
            flipped_ref[:, rows] = normed.T
            out_ref[rows, :] = value
            back_ref[rows, :] = jnp.zeros_like(value)

        row_blocks(length, block, prepare)

    def rows_step(rows):
        feed_rows(
            rows, gate_ref, up_ref, down_ref, gout_ref, normed_ref, out_ref, back_ref, hidden_ref, ggate_ref, gup_ref
        )

    row_blocks(length, 512, rows_step)
    ddown_ref[...] = dot(hidden_ref[...].T, gout_ref[...]).astype(BF16)
    dgate_ref[...] = dot(flipped_ref[...], ggate_ref[...]).astype(BF16)
    dup_ref[...] = dot(flipped_ref[...], gup_ref[...]).astype(BF16)

    @pl.when(step == pl.num_programs(0) - 1)
    def _():
        def finish(rows):
            output_ref[rows, :] = out_ref[rows, :].astype(BF16)
            back = norm_back_rows(second_ref[rows, :], gains_ref[2:3, :], back_ref[rows, :])
            gsecond_ref[rows, :] = back + gout_ref[rows, :].astype(F32)

        row_blocks(length, block, finish)


FEED_INS, FEED_OUTS = 6, 3


def feed_exchange_kernel(*refs, plan):
    ins, refs = refs[:FEED_INS], refs[FEED_INS + 2 :]
    results, refs = refs[:FEED_OUTS], refs[FEED_OUTS:]
    shares, outs, gathered, refs = refs[:2], refs[2:4], refs[4:6], refs[6:]
    moves = Moves(ins, results, refs)
    second_ref, gout_ref, gains_ref, gate_low_ref, up_low_ref, down_ref = moves.held_ins
    output_ref, gsecond_ref, ddown_ref = moves.held_outs
    (
        normed_ref, flipped_ref, out_ref, back_ref, hidden_ref, ggate_ref, gup_ref, gate_ref, up_ref,
        dgate_ref, dup_ref, load_sem, share_sem, *refs,
    ) = moves.rest
    sizes, gather_plan, scatter_plan = plan
    place = Place(sizes)
    gather = Gather(place, gather_plan, (), gathered, *refs[:3])
    lower = [dgate_ref.at[0], dup_ref.at[0]]
    scatter = Scatter(place, scatter_plan, lower, [True, True], outs, refs[3:-3], *refs[-3:])
    upper, every = range(len(gather_plan)), range(len(scatter_plan))
    length, width = second_ref.shape
    columns = gate_low_ref.shape[1]
    block = 256

    def load(number):
        target = (gate_ref, up_ref)[number].at[1]
        return pltpu.make_async_copy(gathered[number].reshape(width, columns), target, load_sem.at[number])

    def low(number):
        target = (gate_ref, up_ref)[number].at[0]
        return pltpu.make_async_copy((ins[3], ins[4])[number], target, load_sem.at[2 + number])

    place.greet()
    moves.load(0, 2, 1)
    for number in (0, 1):
        low(number).start()
    moves.load(5)
    place.meet()
    gather.resume(upper)
    moves.need(0, 2)

    def prepare(rows):
        value = second_ref[rows, :]
        normed = (value * rms(value) * gains_ref[2:3, :]).astype(BF16)
        normed_ref[rows, :] = normed
        flipped_ref[:, rows] = normed.T
        out_ref[rows, :] = value
        back_ref[rows, :] = jnp.zeros_like(value)

    row_blocks(length, block, prepare)
    moves.need(1, 5)
    for number in (0, 1):
        low(number).wait()

    @pl.loop(0, 2)
    def _(half):
        units = pl.ds(pl.multiple_of(half * columns, columns), columns)
        gate, up, down = gate_ref.at[half], up_ref.at[half], down_ref.at[units]

        @pl.loop(0, 2)
        def _(index):
            rows = pl.ds(pl.multiple_of(index * (length // 2), length // 2), length // 2)
            feed_rows(rows, gate, up, down, gout_ref, normed_ref, out_ref, back_ref, hidden_ref, ggate_ref, gup_ref)

            @pl.when((half == 0) & (index == 0))
            def _():
                gather.advance(upper, 2)

            @pl.when((half == 1) & (index == 0))
            def _():
                scatter.advance(every, 2)

            @pl.when((half == 1) & (index == 1))
            def _():
                scatter.advance(every, 3)

        rows_each = width // place.sizes[0]

        @pl.loop(0, place.sizes[0])
        def _(index):
            start = pl.multiple_of(index * rows_each, 64)
            flipped = flipped_ref[pl.ds(start, rows_each), :]
            for target, grad in ((dgate_ref, ggate_ref), (dup_ref, gup_ref)):
                store_shares(target.at[half], EVERY, dot(flipped, grad[...]), start)

        @pl.when(half == 0)
        def _():
            scatter.advance(every, 0)
            gather.advance(upper, 3)

        @pl.loop(0, 2)
        def _(index):
            start = pl.multiple_of(index * (columns // 2), columns // 2)
            flipped = hidden_ref[:, pl.ds(start, columns // 2)].T
            into = pl.ds(pl.multiple_of(half * columns + start, columns // 2), columns // 2)
            ddown_ref[into, :] = dot(flipped, gout_ref[...]).astype(BF16)

        @pl.when(half == 0)
        def _():
            gather.advance(upper, 4)
            for number in upper:
                load(number).start()
            scatter.advance(every, 1)
            for number in upper:
                load(number).wait()

    share = [pltpu.make_async_copy(ref.at[1], shares[i], share_sem.at[i]) for i, ref in enumerate((dgate_ref, dup_ref))]
    for copy in share:
        copy.start()
    moves.store(2)

    def finish(rows):
        output_ref[rows, :] = out_ref[rows, :].astype(BF16)
        back = norm_back_rows(second_ref[rows, :], gains_ref[2:3, :], back_ref[rows, :])
        gsecond_ref[rows, :] = back + gout_ref[rows, :].astype(F32)

    row_blocks(length, block, finish)
    moves.store(0, 1)
    scatter.advance(every, 4)
    for copy in share:
        copy.wait()
    moves.finish()


def backward_head_prepare(group_cols, gm_ref, mixed_ref, delta_ref):
    product = (gm_ref[:, group_cols].astype(F32) * mixed_ref[:, group_cols].astype(F32)).T
    delta_ref[0:1, :] = jnp.sum(product[:DH], axis=0, keepdims=True)
    delta_ref[1:2, :] = jnp.sum(product[DH:], axis=0, keepdims=True)


def backward_block(key_rows, cols, half, start, bias, q_ref, k_ref, v_ref, gm_ref, lse, delta, gk_ref, gv_ref, gqt_ref):
    length = q_ref.shape[0]
    pick = pick_lanes(half)
    queries = pl.ds(start, length - start)
    query = jnp.where(pick, q_ref[queries, cols], 0)
    grad = jnp.where(pick, gm_ref[queries, cols], 0)
    keys = k_ref[key_rows, cols]
    scores = dot(keys, query, 1, 1)
    if bias is not None:
        scores = scores + bias
    probs = jnp.exp(scores - lse[:, start:])
    gv = dot(probs.astype(BF16), grad)
    gprobs = dot(v_ref[key_rows, cols], grad, 1, 1)
    gscores = probs * (gprobs - delta[:, start:])
    low = gscores.astype(BF16)
    gk = dot(low, query)
    gk_ref[key_rows, cols] = jnp.where(pick, gk.astype(BF16), gk_ref[key_rows, cols])
    gv_ref[key_rows, cols] = jnp.where(pick, gv.astype(BF16), gv_ref[key_rows, cols])
    gqt_ref[:, queries] += dot(jnp.where(pick, keys, 0).T, low)
    return gscores


def self_backward_head(
    head, limit, q_ref, k_ref, v_ref, gm_ref, mixed_ref, lse_ref, delta_ref, causal_ref, two_ref, band,
    gk_ref, gv_ref, gqt_ref, causal_sum_ref, two_sum_ref,
):
    length = q_ref.shape[0]
    cols, half = head_cols(head)
    lse = lse_ref[pl.ds(head, 1), :]
    delta = delta_ref[pl.ds(half, 1), :]
    reach = band.reach
    block = 256
    for first in range(0, length, block):
        start = 0 if first < reach else first
        count = length - start
        parts = []
        for key in range(first, first + block, SUB):
            at = band.key_zero - key + start
            bias = causal_ref[:, at : at + count]
            if first < reach:
                at = band.key_zero - key
                two = two_ref[:, at : at + reach]
                inside = (key + lax.broadcasted_iota(jnp.int32, (SUB, reach), 0) < limit) & (
                    lax.broadcasted_iota(jnp.int32, (SUB, reach), 1) < limit
                )
                bias = jnp.concatenate([jnp.where(inside, two, bias[:, :reach]), bias[:, reach:]], axis=1)
            parts.append(bias)
        gscores = backward_block(
            pl.ds(first, block), cols, half, start, jnp.concatenate(parts, axis=0),
            q_ref, k_ref, v_ref, gm_ref, lse, delta, gk_ref, gv_ref, gqt_ref,
        )
        for key in range(first, first + block, SUB):
            part = gscores[key - first : key - first + SUB]
            at = band.key_zero - key + start
            if first < reach:
                inside = (key + lax.broadcasted_iota(jnp.int32, (SUB, reach), 0) < limit) & (
                    lax.broadcasted_iota(jnp.int32, (SUB, reach), 1) < limit
                )
                head_part = part[:, :reach]
                at_two = band.key_zero - key
                two_sum_ref[:, at_two : at_two + reach] += jnp.where(inside, head_part, 0.0)
                causal_sum_ref[:, at : at + reach] += jnp.where(inside, 0.0, head_part)
                causal_sum_ref[:, at + reach : at + count] += part[:, reach:]
            else:
                causal_sum_ref[:, at : at + count] += part


def split_columns(number, columns):
    half = columns // 2
    return [(number, 0, half, "xy"), (number, half, half, "yx")]


CROSS_INS, CROSS_OUTS = 15, 8


def cross_backward_kernel(*refs, heads, plan):
    count = 3 if plan else 0
    ins, refs = refs[:CROSS_INS], refs[CROSS_INS:]
    sources, refs = refs[:count], refs[count:]
    results, refs = refs[:CROSS_OUTS], refs[CROSS_OUTS:]
    outs, refs = refs[:count], refs[count:]
    moves = Moves(ins, results, refs)
    (
        gsecond_ref, first_ref, memory_ref, gains_ref, q_ref, k_ref, v_ref, mixed1_ref, mixed2_ref, lse_ref,
        wo_ref, cq_ref, ck_ref, cv_ref, co_ref,
    ) = moves.held_ins
    gmem_ref, gfirst_ref, gm1_ref, dwo_ref, dcq_ref, dck_ref, dcv_ref, dco_ref = moves.held_outs
    gm_ref, branch_ref, flipped_ref, lse_rows_ref, delta_ref, gq_ref, gk_ref, gv_ref, gqt_ref, *refs = moves.rest
    if plan:
        sizes, pieces = plan
        scatter = Scatter(Place(sizes), pieces, sources, [False] * count, outs, refs[:-3], *refs[-3:])
        waves = [range(number, number + 2) for number in range(0, len(pieces), 2)]
        scatter.place.greet()

    def advance(*steps):
        if plan:
            for wave, phase in steps:
                scatter.advance(waves[wave], phase)

    moves.load(0, 14, 8, 4, 5, 6, 9, 2, 12, 13, 1, 3, 11, 10, 7)
    if plan:
        scatter.place.meet()
    advance((0, 0), (1, 0), (2, 0), (3, 0))
    length, width = first_ref.shape
    source = memory_ref.shape[0]
    block = 256

    def prepare(rows):
        branch = gsecond_ref[rows, :].astype(BF16)
        branch_ref[rows, :] = branch
        gm_ref[rows, :] = dot(branch, co_ref[...], 1, 1).astype(BF16)
        flipped_ref[:, rows] = mixed2_ref[rows, :].T

    moves.need(0, 14, 8)
    row_blocks(length, 256, prepare)

    def out_grad(rows):
        dco_ref[rows, :] = dot(flipped_ref[rows, :], branch_ref[...]).astype(BF16)

    row_blocks(width, 192, out_grad)
    moves.store(7)
    moves.need(4, 5, 6, 9)
    advance((0, 1))
    lse_rows_ref[...] = lse_ref[...].T
    gk_ref[...] = jnp.zeros_like(gk_ref)
    gv_ref[...] = jnp.zeros_like(gv_ref)
    groups = heads // 2

    @pl.loop(0, groups)
    def _(group):
        cols = pl.ds(pl.multiple_of(group * PAIR, PAIR), PAIR)
        backward_head_prepare(cols, gm_ref, mixed2_ref, delta_ref)
        gqt_ref[...] = jnp.zeros_like(gqt_ref)

        @pl.loop(0, 2)
        def _(half):
            head = group * 2 + half
            for when, steps in ((3, ((0, 2), (1, 1))), (7, ((0, 3), (1, 2), (2, 1)))):

                @pl.when(head == when * heads // 12)
                def _(steps=steps):
                    advance(*steps)

            @pl.loop(0, source // block)
            def _(index):
                backward_block(
                    pl.ds(pl.multiple_of(index * block, block), block), cols, half, 0, None, q_ref, k_ref, v_ref, gm_ref,
                    lse_rows_ref[pl.ds(head, 1), :], delta_ref[pl.ds(half, 1), :], gk_ref, gv_ref, gqt_ref,
                )

        gq_ref[:, cols] = gqt_ref[...].T.astype(BF16)

    advance((1, 3), (2, 2), (3, 1))

    def memory_grad(rows):
        gmem_ref[rows, :] = dot(gk_ref[rows, :], ck_ref[...], 1, 1) + dot(gv_ref[rows, :], cv_ref[...], 1, 1)
        flipped_ref[:, rows] = memory_ref[rows, :].T

    moves.need(2, 12, 13)
    row_blocks(source, 256, memory_grad)
    moves.store(0)

    def memory_weights(rows):
        flipped = flipped_ref[rows, :source]
        dck_ref[rows, :] = dot(flipped, gk_ref[...]).astype(BF16)
        dcv_ref[rows, :] = dot(flipped, gv_ref[...]).astype(BF16)

    row_blocks(width, 192, memory_weights)
    moves.store(5, 6)
    moves.need(1, 3, 11, 10, 7)
    advance((2, 3), (3, 2), (0, 4))

    def first_grad(rows):
        value = first_ref[rows, :]
        flipped_ref[:, rows] = (value * rms(value) * gains_ref[1:2, :]).astype(BF16).T
        back = norm_back_rows(value, gains_ref[1:2, :], dot(gq_ref[rows, :], cq_ref[...], 1, 1))
        gfirst = back + gsecond_ref[rows, :]
        gfirst_ref[rows, :] = gfirst
        branch = gfirst.astype(BF16)
        branch_ref[rows, :] = branch
        gm1_ref[rows, :] = dot(branch, wo_ref[...], 1, 1).astype(BF16)

    row_blocks(length, 256, first_grad)
    moves.store(1, 2)
    advance((3, 3), (1, 4))

    def query_weights(rows):
        dcq_ref[rows, :] = dot(flipped_ref[rows, :], gq_ref[...]).astype(BF16)

    row_blocks(width, 192, query_weights)
    moves.store(4)

    def flip_mixed(rows):
        flipped_ref[:, rows] = mixed1_ref[rows, :].T

    row_blocks(length, block, flip_mixed)

    def out_weights(rows):
        dwo_ref[rows, :] = dot(flipped_ref[rows, :], branch_ref[...]).astype(BF16)

    row_blocks(width, 192, out_weights)
    moves.store(3)
    advance((2, 4), (3, 4))
    moves.finish()


def store_shares(ref, cols, value, start):
    if len(ref.shape) == 2:
        ref[pl.ds(start, value.shape[0]), cols] = value.astype(BF16)
    else:
        deep, high, wide, cores, rows, columns = ref.shape
        chunk = high * wide * cores * rows
        ref[lax.div(start, chunk), :, :, :, :, cols] = value.reshape(high, wide, cores, rows, value.shape[1]).astype(BF16)


TILE = 16


def fill_tiles(tiles_ref, gtable):
    deep, high, wide, cores, rows, lanes = tiles_ref.shape
    heads, buckets = gtable.shape
    tiles_ref[...] = jnp.zeros_like(tiles_ref)

    @pl.loop(0, deep)
    def _(z):
        shape = (high, wide, cores, heads, buckets)
        tiles_ref[z, :, :, :, :heads, :buckets] = jnp.broadcast_to(gtable, shape)


REST = 5


def self_parts(columns):
    half, third = columns // 2, columns // 3
    return (0, half), (half, third), (half + third, columns - half - third)


def self_pieces(columns):
    first = [(0, 0, columns, "xy"), (1, 0, columns, "yx")]
    rest = [(2, 0, columns, "xy"), (3, 0, columns, "yx")] + split_columns(4, columns)
    parts = []
    for number, (start, count) in enumerate(self_parts(columns)):
        orders = ("xy", "yx", "xy") if number % 2 else ("yx", "xy", "yx")
        parts.append([(REST + array, start, count, orders[array]) for array in range(3)])
    pieces, groups = [], []
    for group in (first, rest, *parts, [(REST + 3, 0, SUB, "xy")]):
        groups.append(range(len(pieces), len(pieces) + len(group)))
        pieces += group
    return pieces, groups


SELF_INS = 12


def self_backward_kernel(limit_ref, table_ref, map_ref, *refs, band, heads, plan):
    count = REST if plan else 0
    ins, refs = refs[:SELF_INS], refs[SELF_INS:]
    sources, refs = refs[:count], refs[count:]
    gtokens_ref, refs = refs[0], refs[1:]
    if plan:
        outs, refs = refs[: REST + 3], refs[REST + 3 :]
        gtable_ref, refs = refs[0], refs[1:]
    else:
        gtable_ref, dwq_ref, dwk_ref, dwv_ref, *refs = refs
    moves = Moves(ins, (), refs)
    (
        tokens_ref, gains_ref, lse_ref, q_ref, k_ref, v_ref, mixed_ref, gm_ref, gfirst_ref, wq_ref, wk_ref, wv_ref,
    ) = moves.held_ins
    refs = moves.rest
    (
        bias_ref, causal_ref, two_ref, flipped_ref, lse_rows_ref, delta_ref, gq_ref, gk_ref, gv_ref, gqt_ref,
        causal_sum_ref, two_sum_ref, sums_ref, *refs,
    ) = refs
    length, width = tokens_ref.shape
    block = 256
    groups = heads // 2
    if plan:
        sizes, pieces, (first, rest, early, middle, late, table) = plan
        dwq_ref, dwk_ref, dwv_ref, tiles_ref, tile_ref, *refs = refs
        scatter = Scatter(
            Place(sizes), pieces, (*sources, dwq_ref, dwk_ref, dwv_ref, tiles_ref), [False] * REST + [True] * 4,
            (*outs, tile_ref), refs[:-3], *refs[-3:],
        )
        scatter.place.greet()
    moves.load(*range(SELF_INS))
    bias_ref[...] = bias_rows(table_ref, map_ref, band, "keys")
    if plan:
        scatter.place.meet()
        scatter.advance(first, 0)
        scatter.advance(rest, 0)
    moves.need(0, 1, 2)
    lse_rows_ref[...] = lse_ref[...].T
    gk_ref[...] = jnp.zeros_like(gk_ref)
    gv_ref[...] = jnp.zeros_like(gv_ref)
    sums_ref[...] = jnp.zeros_like(sums_ref)

    def flip_normed(rows):
        value = tokens_ref[rows, :].astype(F32)
        flipped_ref[:, rows] = (value * rms(value) * gains_ref[0:1, :]).astype(BF16).T

    row_blocks(length, block, flip_normed)
    moves.need(*range(3, SELF_INS))

    def group_step(group):
        cols = pl.ds(pl.multiple_of(group * PAIR, PAIR), PAIR)
        backward_head_prepare(cols, gm_ref, mixed_ref, delta_ref)
        gqt_ref[...] = jnp.zeros_like(gqt_ref)

        @pl.loop(0, 2)
        def _(half):
            head = group * 2 + half
            if plan:
                for when, numbers, phase in ((1, first, 1), (4, rest, 1), (5, first, 2), (8, first, 3), (9, early, 1), (11, rest, 2)):

                    @pl.when(head == when * heads // 12)
                    def _(numbers=numbers, phase=phase):
                        scatter.advance(numbers, phase)

            fill_bands(head, bias_ref, band, causal_ref, two_ref)
            causal_sum_ref[...] = jnp.zeros_like(causal_sum_ref)
            two_sum_ref[...] = jnp.zeros_like(two_sum_ref)
            self_backward_head(
                head, limit_ref[0], q_ref, k_ref, v_ref, gm_ref, mixed_ref, lse_rows_ref, delta_ref,
                causal_ref, two_ref, band, gk_ref, gv_ref, gqt_ref, causal_sum_ref, two_sum_ref,
            )
            sums_ref[pl.ds(head, 1), : band.causal] = fold(causal_sum_ref[...])
            sums_ref[pl.ds(head, 1), band.causal :] = fold(two_sum_ref[...])

        gq_ref[:, cols] = gqt_ref[...].T.astype(BF16)

    rows_each = width // (sizes["dp"] // (sizes["fsdp"] // 2)) if plan else block

    def weights(cols):
        @pl.loop(0, width // rows_each)
        def _(index):
            start = pl.multiple_of(index * rows_each, 64)
            flipped = flipped_ref[pl.ds(start, rows_each), :]
            for target, grad in ((dwq_ref, gq_ref), (dwk_ref, gk_ref), (dwv_ref, gv_ref)):
                store_shares(target, cols, dot(flipped, grad[:, cols]), start)

    parts = [pl.ds(start, count) for start, count in self_parts(width)]

    @pl.loop(0, groups)
    def _(group):
        if plan:

            @pl.when(group == groups // 2)
            def _():
                weights(parts[0])
                scatter.advance(early, 0)

            @pl.when(group == groups - 1)
            def _():
                weights(parts[1])
                scatter.advance(middle, 0)

        group_step(group)

    if plan:
        weights(parts[2])
        scatter.advance(late, 0)
        scatter.advance(early, 2)
        scatter.advance(rest, 3)
    else:
        for part in parts:
            weights(part)
    hot, unused = one_hot(map_ref, band, "keys")
    gtable = exact_dot(sums_ref[...], hot, 1, 1)
    if plan:
        fill_tiles(tiles_ref, gtable)
        scatter.advance(table, 0)
        scatter.advance(middle, 1)
        scatter.advance(late, 1)

    def tokens_grad(rows):
        value = tokens_ref[rows, :].astype(F32)
        grad = dot(gq_ref[rows, :], wq_ref[...], 1, 1)
        grad += dot(gk_ref[rows, :], wk_ref[...], 1, 1)
        grad += dot(gv_ref[rows, :], wv_ref[...], 1, 1)
        gtokens_ref[rows, :] = norm_back_rows(value, gains_ref[0:1, :], grad) + gfirst_ref[rows, :]

    if plan:
        steps = (
            ((table, 1), (early, 3), (first, 4)),
            ((middle, 2), (late, 2), (table, 2)),
            ((middle, 3), (rest, 4)),
            ((late, 3), (table, 3)),
        )

        @pl.loop(0, len(steps))
        def _(step):
            for start in range(0, length // len(steps), block):
                start = step * (length // len(steps)) + start
                tokens_grad(pl.ds(pl.multiple_of(start, block), block))
            for number, advances in enumerate(steps):

                @pl.when(step == number)
                def _(advances=advances):
                    for numbers, phase in advances:
                        scatter.advance(numbers, phase)

        scatter.advance(early, 4)
        scatter.advance(middle, 4)
        scatter.advance(late, 4)
        scatter.advance(table, 4)
        gtable_ref[...] = tile_ref[:heads, :NB]
    else:
        row_blocks(length, block, tokens_grad)
        gtable_ref[...] = gtable


def gain_grads(gains, weights, grads):
    results = []
    for gain, parts in zip(gains, ((0, 1, 2), (3,), (4, 5))):
        total = 0.0
        for part in parts:
            product = weights[part][...].astype(F32) * grads[part][...]
            total += exact_dot(jnp.ones((8, product.shape[1]), F32), product, 1, 1)
        results.append(total[0:1] / gain[...].astype(F32))
    return results


def hand_on_kernel(*refs, places, norms):
    count = len(places)
    shards, refs = refs[: len(norms) + 3], refs[len(norms) + 3 :]
    ins, (in_sem, out_sem) = refs[:count], refs[-2:]
    refs = refs[count:-2]
    held, outs, ggain_refs = refs[-count:], refs[: -count - 3], refs[-count - 3 : -count]
    loads = [pltpu.make_async_copy(ins[i], held[i], in_sem.at[i]) for i in range(count)]
    stores = []
    for i, (out, start) in enumerate(places):
        target = outs[out] if start is None else outs[out].at[:, start : start + ins[i].shape[1]]
        stores.append(pltpu.make_async_copy(held[i], target, out_sem.at[i]))
    for load in loads:
        load.start()
    for load, store in zip(loads, stores):
        load.wait()
        store.start()
    grads = []
    for number in norms:
        parts = [held[i][...] for i, (out, start) in enumerate(places) if out == number]
        grads.append(jnp.concatenate(parts, axis=1))
    for ref, value in zip(ggain_refs, gain_grads(shards[:3], shards[3:], grads)):
        ref[...] = value
    for store in stores:
        store.wait()


def hand_on(results, norms, gains, weights):
    arrays, places, shapes = [], [], []
    for number, result in enumerate(results):
        parts = result if isinstance(result, tuple) else (result,)
        start = 0
        for part in parts:
            arrays.append(part)
            places.append((number, start if len(parts) > 1 else None))
            start += part.shape[-1]
        shapes.append(jax.ShapeDtypeStruct(parts[0].shape[:-1] + (start,), parts[0].dtype))
    spec = pl.BlockSpec(memory_space=pl.ANY)
    here = pl.BlockSpec(memory_space=pltpu.VMEM)
    shards = [*[gain.reshape(1, -1) for gain in gains], *weights]
    *results, first, second, third = pl.pallas_call(
        functools.partial(hand_on_kernel, places=places, norms=norms),
        out_shape=shapes + [jax.ShapeDtypeStruct((1, gain.shape[0]), F32) for gain in gains],
        in_specs=[here] * len(shards) + [spec] * len(arrays),
        out_specs=[spec] * len(shapes) + [here] * 3,
        scratch_shapes=[pltpu.VMEM(a.shape, a.dtype) for a in arrays] + [pltpu.SemaphoreType.DMA((len(arrays),))] * 2,
        compiler_params=params(),
        name="hand_on",
    )(*shards, *arrays)
    return results, [ggain.reshape(-1) for ggain in (first, second, third)]


def upper_shapes(arrays):
    return [jax.ShapeDtypeStruct(a.shape, a.dtype) for a in arrays]


def vmem(*shapes):
    return [pltpu.VMEM(shape, dtype) for shape, dtype in shapes]


def params(**kw):
    return pltpu.CompilerParams(vmem_limit_bytes=60 * 1024 * 1024, **kw)


def per_device(
    inputs, encoded, out_grad, prefix, bucket_map, bias_table,
    norm_self, self_query, self_key, self_value, self_out,
    norm_cross, cross_query, cross_key, cross_value, cross_out,
    norm_feed, feed_gate, feed_up, feed_down,
):
    seqs, length, width = inputs.shape
    source = encoded.shape[1]
    heads = bias_table.shape[1]
    ff = feed_gate.shape[1]
    band = Band(length, length // 2)
    tokens = inputs.reshape(length, width)
    flipped_table = bias_table.T
    memory = encoded.reshape(source, width)
    gout = out_grad.reshape(length, width)
    gains_in = [norm_self, norm_cross, norm_feed]
    projections = [self_query, self_key, self_value, self_out, cross_query, cross_key, cross_value, cross_out]
    feeds = [feed_gate, feed_up, feed_down]
    sizes = dict(dp=lax.axis_size("dp"), fsdp=lax.axis_size("fsdp"))
    devices = sizes["dp"] * sizes["fsdp"]
    own = self_query.shape[0] % 8 == 0
    if own:
        pieces, groups = gather_pieces(self_query.shape[0], feed_down.shape[0])
        plan = (sizes, pieces, groups)
        copies = Gather.copies(sizes, pieces)
        shards = projections + feeds
    else:
        plan = None
        gains_in = [lax.all_gather(gain, AXES, axis=0, tiled=True) for gain in gains_in]
        shards = [lax.all_gather(shard, AXES, axis=0, tiled=True) for shard in projections]
        gate_full, up_full, down = [lax.all_gather(shard, AXES, axis=0, tiled=True) for shard in feeds]
    gains_in = [gain.reshape(1, -1) for gain in gains_in]

    remote = pl.BlockSpec(memory_space=pl.ANY)
    scalar = pl.BlockSpec(memory_space=pltpu.SMEM)

    def full(shape):
        return pl.BlockSpec(shape, lambda *_: (0,) * len(shape))

    def like(shape, dtype):
        return jax.ShapeDtypeStruct(shape, dtype)

    act = like((length, width), BF16)
    mem = like((source, width), BF16)
    act32 = like((length, width), F32)
    lse_shape = like((length, SUB), F32)
    gain_shape = like((8, width), F32)
    outs = [gain_shape, act, act, act, act, lse_shape, act32, act, mem, mem, act, lse_shape, act32]
    gathered_shapes = []
    if own:
        chips, cores = grid_of(sizes)[:3], grid_of(sizes)[3]
        shapes = [shard.shape for shard in projections]
        shapes += [(feed_gate.shape[0], ff // 2)] * 2 + [feed_down.shape] + [(feed_gate.shape[0], ff // 2)] * 2
        gathered_shapes = [like(chips + (cores * shape[0], shape[1]), BF16) for shape in shapes]
        gathered_shapes.append(like(chips + (cores * 8, SUB), F32))
    forward_in = (tokens, memory, flipped_table, bucket_map, *gains_in)
    results = pl.pallas_call(
        functools.partial(forward_kernel, band=band, heads=heads, plan=plan),
        out_shape=gathered_shapes + outs,
        grid=(1,),
        in_specs=[scalar] + [full(a.shape) for a in forward_in]
        + ([full(a.shape) for a in shards] if own else [remote] * len(shards)),
        out_specs=[remote] * (len(gathered_shapes) + len(outs)),
        scratch_shapes=Moves.scratch(outs)
        + vmem(
            ((heads, band.width), F32), ((SUB, band.causal), F32), ((SUB, band.two_way), F32),
            ((ATTENTION, width, width), BF16), ((8, SUB), F32), ((devices, 8, SUB), F32),
        )
        + [pltpu.SemaphoreType.DMA((ATTENTION + 1,))]
        + ([pltpu.SemaphoreType.DMA((number,)) for number in (len(pieces), copies, copies)] if own else []),
        compiler_params=params(collective_id=0, has_side_effects=True) if own else params(),
        name="forward",
    )(prefix, *forward_in, *shards)
    attention = shards
    if own:
        gathered, results = results[:SHARDS], results[SHARDS:]
        attention = [part.reshape(width, width) for part in gathered[:ATTENTION]]
        gate_low, up_low = gathered[8].reshape(width, ff // 2), gathered[9].reshape(width, ff // 2)
        down = gathered[10].reshape(ff, width)
    gains, q1, k1, v1, mixed1, lse1, first, q2, k2, v2, mixed2, lse2, second = results

    grid = grid_of(sizes)

    def shares(grads):
        return [grad.reshape(grid + (grad.shape[0] // devices, grad.shape[1])) for grad in grads]

    def scatter_scratch(pieces, shapes, kept):
        count = Scatter.copies(sizes, pieces)
        return Scatter.scratch(sizes, pieces, shapes, kept) + [
            pltpu.SemaphoreType.DMA((number,)) for number in (len(pieces), count, count)
        ]

    if own:
        half = ff // 2
        share = feed_gate.shape[0]
        upper = gathered[11:13]
        gather_plan = [(0, 0, share, "zxy"), (1, 0, share, "zyx")]
        scatter_plan = [(0, 0, half, "xy"), (1, 0, half, "yx")]
        feed_in = (second, gout, gains, gate_low, up_low, down)
        feed_out = [act, act32, like((ff, width), BF16)]
        share_shapes = [like(grid + (share, half), BF16)] * 2
        grad_shapes = [like((share, half), F32)] * 2
        copies = Gather.copies(sizes, gather_plan)
        output, gsecond, ddown, *halves = pl.pallas_call(
            functools.partial(feed_exchange_kernel, plan=(sizes, gather_plan, scatter_plan)),
            out_shape=feed_out + share_shapes + grad_shapes + upper_shapes(upper),
            grid=(1,),
            in_specs=[remote] * (FEED_INS + 2),
            out_specs=[remote] * (FEED_OUTS + 2) + [full(o.shape) for o in grad_shapes] + [remote] * 2,
            scratch_shapes=Moves.scratch([*feed_in, *feed_out])
            + vmem(
                ((length, width), BF16), ((width, length), BF16), ((length, width), F32), ((length, width), F32),
                ((length, half), BF16), ((length, half), BF16), ((length, half), BF16),
                ((2, width, half), BF16), ((2, width, half), BF16),
                ((2,) + grid + (share, half), BF16), ((2,) + grid + (share, half), BF16),
            )
            + [pltpu.SemaphoreType.DMA((number,)) for number in (4, 2, len(gather_plan), copies, copies)]
            + scatter_scratch(scatter_plan, [(share, BF16)] * 2, [True, True]),
            input_output_aliases={FEED_INS: FEED_OUTS + 4, FEED_INS + 1: FEED_OUTS + 5},
            compiler_params=params(collective_id=3, has_side_effects=True),
            name="feed",
        )(*feed_in, *upper)
        high_shares, low_grads = halves[:2], halves[2:4]
    else:
        fblock = min(1024, ff)
        feed_out = [
            act, act32, like((width, ff), BF16), like((width, ff), BF16), like((ff, width), BF16)
        ]
        output, gsecond, dgate, dup, ddown = pl.pallas_call(
            feed_kernel,
            out_shape=feed_out,
            grid=(ff // fblock,),
            in_specs=[full(second.shape), full(gout.shape), full(gains.shape)]
            + [
                pl.BlockSpec((width, fblock), lambda i: (0, i)),
                pl.BlockSpec((width, fblock), lambda i: (0, i)),
                pl.BlockSpec((fblock, width), lambda i: (i, 0)),
            ],
            out_specs=[full(o.shape) for o in feed_out[:2]]
            + [
                pl.BlockSpec((width, fblock), lambda i: (0, i)),
                pl.BlockSpec((width, fblock), lambda i: (0, i)),
                pl.BlockSpec((fblock, width), lambda i: (i, 0)),
            ],
            scratch_shapes=vmem(
                ((length, width), BF16), ((width, length), BF16), ((length, width), F32), ((length, width), F32),
                ((length, fblock), BF16), ((length, fblock), BF16), ((length, fblock), BF16),
            ),
            compiler_params=params(),
            name="feed",
        )(second, gout, gains, gate_full, up_full, down)

    square = like((width, width), BF16)
    cross_shapes = [like((source, width), F32), act32, act] + [square] * 5
    cross_in = (gsecond, first, memory, gains, q2, k2, v2, mixed1, mixed2, lse2)
    cross_scratch = vmem(
        ((length, width), BF16), ((length, width), BF16), ((width, length), BF16), ((SUB, length), F32),
        ((8, length), F32), ((length, width), BF16), ((source, width), BF16), ((source, width), BF16),
        ((PAIR, length), F32),
    )
    plan, sources, gate_shapes, scratch = None, [], [], []
    if own:
        sources = high_shares + shares([ddown])
        quarter, third = half // 2, width // 3
        pieces = [(0, 0, quarter, "xy"), (1, 0, quarter, "yx"), (0, quarter, quarter, "xy"), (1, quarter, quarter, "yx")]
        pieces += [(2, 0, third, "xy"), (2, third, third, "yx")]
        pieces += [(2, 2 * third, third // 2, "xy"), (2, 2 * third + third // 2, third // 2, "yx")]
        plan = (sizes, pieces)
        gate_shapes = [like(part.shape[-2:], F32) for part in sources]
        scratch = scatter_scratch(pieces, [(part.shape[-2], BF16) for part in sources], [False] * 3)
    moved = Moves.scratch([*cross_in, *attention[3:], *cross_shapes])
    gmem, gfirst, gm1, dwo, dcq, dck, dcv, dco, *feed_grads = pl.pallas_call(
        functools.partial(cross_backward_kernel, heads=heads, plan=plan),
        out_shape=cross_shapes + gate_shapes,
        grid=(1,),
        in_specs=[remote] * (CROSS_INS + len(sources)),
        out_specs=[remote] * CROSS_OUTS + [full(o.shape) for o in gate_shapes],
        scratch_shapes=moved + cross_scratch + scratch,
        compiler_params=params(collective_id=1, has_side_effects=True) if own else params(),
        name="cross_backward",
    )(*cross_in, *attention[3:], *sources)

    self_in = (flipped_table, bucket_map)
    self_moved = (tokens, gains, lse1, q1, k1, v1, mixed1, gm1, gfirst, *attention[:3])
    self_scratch = vmem(
        ((heads, band.width), F32), ((SUB, band.causal), F32), ((SUB, band.two_way), F32), ((width, length), BF16),
        ((SUB, length), F32), ((8, length), F32), ((length, width), BF16), ((length, width), BF16),
        ((length, width), BF16), ((PAIR, length), F32), ((SUB, band.causal), F32), ((SUB, band.two_way), F32),
        ((heads, band.width), F32),
    )
    plan, sources, scratch = None, [], []
    table_shape = like((heads, NB), F32)
    if own:
        sources = shares([dco, dwo, dcq, dck, dcv])
        pieces, groups = self_pieces(width)
        plan = (sizes, pieces, groups)
        share = width // devices
        kept = [False] * REST + [True] * 4
        shapes = [(part.shape[-2], BF16) for part in sources] + [(share, BF16)] * 3 + [(TILE, F32)]
        self_shapes = [act32] + [like(part.shape[-2:], F32) for part in sources] + [like((share, width), F32)] * 3
        self_shapes += [table_shape]
        scratch = vmem(*[(grid + (share, width), BF16)] * 3, (grid + (TILE, SUB), F32), ((TILE, SUB), F32))
        scratch += scatter_scratch(pieces, shapes, kept)
    else:
        self_shapes = [act32, table_shape] + [square] * 3
    gtokens, *grads = pl.pallas_call(
        functools.partial(self_backward_kernel, band=band, heads=heads, plan=plan),
        out_shape=self_shapes,
        grid=(1,),
        in_specs=[scalar] + [full(a.shape) for a in self_in] + [remote] * (SELF_INS + len(sources)),
        out_specs=[full(o.shape) for o in self_shapes],
        scratch_shapes=Moves.scratch(self_moved) + self_scratch + scratch,
        compiler_params=params(collective_id=2, has_side_effects=True) if own else params(),
        name="self_backward",
    )(prefix, *self_in, *self_moved, *sources)

    gain_parts = (norm_self, norm_cross, norm_feed)
    weight_parts = (self_query, self_key, self_value, cross_query, feed_gate, feed_up)
    if own:
        results = [gtokens, output, gmem, (low_grads[0], feed_grads[0]), (low_grads[1], feed_grads[1]), feed_grads[2]]
        results, ggains = hand_on([*results, *grads], (11, 12, 13, 8, 3, 4), gain_parts, weight_parts)
        gtokens, output, gmem, dgate, dup, ddown, dco, dwo, dcq, dck, dcv, dwq, dwk, dwv, table_grad = results
    else:
        gtable, dwq, dwk, dwv = grads
        table_grad = lax.psum(gtable, AXES)

        def scatter(parts):
            return lax.psum_scatter(jnp.concatenate(parts, axis=1), AXES, scatter_dimension=0, tiled=True).astype(F32)

        dgate, dup = jnp.split(scatter([dgate, dup]), 2, axis=1)
        ddown = scatter([ddown])
        squares = scatter([dwq, dwk, dwv, dwo, dcq, dck, dcv, dco])
        dwq, dwk, dwv, dwo, dcq, dck, dcv, dco = jnp.split(squares, 8, axis=1)
        parts = gain_grads([gain.reshape(1, -1) for gain in gain_parts], weight_parts, (dwq, dwk, dwv, dcq, dgate, dup))
        ggains = [part.reshape(-1) for part in parts]
    return (
        output.reshape(inputs.shape),
        gtokens.reshape(inputs.shape),
        gmem.reshape(encoded.shape),
        table_grad.T,
        ggains[0], dwq, dwk, dwv, dwo,
        ggains[1], dcq, dck, dcv, dco,
        ggains[2], dgate, dup, ddown,
    )


def solution(mesh):
    rows = P(AXES, None)
    gain = P(AXES)
    block = P(AXES, None, None)
    return jax.shard_map(
        per_device,
        mesh=mesh,
        in_specs=(block, block, block, gain, P(), P())
        + (gain, rows, rows, rows, rows)
        + (gain, rows, rows, rows, rows)
        + (gain, rows, rows, rows),
        out_specs=(block, block, block, P())
        + (gain, rows, rows, rows, rows)
        + (gain, rows, rows, rows, rows)
        + (gain, rows, rows, rows),
        check_vma=False,
    )
```

```python
import functools

import jax
import jax.numpy as jnp
from jax import lax
from jax.experimental import pallas as pl
from jax.experimental.pallas import tpu as pltpu
from jax.sharding import PartitionSpec as P

DH = 64
NB = 32
PAIR = 2 * DH
SUB = 128
NEG = -1e30
F32 = jnp.float32
BF16 = jnp.bfloat16
AXES = ("dp", "fsdp")


def dot(a, b, ca=1, cb=0):
    return lax.dot_general(a, b, (((ca,), (cb,)), ((), ())), preferred_element_type=F32)


def exact_dot(a, b, ca=1, cb=0):
    return lax.dot_general(
        a,
        b,
        (((ca,), (cb,)), ((), ())),
        preferred_element_type=F32,
        precision=lax.Precision.HIGHEST,
    )


def rms(value):
    return lax.rsqrt(jnp.mean(value * value, axis=-1, keepdims=True) + 1e-06)


MESH = pl.DeviceIdType.MESH
EVERY = slice(None)


class Place:
    def __init__(self, sizes):
        self.grid = sizes
        self.sizes = grid_of(sizes)
        across, inner = lax.axis_index("dp"), lax.axis_index("fsdp")
        deep, high, wide, cores = self.sizes
        self.at = {
            "z": lax.div(across, high),
            "y": lax.rem(across, high),
            "x": lax.div(inner, cores),
            "c": lax.rem(inner, cores),
        }

    def device(self, **moved):
        at = {**self.at, **moved}
        deep, high, wide, cores = self.sizes
        return (at["z"] * high + at["y"], at["x"] * cores + at["c"])

    def size(self, axis):
        return self.sizes["zyxc".index(axis)]

    def others(self, axis):
        size = self.size(axis)
        return [lax.rem(self.at[axis] + step, size) for step in range(1, size)]

    def greet(self):
        barrier = pltpu.get_barrier_semaphore()
        for peer in self.peers():
            pl.semaphore_signal(barrier, inc=1, device_id=peer, device_id_type=MESH)

    def meet(self):
        pl.semaphore_wait(pltpu.get_barrier_semaphore(), len(self.peers()))

    def peers(self):
        return [self.device(**{axis: other}) for axis in "zyxc" for other in self.others(axis)]


def grid_of(sizes):
    wide = sizes["fsdp"] // 2
    return (sizes["dp"] // wide, wide, wide, 2)


class Moves:
    def __init__(self, ins, outs, refs):
        count = len(ins) + len(outs)
        self.ins, self.outs = ins, outs
        self.held, self.sem, self.rest = refs[:count], refs[count], refs[count + 1 :]
        self.held_ins, self.held_outs = self.held[: len(ins)], self.held[len(ins) :]
        self.stored = []

    @staticmethod
    def scratch(arrays):
        return [pltpu.VMEM(a.shape, a.dtype) for a in arrays] + [pltpu.SemaphoreType.DMA((len(arrays),))]

    def copy(self, number):
        if number < len(self.ins):
            return pltpu.make_async_copy(self.ins[number], self.held[number], self.sem.at[number])
        return pltpu.make_async_copy(self.held[number], self.outs[number - len(self.ins)], self.sem.at[number])

    def load(self, *numbers):
        for number in numbers:
            self.copy(number).start()

    def need(self, *numbers):
        for number in numbers:
            self.copy(number).wait()

    def store(self, *numbers):
        for number in numbers:
            self.copy(len(self.ins) + number).start()
            self.stored.append(len(self.ins) + number)

    def finish(self):
        for number in self.stored:
            self.copy(number).wait()


class Gather:
    PHASES = 4

    def __init__(self, place, pieces, shards, outs, local_sem, send_sem, recv_sem):
        self.place, self.pieces, self.shards, self.outs = place, pieces, shards, outs
        self.local_sem, self.send_sem, self.recv_sem = local_sem, send_sem, recv_sem

    @staticmethod
    def each(sizes):
        grid = grid_of(sizes)
        return sum(size - 1 for size in grid[:3]) + max(grid[:3])

    @staticmethod
    def copies(sizes, pieces):
        return len(pieces) * Gather.each(sizes)

    def view(self, piece, held):
        array, first, rows, order = piece
        start = self.place.at["c"] * (self.outs[array].shape[3] // 2) + first
        where = [held.get(axis, EVERY) for axis in "zyx"]
        return self.outs[array].at[(*where, pl.ds(pl.multiple_of(start, 8), rows), EVERY)]

    def phase(self, number, phase, core):
        piece = self.pieces[number]
        place, at = self.place, self.place.at
        array, first, rows, order = piece
        slot = number * self.each(place.grid) + sum(place.size(axis) - 1 for axis in order[:phase])
        copies = []

        def send(source, target, **moved):
            copies.append(
                pltpu.make_async_remote_copy(
                    source,
                    target,
                    self.send_sem.at[slot + len(copies)],
                    self.recv_sem.at[slot + len(copies)],
                    device_id=place.device(**moved),
                    device_id_type=MESH,
                )
            )

        other_core = place.others("c")[0]
        last = order[2]
        if core:
            slot = number * self.each(place.grid) + sum(place.size(axis) - 1 for axis in order)
            if phase == 2:
                part = self.view(piece, {last: at[last]})
                send(part, part, c=other_core)
            else:
                slot += 1
                for other in place.others(last):
                    part = self.view(piece, {last: other})
                    send(part, part, c=other_core)
            return copies
        axis = order[phase]
        target = self.view(piece, {later: at[later] for later in order[phase:]})
        source = self.shards[array].at[pl.ds(first, rows), :] if phase == 0 else target
        for other in place.others(axis):
            send(source, target, **{axis: other})
        if phase == 0:
            copies.append(pltpu.make_async_copy(source, target, self.local_sem.at[number]))
        return copies

    def advance(self, numbers, phase):
        for number in numbers:
            waits, starts = [], []
            if 0 < phase < 4:
                waits = self.phase(number, phase - 1, False)
            if phase < 3:
                starts = self.phase(number, phase, False)
            if phase in (2, 3):
                starts += self.phase(number, phase, True)
            if phase == 4:
                waits = self.phase(number, 2, True) + self.phase(number, 3, True)
            for copy in waits:
                copy.wait()
            for copy in starts:
                copy.start()

    def settle(self, numbers):
        for number in numbers:
            for copy in self.phase(number, 0, False):
                copy.wait()

    def resume(self, numbers):
        for number in numbers:
            for copy in self.phase(number, 1, False):
                copy.start()


class Scatter:
    PHASES = 4

    def __init__(self, place, pieces, sources, kept, outs, buffers, load_sem, send_sem, recv_sem):
        self.place, self.pieces, self.sources, self.kept, self.outs = place, pieces, sources, kept, outs
        self.buffers, self.load_sem, self.send_sem, self.recv_sem = buffers, load_sem, send_sem, recv_sem

    @staticmethod
    def copies(sizes, pieces):
        return len(pieces) * sum(size - 1 for size in grid_of(sizes))

    @staticmethod
    def scratch(sizes, pieces, shapes, kept):
        deep, high, wide, cores = grid_of(sizes)
        buffers = []
        for source, first, columns, order in pieces:
            rows, dtype = shapes[source]
            near, far = (wide, high) if order == "xy" else (high, wide)
            block = (rows, columns)
            shapes_here = [(deep, high, wide) + block, (near - 1, deep, far) + block, (far - 1, deep) + block, (deep,) + block]
            if not kept[source]:
                shapes_here.append((deep, high, wide) + block)
            buffers += [pltpu.VMEM(shape, dtype) for shape in shapes_here]
        return buffers

    def buffer(self, number, which):
        place = sum(4 if self.kept[piece[0]] else 5 for piece in self.pieces[:number])
        return self.buffers[place + which]

    def half(self, number, core):
        source, first, columns, order = self.pieces[number]
        return self.sources[source].at[:, :, :, core, :, pl.ds(first, columns)]

    def load(self, number):
        return pltpu.make_async_copy(self.half(number, self.place.at["c"]), self.buffer(number, 4), self.load_sem.at[number])

    def phase(self, number, phase):
        place = self.place
        at = place.at
        deep, high, wide, cores = place.sizes
        order = self.pieces[number][3]
        base = number * sum(size - 1 for size in place.sizes)
        axis = ("c" + order + "z")[phase]
        skip = sum(place.size(before) - 1 for before in ("c" + order + "z")[:phase])
        sums = self.buffer(number, 0)
        copies = []
        for step, other in enumerate(place.others(axis)):
            if phase == 0:
                source, target = self.half(number, other), sums
            elif phase == 3:
                source, target = sums.at[other, at["y"], at["x"]], self.buffer(number, 3).at[at["z"]]
            else:
                target = self.buffer(number, phase).at[step]
                y, x = (other, EVERY) if axis == "y" else (EVERY, other)
                if phase == 2:
                    y, x = (other, at["x"]) if axis == "y" else (at["y"], other)
                source = sums.at[:, y, x]
            slot = base + skip + step
            copies.append(
                pltpu.make_async_remote_copy(
                    source,
                    target,
                    self.send_sem.at[slot],
                    self.recv_sem.at[slot],
                    device_id=place.device(**{axis: other}),
                    device_id_type=MESH,
                )
            )
        return copies

    def absorb(self, number, phase):
        source, first, columns, order = self.pieces[number]
        at = self.place.at
        deep = self.place.sizes[0]
        sums = self.buffer(number, 0)
        if phase == 3:
            slots = self.buffer(number, 3)
            slots[at["z"]] = sums[at["z"], at["y"], at["x"]]
            total = slots[0].astype(F32)
            for slot in range(1, deep):
                total += slots[slot].astype(F32)
            self.outs[source][:, first : first + columns] = total
            return

        @pl.loop(0, deep)
        def _(z):
            if phase == 0:
                own = self.sources[source].at[z, :, :, at["c"], :, pl.ds(first, columns)] if self.kept[source] else self.buffer(number, 4).at[z]
                view, parts = sums.at[z], [own[...]]
            else:
                came = self.buffer(number, phase)
                parts = [came[step, z] for step in range(came.shape[0])]
                if phase == 1:
                    view = sums.at[z, :, at["x"]] if order[0] == "x" else sums.at[z, at["y"]]
                else:
                    view = sums.at[z, at["y"], at["x"]]
            if len(parts) == 1:
                view[...] = view[...] + parts[0]
            else:
                total = view[...].astype(F32)
                for part in parts:
                    total += part.astype(F32)
                view[...] = total.astype(view.dtype)

    def advance(self, numbers, phase):
        for number in numbers:
            if phase > 0:
                for copy in self.phase(number, phase - 1):
                    copy.wait()
                if phase == 1 and not self.kept[self.pieces[number][0]]:
                    self.load(number).wait()
                self.absorb(number, phase - 1)
            elif not self.kept[self.pieces[number][0]]:
                self.load(number).start()
            if phase < self.PHASES:
                for copy in self.phase(number, phase):
                    copy.start()


class Band:
    def __init__(self, length, reach):
        self.reach = reach
        self.causal = length + reach
        self.two_way = 2 * reach
        self.width = self.causal + self.two_way
        self.query_zero = length - SUB
        self.query_zero_two = reach - SUB
        self.key_zero = reach - SUB

    def distances(self, rows):
        causal = lax.broadcasted_iota(jnp.int32, (1, self.causal), 1)
        two_way = lax.broadcasted_iota(jnp.int32, (1, self.two_way), 1)
        if rows == "queries":
            causal, two_way = self.query_zero - causal, self.query_zero_two - two_way
            return (
                jnp.where(causal <= -self.reach, causal + self.causal, causal),
                jnp.where(two_way <= -self.reach, two_way + self.two_way, two_way),
            )
        causal, two_way = causal - self.key_zero, two_way - self.key_zero
        return (
            jnp.where(causal >= self.causal - self.reach, causal - self.causal, causal),
            jnp.where(two_way >= self.reach, two_way - self.two_way, two_way),
        )


def one_hot(map_ref, band, rows):
    bucket = lax.broadcasted_iota(jnp.int32, (NB, 1), 0)

    def edges(row, number):
        entries = map_ref[row : row + 1, :]
        below = jnp.sum((entries < number).astype(jnp.int32), axis=1, keepdims=True)
        return below, below + jnp.sum((entries == number).astype(jnp.int32), axis=1, keepdims=True)

    causal, two_way = band.distances(rows)
    low, high = edges(0, bucket)
    one = (causal >= low) & (causal < high)
    ahead = bucket >= NB // 2
    low, high = edges(1, jnp.where(ahead, bucket - NB // 2, bucket))
    apart = jnp.abs(two_way)
    two = (apart >= low) & (apart < high) & ((two_way < 0) == ahead)
    return jnp.concatenate([jnp.where(one, 1.0, 0.0), jnp.where(two, 1.0, 0.0)], axis=1), causal


def spread(row, width):
    return pltpu.roll(jnp.broadcast_to(row, (SUB, width)), 0, 1, stride=1, stride_axis=0)


def fold(band):
    width = band.shape[1]
    half = SUB // 2
    while half >= 8:
        band = band[:half] + pltpu.roll(band[half:], width - half, 1)
        half //= 2
    row = lax.broadcasted_iota(jnp.int32, band.shape, 0)
    for bit in (4, 2, 1):
        band = jnp.where((row & bit) != 0, pltpu.roll(band, width - bit, 1), band)
    return jnp.sum(band, axis=0, keepdims=True)


def fill_bands(head, bias_ref, band, causal_ref, two_ref):
    row = bias_ref[pl.ds(head, 1), :]
    causal_ref[...] = spread(row[:, : band.causal], band.causal)
    two_ref[...] = spread(row[:, band.causal :], band.two_way)


def bias_rows(table_ref, map_ref, band, rows):
    hot, causal = one_hot(map_ref, band, rows)
    bias = dot(table_ref[...], hot.astype(BF16))
    return jnp.concatenate([jnp.where(causal < 0, NEG, bias[:, : band.causal]), bias[:, band.causal :]], axis=1)


def head_cols(head):
    group = head // 2
    return pl.ds(pl.multiple_of(group * PAIR, PAIR), PAIR), head % 2


def pick_lanes(half):
    return lax.broadcasted_iota(jnp.int32, (1, PAIR), 1) // DH == half


def soft_rows(scores):
    high = jnp.max(scores, axis=-1, keepdims=True)
    weights = jnp.exp(scores - high)
    total = jnp.sum(weights, axis=-1, keepdims=True)
    return weights.astype(BF16), total, high + jnp.log(total)


def store_head(mixed_ref, lse_ref, rows, cols, head, half, out, total, lse):
    pick = pick_lanes(half)
    mixed_ref[rows, cols] = jnp.where(pick, (out / total).astype(BF16), mixed_ref[rows, cols])
    lane = lax.broadcasted_iota(jnp.int32, (1, lse_ref.shape[1]), 1)
    lse_ref[rows, :] = jnp.where(lane == head, lse, lse_ref[rows, :])


def self_forward_head(head, limit, q_ref, k_ref, v_ref, causal_ref, two_ref, band, mixed_ref, lse_ref):
    length = q_ref.shape[0]
    cols, half = head_cols(head)
    pick = pick_lanes(half)
    block = 256
    for start in range(0, length, block):
        keys = max(start + block, band.reach)
        rows = pl.ds(start, block)
        query = jnp.where(pick, q_ref[rows, cols], 0)
        scores = dot(query, k_ref[pl.ds(0, keys), cols], 1, 1)
        parts = []
        for first in range(start, start + block, SUB):
            at = band.query_zero - first
            bias = causal_ref[:, at : at + keys]
            if start < band.reach:
                at = band.query_zero_two - first
                two = two_ref[:, at : at + keys]
                inside = (first + lax.broadcasted_iota(jnp.int32, (SUB, keys), 0) < limit) & (
                    lax.broadcasted_iota(jnp.int32, (SUB, keys), 1) < limit
                )
                bias = jnp.where(inside, two, bias)
            parts.append(bias)
        weights, total, lse = soft_rows(scores + jnp.concatenate(parts, axis=0))
        out = dot(weights, v_ref[pl.ds(0, keys), cols])
        store_head(mixed_ref, lse_ref, rows, cols, head, half, out, total, lse)


def cross_forward_head(head, q_ref, k_ref, v_ref, mixed_ref, lse_ref):
    length = q_ref.shape[0]
    cols, half = head_cols(head)
    pick = pick_lanes(half)
    block = 256
    for start in range(0, length, block):
        rows = pl.ds(start, block)
        query = jnp.where(pick, q_ref[rows, cols], 0)
        weights, total, lse = soft_rows(dot(query, k_ref[:, cols], 1, 1))
        out = dot(weights, v_ref[:, cols])
        store_head(mixed_ref, lse_ref, rows, cols, head, half, out, total, lse)


def row_blocks(count, block, step):
    @pl.loop(0, count // block)
    def _(index):
        step(pl.ds(pl.multiple_of(index * block, block), block))


def gain_rows(gathered, width):
    devices = gathered.shape[0]
    share = width // devices
    lane = lax.broadcasted_iota(jnp.int32, (SUB, width), 1)
    select = jnp.where(lax.rem(lane, share) == lax.broadcasted_iota(jnp.int32, (SUB, width), 0), 1.0, 0.0)
    first = share * lax.broadcasted_iota(jnp.int32, (devices, width), 0)
    lane = lax.broadcasted_iota(jnp.int32, (devices, width), 1)
    own = (lane >= first) & (lane < first + share)
    rows = []
    for number in range(8):
        spread_out = exact_dot(gathered[:, number, :], select)
        rows.append(jnp.sum(jnp.where(own, spread_out, 0.0), axis=0, keepdims=True))
    return jnp.concatenate(rows, axis=0)


ATTENTION = 8
SHARDS = 14


def gather_pieces(rows, down_rows):
    head, tail = rows // 3 // 8 * 8, rows - rows // 3 // 8 * 8
    half = down_rows // 2
    table = {
        "qk": [(0, 0, rows, "zxy"), (1, 0, rows, "zyx"), (13, 0, 8, "zxy")],
        "v": [(2, 0, head, "xzy"), (2, head, tail, "yzx")],
        "out": [(3, 0, rows, "zxy"), (4, 0, rows, "zyx"), (7, 0, tail, "zxy"), (7, tail, head, "zyx")],
        "memory": [(5, 0, rows, "xzy"), (6, 0, rows, "yzx")],
        "gate": [(8, 0, rows, "zxy"), (9, 0, rows, "zyx")],
        "down": [(10, 0, half, "xzy"), (10, half, half, "yzx")],
        "upper": [(11, 0, rows, "zxy"), (12, 0, rows, "zyx")],
    }
    pieces, groups = [], {}
    for name, group in table.items():
        groups[name] = range(len(pieces), len(pieces) + len(group))
        pieces += group
    return pieces, groups


FORWARD_OUTS = 13


def forward_kernel(
    limit_ref, tokens_ref, memory_ref, table_ref, map_ref, gain1_ref, gain2_ref, gain3_ref, *refs, band, heads, plan,
):
    count = ATTENTION + 3 if plan else ATTENTION
    shards, refs = refs[:count], refs[count:]
    if plan:
        gathered, refs = refs[:SHARDS], refs[SHARDS:]
    else:
        gathered = shards
    moves = Moves((), refs[:FORWARD_OUTS], refs[FORWARD_OUTS:])
    (
        gains_ref, q1_ref, k1_ref, v1_ref, mixed1_ref, lse1_ref, first_ref,
        q2_ref, k2_ref, v2_ref, mixed2_ref, lse2_ref, second_ref,
    ) = moves.held_outs
    bias_ref, causal_ref, two_ref, weights_ref, share_ref, tile_ref, load_sem, *gather_sems = moves.rest
    length, width = tokens_ref.shape
    if plan:
        sizes, pieces, groups = plan
        place = Place(sizes)
        columns = gathered[8].shape[-1]
        halves = [[ref.at[:, start : start + columns] for ref in shards[8:10]] for start in (0, columns)]
        parts = (*shards[:8], *halves[0], shards[10], *halves[1], share_ref)
        gather = Gather(place, pieces, parts, gathered, *gather_sems)

    def advance(*steps):
        if plan:
            for numbers, phase in steps:
                gather.advance(groups[numbers], phase)

    def load(number):
        return pltpu.make_async_copy(gathered[number].reshape(width, width), weights_ref.at[number], load_sem.at[number])

    def load_tile():
        return pltpu.make_async_copy(gathered[SHARDS - 1].reshape(tile_ref.shape), tile_ref, load_sem.at[ATTENTION])

    gain_refs = (gain1_ref, gain2_ref, gain3_ref)
    if plan:
        share_ref[...] = jnp.zeros_like(share_ref)
        for number, gain_ref in enumerate(gain_refs):
            share_ref[number : number + 1, : gain_ref.shape[1]] = gain_ref[...].astype(F32)
        place.greet()
    bias_ref[...] = bias_rows(table_ref, map_ref, band, "queries")
    lse1_ref[...] = jnp.zeros_like(lse1_ref)
    lse2_ref[...] = jnp.zeros_like(lse2_ref)
    mixed1_ref[...] = jnp.zeros_like(mixed1_ref)
    mixed2_ref[...] = jnp.zeros_like(mixed2_ref)
    if plan:
        place.meet()
    advance(("qk", 0), ("v", 0), ("memory", 0))
    advance(("v", 1), ("qk", 1), ("qk", 2), ("v", 2), ("out", 0))
    advance(("qk", 3), ("v", 3), ("qk", 4), ("v", 4), ("memory", 1), ("out", 1), ("gate", 0), ("down", 0))
    for number in range(3):
        load(number).start()
    if plan:
        load_tile().start()
        load_tile().wait()
        gains_ref[...] = gain_rows(tile_ref[...], width)
    else:
        gains_ref[...] = jnp.zeros_like(gains_ref)
        for number, gain_ref in enumerate(gain_refs):
            gains_ref[number : number + 1, :] = gain_ref[...].astype(F32)
    for number in range(3):
        load(number).wait()

    def project_self(rows):
        value = tokens_ref[rows, :].astype(F32)
        normed = (value * rms(value) * gains_ref[0:1, :]).astype(BF16)
        q1_ref[rows, :] = dot(normed, weights_ref[0]).astype(BF16)
        k1_ref[rows, :] = dot(normed, weights_ref[1]).astype(BF16)
        v1_ref[rows, :] = dot(normed, weights_ref[2]).astype(BF16)

    for start in range(0, length, length // 2):
        project_self(pl.ds(start, length // 2))
        if start == 0:
            advance(("out", 2))
    moves.store(0, 1, 2, 3)

    @pl.loop(0, heads)
    def _(head):
        fill_bands(head, bias_ref, band, causal_ref, two_ref)
        self_forward_head(head, limit_ref[0], q1_ref, k1_ref, v1_ref, causal_ref, two_ref, band, mixed1_ref, lse1_ref)

        for when, steps in (
            (2, (("out", 3),)),
            (3, (("memory", 2),)),
            (4, (("out", 4), ("down", 1))),
            (6, (("memory", 3),)),
            (8, (("memory", 4), ("gate", 1), ("upper", 0))),
        ):

            @pl.when(head == when * heads // 12)
            def _(when=when, steps=steps):
                advance(*steps)
                for number in {4: (3, 4, 7), 8: (5, 6)}.get(when, ()):
                    load(number).start()

    advance(("gate", 2))
    moves.store(4, 5)
    for number in range(3, ATTENTION):
        load(number).wait()

    def project_memory(rows):
        k2_ref[rows, :] = dot(memory_ref[rows, :], weights_ref[5]).astype(BF16)
        v2_ref[rows, :] = dot(memory_ref[rows, :], weights_ref[6]).astype(BF16)

    row_blocks(memory_ref.shape[0], 512, project_memory)

    def project_cross(rows):
        value = tokens_ref[rows, :].astype(F32) + dot(mixed1_ref[rows, :], weights_ref[3])
        first_ref[rows, :] = value
        normed = (value * rms(value) * gains_ref[1:2, :]).astype(BF16)
        q2_ref[rows, :] = dot(normed, weights_ref[4]).astype(BF16)

    row_blocks(length, 512, project_cross)
    moves.store(6, 7, 8, 9)

    @pl.loop(0, heads)
    def _(head):
        cross_forward_head(head, q2_ref, k2_ref, v2_ref, mixed2_ref, lse2_ref)

        @pl.when(head == heads // 4)
        def _():
            advance(("down", 2))

        @pl.when(head == heads * 2 // 3)
        def _():
            advance(("gate", 3))

    advance(("down", 3))
    moves.store(10, 11)

    def project_second(rows):
        second_ref[rows, :] = first_ref[rows, :] + dot(mixed2_ref[rows, :], weights_ref[7])

    row_blocks(length, 512, project_second)
    moves.store(12)
    advance(("gate", 4), ("down", 4))
    if plan:
        gather.settle(groups["upper"])
    moves.finish()


def norm_back_rows(value, gain, grad):
    scale = rms(value)
    unit = value * scale
    scaled = grad * gain
    return scale * (scaled - unit * jnp.mean(scaled * unit, axis=-1, keepdims=True))


GELU_A = 0.7978845608028654
GELU_B = 0.044715


def feed_rows(
    rows, gate_ref, up_ref, down_ref, gout_ref, normed_ref, out_ref, back_ref, hidden_ref, ggate_ref, gup_ref
):
    normed = normed_ref[rows, :]
    gate = dot(normed, gate_ref[...])
    upward = dot(normed, up_ref[...])
    square = gate * gate
    bend = jnp.tanh(GELU_A * gate * (1.0 + GELU_B * square))
    half = 0.5 * (1.0 + bend)
    active = gate * half
    hidden = (active * upward).astype(BF16)
    hidden_ref[rows, :] = hidden
    out_ref[rows, :] += dot(hidden, down_ref[...])
    ghidden = dot(gout_ref[rows, :], down_ref[...], 1, 1)
    slope = half + 0.5 * gate * (1.0 - bend * bend) * (GELU_A * (1.0 + 3.0 * GELU_B * square))
    ggate = (ghidden * upward * slope).astype(BF16)
    gup = (ghidden * active).astype(BF16)
    ggate_ref[rows, :] = ggate
    gup_ref[rows, :] = gup
    back_ref[rows, :] += dot(ggate, gate_ref[...], 1, 1) + dot(gup, up_ref[...], 1, 1)


def feed_kernel(
    second_ref, gout_ref, gains_ref, gate_ref, up_ref, down_ref,
    output_ref, gsecond_ref, dgate_ref, dup_ref, ddown_ref,
    normed_ref, flipped_ref, out_ref, back_ref, hidden_ref, ggate_ref, gup_ref,
):
    step = pl.program_id(0)
    length = second_ref.shape[0]
    block = 256

    @pl.when(step == 0)
    def _():
        def prepare(rows):
            value = second_ref[rows, :]
            normed = (value * rms(value) * gains_ref[2:3, :]).astype(BF16)
            normed_ref[rows, :] = normed
            flipped_ref[:, rows] = normed.T
            out_ref[rows, :] = value
            back_ref[rows, :] = jnp.zeros_like(value)

        row_blocks(length, block, prepare)

    def rows_step(rows):
        feed_rows(
            rows, gate_ref, up_ref, down_ref, gout_ref, normed_ref, out_ref, back_ref, hidden_ref, ggate_ref, gup_ref
        )

    row_blocks(length, 512, rows_step)
    ddown_ref[...] = dot(hidden_ref[...].T, gout_ref[...]).astype(BF16)
    dgate_ref[...] = dot(flipped_ref[...], ggate_ref[...]).astype(BF16)
    dup_ref[...] = dot(flipped_ref[...], gup_ref[...]).astype(BF16)

    @pl.when(step == pl.num_programs(0) - 1)
    def _():
        def finish(rows):
            output_ref[rows, :] = out_ref[rows, :].astype(BF16)
            back = norm_back_rows(second_ref[rows, :], gains_ref[2:3, :], back_ref[rows, :])
            gsecond_ref[rows, :] = back + gout_ref[rows, :].astype(F32)

        row_blocks(length, block, finish)


FEED_INS, FEED_OUTS = 6, 3


def feed_exchange_kernel(*refs, plan):
    ins, refs = refs[:FEED_INS], refs[FEED_INS + 2 :]
    results, refs = refs[:FEED_OUTS], refs[FEED_OUTS:]
    shares, outs, gathered, refs = refs[:2], refs[2:4], refs[4:6], refs[6:]
    moves = Moves(ins, results, refs)
    second_ref, gout_ref, gains_ref, gate_low_ref, up_low_ref, down_ref = moves.held_ins
    output_ref, gsecond_ref, ddown_ref = moves.held_outs
    (
        normed_ref, flipped_ref, out_ref, back_ref, hidden_ref, ggate_ref, gup_ref, gate_ref, up_ref,
        dgate_ref, dup_ref, load_sem, share_sem, *refs,
    ) = moves.rest
    sizes, gather_plan, scatter_plan = plan
    place = Place(sizes)
    gather = Gather(place, gather_plan, (), gathered, *refs[:3])
    lower = [dgate_ref.at[0], dup_ref.at[0]]
    scatter = Scatter(place, scatter_plan, lower, [True, True], outs, refs[3:-3], *refs[-3:])
    upper, every = range(len(gather_plan)), range(len(scatter_plan))
    length, width = second_ref.shape
    columns = gate_low_ref.shape[1]
    block = 256

    def load(number):
        target = (gate_ref, up_ref)[number].at[1]
        return pltpu.make_async_copy(gathered[number].reshape(width, columns), target, load_sem.at[number])

    def low(number):
        target = (gate_ref, up_ref)[number].at[0]
        return pltpu.make_async_copy((ins[3], ins[4])[number], target, load_sem.at[2 + number])

    place.greet()
    moves.load(0, 2, 1)
    for number in (0, 1):
        low(number).start()
    moves.load(5)
    place.meet()
    gather.resume(upper)
    moves.need(0, 2)

    def prepare(rows):
        value = second_ref[rows, :]
        normed = (value * rms(value) * gains_ref[2:3, :]).astype(BF16)
        normed_ref[rows, :] = normed
        flipped_ref[:, rows] = normed.T
        out_ref[rows, :] = value
        back_ref[rows, :] = jnp.zeros_like(value)

    row_blocks(length, block, prepare)
    moves.need(1, 5)
    for number in (0, 1):
        low(number).wait()

    @pl.loop(0, 2)
    def _(half):
        units = pl.ds(pl.multiple_of(half * columns, columns), columns)
        gate, up, down = gate_ref.at[half], up_ref.at[half], down_ref.at[units]

        @pl.loop(0, 2)
        def _(index):
            rows = pl.ds(pl.multiple_of(index * (length // 2), length // 2), length // 2)
            feed_rows(rows, gate, up, down, gout_ref, normed_ref, out_ref, back_ref, hidden_ref, ggate_ref, gup_ref)

            @pl.when((half == 0) & (index == 0))
            def _():
                gather.advance(upper, 2)

            @pl.when((half == 1) & (index == 0))
            def _():
                scatter.advance(every, 2)

            @pl.when((half == 1) & (index == 1))
            def _():
                scatter.advance(every, 3)

        rows_each = width // place.sizes[0]

        @pl.loop(0, place.sizes[0])
        def _(index):
            start = pl.multiple_of(index * rows_each, 64)
            flipped = flipped_ref[pl.ds(start, rows_each), :]
            for target, grad in ((dgate_ref, ggate_ref), (dup_ref, gup_ref)):
                store_shares(target.at[half], EVERY, dot(flipped, grad[...]), start)

        @pl.when(half == 0)
        def _():
            scatter.advance(every, 0)
            gather.advance(upper, 3)

        @pl.loop(0, 2)
        def _(index):
            start = pl.multiple_of(index * (columns // 2), columns // 2)
            flipped = hidden_ref[:, pl.ds(start, columns // 2)].T
            into = pl.ds(pl.multiple_of(half * columns + start, columns // 2), columns // 2)
            ddown_ref[into, :] = dot(flipped, gout_ref[...]).astype(BF16)

        @pl.when(half == 0)
        def _():
            gather.advance(upper, 4)
            for number in upper:
                load(number).start()
            scatter.advance(every, 1)
            for number in upper:
                load(number).wait()

    share = [pltpu.make_async_copy(ref.at[1], shares[i], share_sem.at[i]) for i, ref in enumerate((dgate_ref, dup_ref))]
    for copy in share:
        copy.start()
    moves.store(2)

    def finish(rows):
        output_ref[rows, :] = out_ref[rows, :].astype(BF16)
        back = norm_back_rows(second_ref[rows, :], gains_ref[2:3, :], back_ref[rows, :])
        gsecond_ref[rows, :] = back + gout_ref[rows, :].astype(F32)

    row_blocks(length, block, finish)
    moves.store(0, 1)
    scatter.advance(every, 4)
    for copy in share:
        copy.wait()
    moves.finish()


def backward_head_prepare(group_cols, gm_ref, mixed_ref, delta_ref):
    product = (gm_ref[:, group_cols].astype(F32) * mixed_ref[:, group_cols].astype(F32)).T
    delta_ref[0:1, :] = jnp.sum(product[:DH], axis=0, keepdims=True)
    delta_ref[1:2, :] = jnp.sum(product[DH:], axis=0, keepdims=True)


def backward_block(key_rows, cols, half, start, bias, q_ref, k_ref, v_ref, gm_ref, lse, delta, gk_ref, gv_ref, gqt_ref):
    length = q_ref.shape[0]
    pick = pick_lanes(half)
    queries = pl.ds(start, length - start)
    query = jnp.where(pick, q_ref[queries, cols], 0)
    grad = jnp.where(pick, gm_ref[queries, cols], 0)
    keys = k_ref[key_rows, cols]
    scores = dot(keys, query, 1, 1)
    if bias is not None:
        scores = scores + bias
    probs = jnp.exp(scores - lse[:, start:])
    gv = dot(probs.astype(BF16), grad)
    gprobs = dot(v_ref[key_rows, cols], grad, 1, 1)
    gscores = probs * (gprobs - delta[:, start:])
    low = gscores.astype(BF16)
    gk = dot(low, query)
    gk_ref[key_rows, cols] = jnp.where(pick, gk.astype(BF16), gk_ref[key_rows, cols])
    gv_ref[key_rows, cols] = jnp.where(pick, gv.astype(BF16), gv_ref[key_rows, cols])
    gqt_ref[:, queries] += dot(jnp.where(pick, keys, 0).T, low)
    return gscores


def self_backward_head(
    head, limit, q_ref, k_ref, v_ref, gm_ref, mixed_ref, lse_ref, delta_ref, causal_ref, two_ref, band,
    gk_ref, gv_ref, gqt_ref, causal_sum_ref, two_sum_ref,
):
    length = q_ref.shape[0]
    cols, half = head_cols(head)
    lse = lse_ref[pl.ds(head, 1), :]
    delta = delta_ref[pl.ds(half, 1), :]
    reach = band.reach
    block = 256
    for first in range(0, length, block):
        start = 0 if first < reach else first
        count = length - start
        parts = []
        for key in range(first, first + block, SUB):
            at = band.key_zero - key + start
            bias = causal_ref[:, at : at + count]
            if first < reach:
                at = band.key_zero - key
                two = two_ref[:, at : at + reach]
                inside = (key + lax.broadcasted_iota(jnp.int32, (SUB, reach), 0) < limit) & (
                    lax.broadcasted_iota(jnp.int32, (SUB, reach), 1) < limit
                )
                bias = jnp.concatenate([jnp.where(inside, two, bias[:, :reach]), bias[:, reach:]], axis=1)
            parts.append(bias)
        gscores = backward_block(
            pl.ds(first, block), cols, half, start, jnp.concatenate(parts, axis=0),
            q_ref, k_ref, v_ref, gm_ref, lse, delta, gk_ref, gv_ref, gqt_ref,
        )
        for key in range(first, first + block, SUB):
            part = gscores[key - first : key - first + SUB]
            at = band.key_zero - key + start
            if first < reach:
                inside = (key + lax.broadcasted_iota(jnp.int32, (SUB, reach), 0) < limit) & (
                    lax.broadcasted_iota(jnp.int32, (SUB, reach), 1) < limit
                )
                head_part = part[:, :reach]
                at_two = band.key_zero - key
                two_sum_ref[:, at_two : at_two + reach] += jnp.where(inside, head_part, 0.0)
                causal_sum_ref[:, at : at + reach] += jnp.where(inside, 0.0, head_part)
                causal_sum_ref[:, at + reach : at + count] += part[:, reach:]
            else:
                causal_sum_ref[:, at : at + count] += part


def split_columns(number, columns):
    half = columns // 2
    return [(number, 0, half, "xy"), (number, half, half, "yx")]


CROSS_INS, CROSS_OUTS = 15, 8


def cross_backward_kernel(*refs, heads, plan):
    count = 3 if plan else 0
    ins, refs = refs[:CROSS_INS], refs[CROSS_INS:]
    sources, refs = refs[:count], refs[count:]
    results, refs = refs[:CROSS_OUTS], refs[CROSS_OUTS:]
    outs, refs = refs[:count], refs[count:]
    moves = Moves(ins, results, refs)
    (
        gsecond_ref, first_ref, memory_ref, gains_ref, q_ref, k_ref, v_ref, mixed1_ref, mixed2_ref, lse_ref,
        wo_ref, cq_ref, ck_ref, cv_ref, co_ref,
    ) = moves.held_ins
    gmem_ref, gfirst_ref, gm1_ref, dwo_ref, dcq_ref, dck_ref, dcv_ref, dco_ref = moves.held_outs
    gm_ref, branch_ref, flipped_ref, lse_rows_ref, delta_ref, gq_ref, gk_ref, gv_ref, gqt_ref, *refs = moves.rest
    if plan:
        sizes, pieces = plan
        scatter = Scatter(Place(sizes), pieces, sources, [False] * count, outs, refs[:-3], *refs[-3:])
        waves = [range(number, number + 2) for number in range(0, len(pieces), 2)]
        scatter.place.greet()

    def advance(*steps):
        if plan:
            for wave, phase in steps:
                scatter.advance(waves[wave], phase)

    moves.load(0, 14, 8, 4, 5, 6, 9, 2, 12, 13, 1, 3, 11, 10, 7)
    if plan:
        scatter.place.meet()
    advance((0, 0), (1, 0), (2, 0), (3, 0))
    length, width = first_ref.shape
    source = memory_ref.shape[0]
    block = 256

    def prepare(rows):
        branch = gsecond_ref[rows, :].astype(BF16)
        branch_ref[rows, :] = branch
        gm_ref[rows, :] = dot(branch, co_ref[...], 1, 1).astype(BF16)
        flipped_ref[:, rows] = mixed2_ref[rows, :].T

    moves.need(0, 14, 8)
    row_blocks(length, 256, prepare)

    def out_grad(rows):
        dco_ref[rows, :] = dot(flipped_ref[rows, :], branch_ref[...]).astype(BF16)

    row_blocks(width, 192, out_grad)
    moves.store(7)
    moves.need(4, 5, 6, 9)
    advance((0, 1))
    lse_rows_ref[...] = lse_ref[...].T
    gk_ref[...] = jnp.zeros_like(gk_ref)
    gv_ref[...] = jnp.zeros_like(gv_ref)
    groups = heads // 2

    @pl.loop(0, groups)
    def _(group):
        cols = pl.ds(pl.multiple_of(group * PAIR, PAIR), PAIR)
        backward_head_prepare(cols, gm_ref, mixed2_ref, delta_ref)
        gqt_ref[...] = jnp.zeros_like(gqt_ref)

        @pl.loop(0, 2)
        def _(half):
            head = group * 2 + half
            for when, steps in ((3, ((0, 2), (1, 1))), (7, ((0, 3), (1, 2), (2, 1)))):

                @pl.when(head == when * heads // 12)
                def _(steps=steps):
                    advance(*steps)

            @pl.loop(0, source // block)
            def _(index):
                backward_block(
                    pl.ds(pl.multiple_of(index * block, block), block), cols, half, 0, None, q_ref, k_ref, v_ref, gm_ref,
                    lse_rows_ref[pl.ds(head, 1), :], delta_ref[pl.ds(half, 1), :], gk_ref, gv_ref, gqt_ref,
                )

        gq_ref[:, cols] = gqt_ref[...].T.astype(BF16)

    advance((1, 3), (2, 2), (3, 1))

    def memory_grad(rows):
        gmem_ref[rows, :] = dot(gk_ref[rows, :], ck_ref[...], 1, 1) + dot(gv_ref[rows, :], cv_ref[...], 1, 1)
        flipped_ref[:, rows] = memory_ref[rows, :].T

    moves.need(2, 12, 13)
    row_blocks(source, 256, memory_grad)
    moves.store(0)

    def memory_weights(rows):
        flipped = flipped_ref[rows, :source]
        dck_ref[rows, :] = dot(flipped, gk_ref[...]).astype(BF16)
        dcv_ref[rows, :] = dot(flipped, gv_ref[...]).astype(BF16)

    row_blocks(width, 192, memory_weights)
    moves.store(5, 6)
    moves.need(1, 3, 11, 10, 7)
    advance((2, 3), (3, 2), (0, 4))

    def first_grad(rows):
        value = first_ref[rows, :]
        flipped_ref[:, rows] = (value * rms(value) * gains_ref[1:2, :]).astype(BF16).T
        back = norm_back_rows(value, gains_ref[1:2, :], dot(gq_ref[rows, :], cq_ref[...], 1, 1))
        gfirst = back + gsecond_ref[rows, :]
        gfirst_ref[rows, :] = gfirst
        branch = gfirst.astype(BF16)
        branch_ref[rows, :] = branch
        gm1_ref[rows, :] = dot(branch, wo_ref[...], 1, 1).astype(BF16)

    row_blocks(length, 256, first_grad)
    moves.store(1, 2)
    advance((3, 3), (1, 4))

    def query_weights(rows):
        dcq_ref[rows, :] = dot(flipped_ref[rows, :], gq_ref[...]).astype(BF16)

    row_blocks(width, 192, query_weights)
    moves.store(4)

    def flip_mixed(rows):
        flipped_ref[:, rows] = mixed1_ref[rows, :].T

    row_blocks(length, block, flip_mixed)

    def out_weights(rows):
        dwo_ref[rows, :] = dot(flipped_ref[rows, :], branch_ref[...]).astype(BF16)

    row_blocks(width, 192, out_weights)
    moves.store(3)
    advance((2, 4), (3, 4))
    moves.finish()


def store_shares(ref, cols, value, start):
    if len(ref.shape) == 2:
        ref[pl.ds(start, value.shape[0]), cols] = value.astype(BF16)
    else:
        deep, high, wide, cores, rows, columns = ref.shape
        chunk = high * wide * cores * rows
        ref[lax.div(start, chunk), :, :, :, :, cols] = value.reshape(high, wide, cores, rows, value.shape[1]).astype(BF16)


TILE = 16


def fill_tiles(tiles_ref, gtable):
    deep, high, wide, cores, rows, lanes = tiles_ref.shape
    heads, buckets = gtable.shape
    tiles_ref[...] = jnp.zeros_like(tiles_ref)

    @pl.loop(0, deep)
    def _(z):
        shape = (high, wide, cores, heads, buckets)
        tiles_ref[z, :, :, :, :heads, :buckets] = jnp.broadcast_to(gtable, shape)


REST = 5


def self_parts(columns):
    half, third = columns // 2, columns // 3
    return (0, half), (half, third), (half + third, columns - half - third)


def self_pieces(columns):
    first = [(0, 0, columns, "xy"), (1, 0, columns, "yx")]
    rest = [(2, 0, columns, "xy"), (3, 0, columns, "yx")] + split_columns(4, columns)
    parts = []
    for number, (start, count) in enumerate(self_parts(columns)):
        orders = ("xy", "yx", "xy") if number % 2 else ("yx", "xy", "yx")
        parts.append([(REST + array, start, count, orders[array]) for array in range(3)])
    pieces, groups = [], []
    for group in (first, rest, *parts, [(REST + 3, 0, SUB, "xy")]):
        groups.append(range(len(pieces), len(pieces) + len(group)))
        pieces += group
    return pieces, groups


SELF_INS = 12


def self_backward_kernel(limit_ref, table_ref, map_ref, *refs, band, heads, plan):
    count = REST if plan else 0
    ins, refs = refs[:SELF_INS], refs[SELF_INS:]
    sources, refs = refs[:count], refs[count:]
    gtokens_ref, refs = refs[0], refs[1:]
    if plan:
        outs, refs = refs[: REST + 3], refs[REST + 3 :]
        gtable_ref, refs = refs[0], refs[1:]
    else:
        gtable_ref, dwq_ref, dwk_ref, dwv_ref, *refs = refs
    moves = Moves(ins, (), refs)
    (
        tokens_ref, gains_ref, lse_ref, q_ref, k_ref, v_ref, mixed_ref, gm_ref, gfirst_ref, wq_ref, wk_ref, wv_ref,
    ) = moves.held_ins
    refs = moves.rest
    (
        bias_ref, causal_ref, two_ref, flipped_ref, lse_rows_ref, delta_ref, gq_ref, gk_ref, gv_ref, gqt_ref,
        causal_sum_ref, two_sum_ref, sums_ref, *refs,
    ) = refs
    length, width = tokens_ref.shape
    block = 256
    groups = heads // 2
    if plan:
        sizes, pieces, (first, rest, early, middle, late, table) = plan
        dwq_ref, dwk_ref, dwv_ref, tiles_ref, tile_ref, *refs = refs
        scatter = Scatter(
            Place(sizes), pieces, (*sources, dwq_ref, dwk_ref, dwv_ref, tiles_ref), [False] * REST + [True] * 4,
            (*outs, tile_ref), refs[:-3], *refs[-3:],
        )
        scatter.place.greet()
    moves.load(*range(SELF_INS))
    bias_ref[...] = bias_rows(table_ref, map_ref, band, "keys")
    if plan:
        scatter.place.meet()
        scatter.advance(first, 0)
        scatter.advance(rest, 0)
    moves.need(0, 1, 2)
    lse_rows_ref[...] = lse_ref[...].T
    gk_ref[...] = jnp.zeros_like(gk_ref)
    gv_ref[...] = jnp.zeros_like(gv_ref)
    sums_ref[...] = jnp.zeros_like(sums_ref)

    def flip_normed(rows):
        value = tokens_ref[rows, :].astype(F32)
        flipped_ref[:, rows] = (value * rms(value) * gains_ref[0:1, :]).astype(BF16).T

    row_blocks(length, block, flip_normed)
    moves.need(*range(3, SELF_INS))

    def group_step(group):
        cols = pl.ds(pl.multiple_of(group * PAIR, PAIR), PAIR)
        backward_head_prepare(cols, gm_ref, mixed_ref, delta_ref)
        gqt_ref[...] = jnp.zeros_like(gqt_ref)

        @pl.loop(0, 2)
        def _(half):
            head = group * 2 + half
            if plan:
                for when, numbers, phase in ((1, first, 1), (3, rest, 1), (5, first, 2), (8, first, 3), (9, rest, 2), (10, early, 1), (11, rest, 3)):

                    @pl.when(head == when * heads // 12)
                    def _(numbers=numbers, phase=phase):
                        scatter.advance(numbers, phase)

            fill_bands(head, bias_ref, band, causal_ref, two_ref)
            causal_sum_ref[...] = jnp.zeros_like(causal_sum_ref)
            two_sum_ref[...] = jnp.zeros_like(two_sum_ref)
            self_backward_head(
                head, limit_ref[0], q_ref, k_ref, v_ref, gm_ref, mixed_ref, lse_rows_ref, delta_ref,
                causal_ref, two_ref, band, gk_ref, gv_ref, gqt_ref, causal_sum_ref, two_sum_ref,
            )
            sums_ref[pl.ds(head, 1), : band.causal] = fold(causal_sum_ref[...])
            sums_ref[pl.ds(head, 1), band.causal :] = fold(two_sum_ref[...])

        gq_ref[:, cols] = gqt_ref[...].T.astype(BF16)

    rows_each = width // (sizes["dp"] // (sizes["fsdp"] // 2)) if plan else block

    def weights(cols):
        @pl.loop(0, width // rows_each)
        def _(index):
            start = pl.multiple_of(index * rows_each, 64)
            flipped = flipped_ref[pl.ds(start, rows_each), :]
            for target, grad in ((dwq_ref, gq_ref), (dwk_ref, gk_ref), (dwv_ref, gv_ref)):
                store_shares(target, cols, dot(flipped, grad[:, cols]), start)

    parts = [pl.ds(start, count) for start, count in self_parts(width)]

    @pl.loop(0, groups)
    def _(group):
        if plan:

            @pl.when(group == groups // 2)
            def _():
                weights(parts[0])
                scatter.advance(early, 0)

            @pl.when(group == groups - 1)
            def _():
                weights(parts[1])
                scatter.advance(middle, 0)

        group_step(group)

    if plan:
        weights(parts[2])
        scatter.advance(late, 0)
        scatter.advance(early, 2)
    else:
        for part in parts:
            weights(part)
    hot, unused = one_hot(map_ref, band, "keys")
    gtable = exact_dot(sums_ref[...], hot, 1, 1)
    if plan:
        fill_tiles(tiles_ref, gtable)
        scatter.advance(table, 0)
        scatter.advance(middle, 1)
        scatter.advance(late, 1)

    def tokens_grad(rows):
        value = tokens_ref[rows, :].astype(F32)
        grad = dot(gq_ref[rows, :], wq_ref[...], 1, 1)
        grad += dot(gk_ref[rows, :], wk_ref[...], 1, 1)
        grad += dot(gv_ref[rows, :], wv_ref[...], 1, 1)
        gtokens_ref[rows, :] = norm_back_rows(value, gains_ref[0:1, :], grad) + gfirst_ref[rows, :]

    if plan:
        steps = (
            ((table, 1), (early, 3), (first, 4)),
            ((middle, 2), (late, 2), (table, 2)),
            ((middle, 3), (rest, 4)),
            ((late, 3), (table, 3)),
        )

        @pl.loop(0, len(steps))
        def _(step):
            for start in range(0, length // len(steps), block):
                start = step * (length // len(steps)) + start
                tokens_grad(pl.ds(pl.multiple_of(start, block), block))
            for number, advances in enumerate(steps):

                @pl.when(step == number)
                def _(advances=advances):
                    for numbers, phase in advances:
                        scatter.advance(numbers, phase)

        scatter.advance(early, 4)
        scatter.advance(middle, 4)
        scatter.advance(late, 4)
        scatter.advance(table, 4)
        gtable_ref[...] = tile_ref[:heads, :NB]
    else:
        row_blocks(length, block, tokens_grad)
        gtable_ref[...] = gtable


def gain_grads(gains, weights, grads):
    results = []
    for gain, parts in zip(gains, ((0, 1, 2), (3,), (4, 5))):
        total = 0.0
        for part in parts:
            product = weights[part][...].astype(F32) * grads[part][...]
            total += exact_dot(jnp.ones((8, product.shape[1]), F32), product, 1, 1)
        results.append(total[0:1] / gain[...].astype(F32))
    return results


def hand_on_kernel(*refs, places, norms):
    count = len(places)
    shards, refs = refs[: len(norms) + 3], refs[len(norms) + 3 :]
    ins, (in_sem, out_sem) = refs[:count], refs[-2:]
    refs = refs[count:-2]
    held, outs, ggain_refs = refs[-count:], refs[: -count - 3], refs[-count - 3 : -count]
    loads = [pltpu.make_async_copy(ins[i], held[i], in_sem.at[i]) for i in range(count)]
    stores = []
    for i, (out, start) in enumerate(places):
        target = outs[out] if start is None else outs[out].at[:, start : start + ins[i].shape[1]]
        stores.append(pltpu.make_async_copy(held[i], target, out_sem.at[i]))
    for load in loads:
        load.start()
    for load, store in zip(loads, stores):
        load.wait()
        store.start()
    grads = []
    for number in norms:
        parts = [held[i][...] for i, (out, start) in enumerate(places) if out == number]
        grads.append(jnp.concatenate(parts, axis=1))
    for ref, value in zip(ggain_refs, gain_grads(shards[:3], shards[3:], grads)):
        ref[...] = value
    for store in stores:
        store.wait()


def hand_on(results, norms, gains, weights):
    arrays, places, shapes = [], [], []
    for number, result in enumerate(results):
        parts = result if isinstance(result, tuple) else (result,)
        start = 0
        for part in parts:
            arrays.append(part)
            places.append((number, start if len(parts) > 1 else None))
            start += part.shape[-1]
        shapes.append(jax.ShapeDtypeStruct(parts[0].shape[:-1] + (start,), parts[0].dtype))
    spec = pl.BlockSpec(memory_space=pl.ANY)
    here = pl.BlockSpec(memory_space=pltpu.VMEM)
    shards = [*[gain.reshape(1, -1) for gain in gains], *weights]
    *results, first, second, third = pl.pallas_call(
        functools.partial(hand_on_kernel, places=places, norms=norms),
        out_shape=shapes + [jax.ShapeDtypeStruct((1, gain.shape[0]), F32) for gain in gains],
        in_specs=[here] * len(shards) + [spec] * len(arrays),
        out_specs=[spec] * len(shapes) + [here] * 3,
        scratch_shapes=[pltpu.VMEM(a.shape, a.dtype) for a in arrays] + [pltpu.SemaphoreType.DMA((len(arrays),))] * 2,
        compiler_params=params(),
        name="hand_on",
    )(*shards, *arrays)
    return results, [ggain.reshape(-1) for ggain in (first, second, third)]


def upper_shapes(arrays):
    return [jax.ShapeDtypeStruct(a.shape, a.dtype) for a in arrays]


def vmem(*shapes):
    return [pltpu.VMEM(shape, dtype) for shape, dtype in shapes]


def params(**kw):
    return pltpu.CompilerParams(vmem_limit_bytes=60 * 1024 * 1024, **kw)


def per_device(
    inputs, encoded, out_grad, prefix, bucket_map, bias_table,
    norm_self, self_query, self_key, self_value, self_out,
    norm_cross, cross_query, cross_key, cross_value, cross_out,
    norm_feed, feed_gate, feed_up, feed_down,
):
    seqs, length, width = inputs.shape
    source = encoded.shape[1]
    heads = bias_table.shape[1]
    ff = feed_gate.shape[1]
    band = Band(length, length // 2)
    tokens = inputs.reshape(length, width)
    flipped_table = bias_table.T
    memory = encoded.reshape(source, width)
    gout = out_grad.reshape(length, width)
    gains_in = [norm_self, norm_cross, norm_feed]
    projections = [self_query, self_key, self_value, self_out, cross_query, cross_key, cross_value, cross_out]
    feeds = [feed_gate, feed_up, feed_down]
    sizes = dict(dp=lax.axis_size("dp"), fsdp=lax.axis_size("fsdp"))
    devices = sizes["dp"] * sizes["fsdp"]
    own = self_query.shape[0] % 8 == 0
    if own:
        pieces, groups = gather_pieces(self_query.shape[0], feed_down.shape[0])
        plan = (sizes, pieces, groups)
        copies = Gather.copies(sizes, pieces)
        shards = projections + feeds
    else:
        plan = None
        gains_in = [lax.all_gather(gain, AXES, axis=0, tiled=True) for gain in gains_in]
        shards = [lax.all_gather(shard, AXES, axis=0, tiled=True) for shard in projections]
        gate_full, up_full, down = [lax.all_gather(shard, AXES, axis=0, tiled=True) for shard in feeds]
    gains_in = [gain.reshape(1, -1) for gain in gains_in]

    remote = pl.BlockSpec(memory_space=pl.ANY)
    scalar = pl.BlockSpec(memory_space=pltpu.SMEM)

    def full(shape):
        return pl.BlockSpec(shape, lambda *_: (0,) * len(shape))

    def like(shape, dtype):
        return jax.ShapeDtypeStruct(shape, dtype)

    act = like((length, width), BF16)
    mem = like((source, width), BF16)
    act32 = like((length, width), F32)
    lse_shape = like((length, SUB), F32)
    gain_shape = like((8, width), F32)
    outs = [gain_shape, act, act, act, act, lse_shape, act32, act, mem, mem, act, lse_shape, act32]
    gathered_shapes = []
    if own:
        chips, cores = grid_of(sizes)[:3], grid_of(sizes)[3]
        shapes = [shard.shape for shard in projections]
        shapes += [(feed_gate.shape[0], ff // 2)] * 2 + [feed_down.shape] + [(feed_gate.shape[0], ff // 2)] * 2
        gathered_shapes = [like(chips + (cores * shape[0], shape[1]), BF16) for shape in shapes]
        gathered_shapes.append(like(chips + (cores * 8, SUB), F32))
    forward_in = (tokens, memory, flipped_table, bucket_map, *gains_in)
    results = pl.pallas_call(
        functools.partial(forward_kernel, band=band, heads=heads, plan=plan),
        out_shape=gathered_shapes + outs,
        grid=(1,),
        in_specs=[scalar] + [full(a.shape) for a in forward_in]
        + ([full(a.shape) for a in shards] if own else [remote] * len(shards)),
        out_specs=[remote] * (len(gathered_shapes) + len(outs)),
        scratch_shapes=Moves.scratch(outs)
        + vmem(
            ((heads, band.width), F32), ((SUB, band.causal), F32), ((SUB, band.two_way), F32),
            ((ATTENTION, width, width), BF16), ((8, SUB), F32), ((devices, 8, SUB), F32),
        )
        + [pltpu.SemaphoreType.DMA((ATTENTION + 1,))]
        + ([pltpu.SemaphoreType.DMA((number,)) for number in (len(pieces), copies, copies)] if own else []),
        compiler_params=params(collective_id=0, has_side_effects=True) if own else params(),
        name="forward",
    )(prefix, *forward_in, *shards)
    attention = shards
    if own:
        gathered, results = results[:SHARDS], results[SHARDS:]
        attention = [part.reshape(width, width) for part in gathered[:ATTENTION]]
        gate_low, up_low = gathered[8].reshape(width, ff // 2), gathered[9].reshape(width, ff // 2)
        down = gathered[10].reshape(ff, width)
    gains, q1, k1, v1, mixed1, lse1, first, q2, k2, v2, mixed2, lse2, second = results

    grid = grid_of(sizes)

    def shares(grads):
        return [grad.reshape(grid + (grad.shape[0] // devices, grad.shape[1])) for grad in grads]

    def scatter_scratch(pieces, shapes, kept):
        count = Scatter.copies(sizes, pieces)
        return Scatter.scratch(sizes, pieces, shapes, kept) + [
            pltpu.SemaphoreType.DMA((number,)) for number in (len(pieces), count, count)
        ]

    if own:
        half = ff // 2
        share = feed_gate.shape[0]
        upper = gathered[11:13]
        gather_plan = [(0, 0, share, "zxy"), (1, 0, share, "zyx")]
        scatter_plan = [(0, 0, half, "xy"), (1, 0, half, "yx")]
        feed_in = (second, gout, gains, gate_low, up_low, down)
        feed_out = [act, act32, like((ff, width), BF16)]
        share_shapes = [like(grid + (share, half), BF16)] * 2
        grad_shapes = [like((share, half), F32)] * 2
        copies = Gather.copies(sizes, gather_plan)
        output, gsecond, ddown, *halves = pl.pallas_call(
            functools.partial(feed_exchange_kernel, plan=(sizes, gather_plan, scatter_plan)),
            out_shape=feed_out + share_shapes + grad_shapes + upper_shapes(upper),
            grid=(1,),
            in_specs=[remote] * (FEED_INS + 2),
            out_specs=[remote] * (FEED_OUTS + 2) + [full(o.shape) for o in grad_shapes] + [remote] * 2,
            scratch_shapes=Moves.scratch([*feed_in, *feed_out])
            + vmem(
                ((length, width), BF16), ((width, length), BF16), ((length, width), F32), ((length, width), F32),
                ((length, half), BF16), ((length, half), BF16), ((length, half), BF16),
                ((2, width, half), BF16), ((2, width, half), BF16),
                ((2,) + grid + (share, half), BF16), ((2,) + grid + (share, half), BF16),
            )
            + [pltpu.SemaphoreType.DMA((number,)) for number in (4, 2, len(gather_plan), copies, copies)]
            + scatter_scratch(scatter_plan, [(share, BF16)] * 2, [True, True]),
            input_output_aliases={FEED_INS: FEED_OUTS + 4, FEED_INS + 1: FEED_OUTS + 5},
            compiler_params=params(collective_id=3, has_side_effects=True),
            name="feed",
        )(*feed_in, *upper)
        high_shares, low_grads = halves[:2], halves[2:4]
    else:
        fblock = min(1024, ff)
        feed_out = [
            act, act32, like((width, ff), BF16), like((width, ff), BF16), like((ff, width), BF16)
        ]
        output, gsecond, dgate, dup, ddown = pl.pallas_call(
            feed_kernel,
            out_shape=feed_out,
            grid=(ff // fblock,),
            in_specs=[full(second.shape), full(gout.shape), full(gains.shape)]
            + [
                pl.BlockSpec((width, fblock), lambda i: (0, i)),
                pl.BlockSpec((width, fblock), lambda i: (0, i)),
                pl.BlockSpec((fblock, width), lambda i: (i, 0)),
            ],
            out_specs=[full(o.shape) for o in feed_out[:2]]
            + [
                pl.BlockSpec((width, fblock), lambda i: (0, i)),
                pl.BlockSpec((width, fblock), lambda i: (0, i)),
                pl.BlockSpec((fblock, width), lambda i: (i, 0)),
            ],
            scratch_shapes=vmem(
                ((length, width), BF16), ((width, length), BF16), ((length, width), F32), ((length, width), F32),
                ((length, fblock), BF16), ((length, fblock), BF16), ((length, fblock), BF16),
            ),
            compiler_params=params(),
            name="feed",
        )(second, gout, gains, gate_full, up_full, down)

    square = like((width, width), BF16)
    cross_shapes = [like((source, width), F32), act32, act] + [square] * 5
    cross_in = (gsecond, first, memory, gains, q2, k2, v2, mixed1, mixed2, lse2)
    cross_scratch = vmem(
        ((length, width), BF16), ((length, width), BF16), ((width, length), BF16), ((SUB, length), F32),
        ((8, length), F32), ((length, width), BF16), ((source, width), BF16), ((source, width), BF16),
        ((PAIR, length), F32),
    )
    plan, sources, gate_shapes, scratch = None, [], [], []
    if own:
        sources = high_shares + shares([ddown])
        quarter, third = half // 2, width // 3
        pieces = [(0, 0, quarter, "xy"), (1, 0, quarter, "yx"), (0, quarter, quarter, "xy"), (1, quarter, quarter, "yx")]
        pieces += [(2, 0, third, "xy"), (2, third, third, "yx")]
        pieces += [(2, 2 * third, third // 2, "xy"), (2, 2 * third + third // 2, third // 2, "yx")]
        plan = (sizes, pieces)
        gate_shapes = [like(part.shape[-2:], F32) for part in sources]
        scratch = scatter_scratch(pieces, [(part.shape[-2], BF16) for part in sources], [False] * 3)
    moved = Moves.scratch([*cross_in, *attention[3:], *cross_shapes])
    gmem, gfirst, gm1, dwo, dcq, dck, dcv, dco, *feed_grads = pl.pallas_call(
        functools.partial(cross_backward_kernel, heads=heads, plan=plan),
        out_shape=cross_shapes + gate_shapes,
        grid=(1,),
        in_specs=[remote] * (CROSS_INS + len(sources)),
        out_specs=[remote] * CROSS_OUTS + [full(o.shape) for o in gate_shapes],
        scratch_shapes=moved + cross_scratch + scratch,
        compiler_params=params(collective_id=1, has_side_effects=True) if own else params(),
        name="cross_backward",
    )(*cross_in, *attention[3:], *sources)

    self_in = (flipped_table, bucket_map)
    self_moved = (tokens, gains, lse1, q1, k1, v1, mixed1, gm1, gfirst, *attention[:3])
    self_scratch = vmem(
        ((heads, band.width), F32), ((SUB, band.causal), F32), ((SUB, band.two_way), F32), ((width, length), BF16),
        ((SUB, length), F32), ((8, length), F32), ((length, width), BF16), ((length, width), BF16),
        ((length, width), BF16), ((PAIR, length), F32), ((SUB, band.causal), F32), ((SUB, band.two_way), F32),
        ((heads, band.width), F32),
    )
    plan, sources, scratch = None, [], []
    table_shape = like((heads, NB), F32)
    if own:
        sources = shares([dco, dwo, dcq, dck, dcv])
        pieces, groups = self_pieces(width)
        plan = (sizes, pieces, groups)
        share = width // devices
        kept = [False] * REST + [True] * 4
        shapes = [(part.shape[-2], BF16) for part in sources] + [(share, BF16)] * 3 + [(TILE, F32)]
        self_shapes = [act32] + [like(part.shape[-2:], F32) for part in sources] + [like((share, width), F32)] * 3
        self_shapes += [table_shape]
        scratch = vmem(*[(grid + (share, width), BF16)] * 3, (grid + (TILE, SUB), F32), ((TILE, SUB), F32))
        scratch += scatter_scratch(pieces, shapes, kept)
    else:
        self_shapes = [act32, table_shape] + [square] * 3
    gtokens, *grads = pl.pallas_call(
        functools.partial(self_backward_kernel, band=band, heads=heads, plan=plan),
        out_shape=self_shapes,
        grid=(1,),
        in_specs=[scalar] + [full(a.shape) for a in self_in] + [remote] * (SELF_INS + len(sources)),
        out_specs=[full(o.shape) for o in self_shapes],
        scratch_shapes=Moves.scratch(self_moved) + self_scratch + scratch,
        compiler_params=params(collective_id=2, has_side_effects=True) if own else params(),
        name="self_backward",
    )(prefix, *self_in, *self_moved, *sources)

    gain_parts = (norm_self, norm_cross, norm_feed)
    weight_parts = (self_query, self_key, self_value, cross_query, feed_gate, feed_up)
    if own:
        results = [gtokens, output, gmem, (low_grads[0], feed_grads[0]), (low_grads[1], feed_grads[1]), feed_grads[2]]
        results, ggains = hand_on([*results, *grads], (11, 12, 13, 8, 3, 4), gain_parts, weight_parts)
        gtokens, output, gmem, dgate, dup, ddown, dco, dwo, dcq, dck, dcv, dwq, dwk, dwv, table_grad = results
    else:
        gtable, dwq, dwk, dwv = grads
        table_grad = lax.psum(gtable, AXES)

        def scatter(parts):
            return lax.psum_scatter(jnp.concatenate(parts, axis=1), AXES, scatter_dimension=0, tiled=True).astype(F32)

        dgate, dup = jnp.split(scatter([dgate, dup]), 2, axis=1)
        ddown = scatter([ddown])
        squares = scatter([dwq, dwk, dwv, dwo, dcq, dck, dcv, dco])
        dwq, dwk, dwv, dwo, dcq, dck, dcv, dco = jnp.split(squares, 8, axis=1)
        parts = gain_grads([gain.reshape(1, -1) for gain in gain_parts], weight_parts, (dwq, dwk, dwv, dcq, dgate, dup))
        ggains = [part.reshape(-1) for part in parts]
    return (
        output.reshape(inputs.shape),
        gtokens.reshape(inputs.shape),
        gmem.reshape(encoded.shape),
        table_grad.T,
        ggains[0], dwq, dwk, dwv, dwo,
        ggains[1], dcq, dck, dcv, dco,
        ggains[2], dgate, dup, ddown,
    )


def solution(mesh):
    rows = P(AXES, None)
    gain = P(AXES)
    block = P(AXES, None, None)
    return jax.shard_map(
        per_device,
        mesh=mesh,
        in_specs=(block, block, block, gain, P(), P())
        + (gain, rows, rows, rows, rows)
        + (gain, rows, rows, rows, rows)
        + (gain, rows, rows, rows),
        out_specs=(block, block, block, P())
        + (gain, rows, rows, rows, rows)
        + (gain, rows, rows, rows, rows)
        + (gain, rows, rows, rows),
        check_vma=False,
    )
```
